32 devices in a mesh: gx: 4 (over y, x), gy: 8 (over z, core).
Axes of the slice: x: 2, y: 2, z: 4, core: 2. Of those that a mesh axis runs over, the one named last changes fastest.
Arguments:
- charges: float32 [4, 8, 16384], P('gx', 'gy'), may hold values from -1.2 to 1.2
- fractions: float32 [4, 8, 3, 16384], P('gx', 'gy'), may hold values from 0 to 1
- cells: int32 [4, 8, 2, 16384], P('gx', 'gy'), may hold values from 0 to 127, as said below
Outputs:
- potential_grid: float32 [128, 128, 128], P('gx', 'gy')
- atom_potential: float32 [4, 8, 16384], P('gx', 'gy')
The draws below stay inside these ranges and needn't reach their ends.
Inputs may be any that keep to these rules, and one draw needn't show every extreme that they name: cells[i, j, 0, a] lies in i-independent range j * 16 + 1 to j * 16 + 16, taken modulo 128; cells[i, j, 1, a] is a cell along the third dimension.
All inputs are finite; a program needn't handle non-finite values.
Results may differ from the reference program's by a relative error of at most 0.0003.
Values sent between devices are 32-bit elements; how exact they have to be, the bound alone decides.
No kernel may reach another device: no remote copies, remote signals or barrier semaphores. Data moves between devices by JAX's collectives and lax.ppermute only.
A program may use at most 128 MiB of HBM per device.

```python
import jax
import jax.numpy as jnp
import numpy as np
from jax import lax

CX = 32
CY = 16
NZ = 128
ATOMS_DEV = 16384
N_GX = 4
N_GY = 8


def draw_cells(key, part):
    first_key, second_key = jax.random.split(jax.random.fold_in(key, 11))
    offsets_y = jax.random.randint(first_key, (N_GX, N_GY, ATOMS_DEV), 0, CY)
    column = jnp.arange(N_GY, dtype=jnp.int32)[None, :, None] * CY
    cell_y = (column + 1 + offsets_y) % (CY * N_GY)
    cell_z = jax.random.randint(second_key, (N_GX, N_GY, ATOMS_DEV), 0, NZ)
    return jnp.stack([cell_y, cell_z], axis=2).astype(jnp.int32)


def level_of(stream_key, dims, shards, least, largest):
    level = 1.0
    for dim, shards_of in shards:
        heights = jax.random.uniform(jax.random.fold_in(jax.random.fold_in(stream_key, 6), dim), (shards_of,), jnp.float32, least / len(shards), largest / len(shards))
        level = level * jnp.repeat(jnp.exp(heights), dims[dim] // shards_of).reshape((-1,) + (1,) * (len(dims) - 1 - dim))
    return level


def noise(own_key, shape, deviation, bound, cuts=(), kind=jnp.bfloat16):
    result = jax.random.normal(own_key, shape, jnp.float32) * deviation
    if len(cuts) > 0:
        result = level_of(own_key, shape, cuts, -0.22, 0.18) * result
    return jnp.clip(result, min=-bound, max=bound).astype(kind)


def setup_inputs(seed: int = 0) -> dict:
    streams_of = jax.random.split(jax.random.key(seed), 4)
    return {
        "charges": noise(streams_of[0], (N_GX, N_GY, ATOMS_DEV), 0.2, 1.2, ((0, 4), (1, 8)), jnp.float32),
        "fractions": jnp.clip(1.0 * jax.random.uniform(streams_of[1], (N_GX, N_GY, 3, ATOMS_DEV), jnp.float32) ** level_of(streams_of[1], (N_GX, N_GY, 3, ATOMS_DEV), ((0, 4), (1, 8)), -0.2, 0.2), 0.0, 1.0),
        "cells": draw_cells(jax.random.fold_in(streams_of[3], 71), 0),
    }


restrict_taps = ((-3, -0.0625), (-1, 0.5625), (0, 1.0), (1, 0.5625), (3, -0.0625))

def spline_weights(frac):

    def near_weight(distance):
        return (1.0 - distance) * (1.0 + distance - 1.5 * distance * distance)

    def far_weight(distance):
        return -0.5 * (distance - 1.0) * (2.0 - distance) * (2.0 - distance)
    return [far_weight(1.0 + frac), near_weight(frac), near_weight(1.0 - frac), far_weight(2.0 - frac)]

def smooth_numpy(rho):
    return np.where(rho < 1.0, 1.875 - 1.25 * rho * rho + 0.375 * rho ** 4, 1.0 / np.maximum(rho, 1.0))

def smooth_jnp(rho):
    return jnp.where(rho < 1.0, 1.875 - 1.25 * rho * rho + 0.375 * rho ** 4, 1.0 / jnp.maximum(rho, 1.0))

def stencil_full(level, shape, dtype):
    offsets = np.arange(-3, 4)
    grid_a, grid_b, grid_c = np.meshgrid(offsets, offsets, offsets, indexing='ij')
    radius = np.sqrt(grid_a ** 2.0 + grid_b ** 2.0 + grid_c ** 2.0)
    values = (smooth_numpy(radius / 1.5) / 1.5 - smooth_numpy(radius / 3.0) / 3.0) / 2.0 ** (level - 1)
    full = jnp.zeros(shape, dtype)
    return full.at[(grid_a % shape[0]).ravel(), (grid_b % shape[1]).ravel(), (grid_c % shape[2]).ravel()].set(jnp.asarray(values.ravel(), dtype))

def signed_offsets(count, dtype):
    places = jnp.arange(count).astype(dtype)
    return jnp.where(places > count // 2, places - count, places)

def coarse_kernel(shape, dtype):
    first = signed_offsets(shape[0], dtype)[:, None, None]
    second = signed_offsets(shape[1], dtype)[None, :, None]
    third = signed_offsets(shape[2], dtype)[None, None, :]
    radius = jnp.sqrt(first * first + second * second + third * third)
    return smooth_jnp(radius / 1.5) / 12.0

def periodic_convolve(field, kernel):
    return jnp.fft.irfftn(jnp.fft.rfftn(field) * jnp.fft.rfftn(kernel), s=field.shape).astype(field.dtype)

def restrict_grid(field):
    for axis in range(3):
        total = jnp.zeros_like(field)
        for offset, weight in restrict_taps:
            total = total + weight * jnp.roll(field, -offset, axis=axis)
        field = lax.slice_in_dim(total, 0, field.shape[axis], 2, axis)
    return field

def prolong_grid(field):
    for axis in range(3):
        odd_rows = 0.5625 * (field + jnp.roll(field, -1, axis=axis)) - 0.0625 * (jnp.roll(field, 1, axis=axis) + jnp.roll(field, -2, axis=axis))
        stacked = jnp.stack([field, odd_rows], axis=axis + 1)
        shape = list(field.shape)
        shape[axis] = 2 * shape[axis]
        field = stacked.reshape(shape)
    return field

def reference(charges, fractions, cells):
    total_x = CX * N_GX
    total_y = CY * N_GY
    per_plane = ATOMS_DEV // CX
    plane = jnp.arange(ATOMS_DEV, dtype=jnp.int32) // per_plane
    base_x = jnp.arange(N_GX, dtype=jnp.int32)[:, None, None] * CX + plane[None, None, :] + jnp.zeros((N_GX, N_GY, ATOMS_DEV), jnp.int32)
    base_y = cells[:, :, 0] - 1
    base_z = cells[:, :, 1] - 1
    weights_x = spline_weights(fractions[:, :, 0])
    weights_y = spline_weights(fractions[:, :, 1])
    weights_z = spline_weights(fractions[:, :, 2])
    flat_points = []
    level_one = jnp.zeros((total_x * total_y * NZ,), fractions.dtype)
    for tap_x in range(4):
        for tap_y in range(4):
            for tap_z in range(4):
                flat = ((base_x + tap_x) % total_x * total_y + (base_y + tap_y) % total_y) * NZ + (base_z + tap_z) % NZ
                flat = flat.astype(jnp.int32)
                product = weights_x[tap_x] * weights_y[tap_y] * weights_z[tap_z]
                flat_points.append((flat, product))
                level_one = level_one.at[flat.ravel()].add((charges * product).ravel())
    grids = [level_one.reshape(total_x, total_y, NZ)]
    for level in range(3):
        grids.append(restrict_grid(grids[-1]))
    potential = periodic_convolve(grids[3], coarse_kernel(grids[3].shape, grids[3].dtype))
    for level in (3, 2, 1):
        field = grids[level - 1]
        potential = periodic_convolve(field, stencil_full(level, field.shape, field.dtype)) + prolong_grid(potential)
    flat_potential = potential.reshape(-1)
    atom_values = jnp.zeros_like(charges)
    for flat, product in flat_points:
        atom_values = atom_values + product * flat_potential[flat]
    return (potential, atom_values)
```

```python
import functools

import jax
import jax.numpy as jnp
import numpy as np
from jax import lax
from jax.experimental import pallas as pl
from jax.experimental.pallas import tpu as pltpu
from jax.sharding import PartitionSpec as P

CX = 32
CY = 16
NZ = 128
ATOMS_DEV = 16384

HIGHEST = lax.Precision.HIGHEST
RESTRICT_TAPS = ((-3, -0.0625), (-1, 0.5625), (0, 1.0), (1, 0.5625), (3, -0.0625))
PER_PLANE = ATOMS_DEV // CX
LANES = 128
CHUNKS = PER_PLANE // LANES
Z2, Z3, Z4 = (NZ // 2, NZ // 4, NZ // 8)
LANE3 = Z2
LANE4 = Z2 + Z3

X1, Y1 = (0, CX + 3), (0, CY + 3)


def coarser(window):
    first, count = window
    last = first + count - 1
    starts = [m for m in range(first - 4, last + 4) if any(first <= 2 * m + k <= last for k, _ in RESTRICT_TAPS)]
    return (starts[0], starts[-1] - starts[0] + 1)


X2, Y2 = coarser(X1), coarser(Y1)
X3, Y3 = coarser(X2), coarser(Y2)
X4, Y4 = coarser(X3), coarser(Y3)


def up8(count):
    return -(-count // 8) * 8


YP1, YP2, YP3, YP4 = (up8(Y1[1]), up8(Y2[1]), up8(Y3[1]), up8(Y4[1]))
PAD = 8


def real_basis(count):
    places = np.arange(count)
    rows = [np.full(count, 1.0 / np.sqrt(count))]
    for k in range(1, count // 2):
        rows.append(np.sqrt(2.0 / count) * np.cos(2 * np.pi * k * places / count))
        rows.append(np.sqrt(2.0 / count) * np.sin(2 * np.pi * k * places / count))
    rows.append(np.where(places % 2 == 0, 1.0, -1.0) / np.sqrt(count))
    return np.stack(rows)


def basis_frequency(count):
    return np.array([0] + [k for k in range(1, count // 2) for _ in range(2)] + [count // 2])


def restrict_matrix(count):
    matrix = np.zeros((count // 2, count))
    for m in range(count // 2):
        for k, weight in RESTRICT_TAPS:
            matrix[m, (2 * m + k) % count] += weight
    return matrix


def depth_matrix():
    first = restrict_matrix(NZ)
    second = restrict_matrix(Z2) @ first
    third = restrict_matrix(Z3) @ second
    parts = [real_basis(NZ), real_basis(Z2) @ first, real_basis(Z3) @ second, real_basis(Z4) @ third]
    parts.append(np.zeros((2 * LANES - sum(p.shape[0] for p in parts), NZ)))
    return np.concatenate(parts, axis=0)


def smooth_numpy(rho):
    return np.where(rho < 1.0, 1.875 - 1.25 * rho * rho + 0.375 * rho**4, 1.0 / np.maximum(rho, 1.0))


def stencil_spectrum(level, count):
    offsets = np.arange(-3, 4) * 1.0
    near = np.arange(0, 4) * 1.0
    radius = np.sqrt(near[:, None, None] ** 2 + near[None, :, None] ** 2 + offsets[None, None, :] ** 2)
    stencil = (smooth_numpy(radius / 1.5) / 1.5 - smooth_numpy(radius / 3.0) / 3.0) / 2.0 ** (level - 1)
    waves = np.cos(2 * np.pi * offsets[:, None] * basis_frequency(count)[None, :] / count)
    return np.einsum("abd,dk->abk", stencil, waves)


def spectra():
    fine = stencil_spectrum(1, NZ).reshape(16, NZ)
    coarse = np.zeros((16, LANES))
    coarse[:, :Z2] = stencil_spectrum(2, Z2).reshape(16, Z2)
    coarse[:, LANE3:LANE4] = stencil_spectrum(3, Z3).reshape(16, Z3)
    return np.stack([fine, coarse])


def signed(count):
    places = np.arange(count)
    return np.where(places > count // 2, places - count, places) * 1.0


def coarse_tables(size_x, size_y):
    total_x = CX // 8 * size_x
    total_y = CY // 8 * size_y
    first = signed(total_x)[:, None, None]
    second = signed(total_y)[None, :, None]
    third = signed(Z4)[None, None, :]
    kernel = smooth_numpy(np.sqrt(first**2 + second**2 + third**2) / 1.5) / 12.0

    def cosines(count):
        return np.cos(2 * np.pi * basis_frequency(count)[:, None] * np.arange(count)[None, :] / count)

    spectrum = np.einsum("xyz,ax,by,cz->abc", kernel, cosines(total_x), cosines(total_y), cosines(Z4), optimize=True)
    spectrum = spectrum.reshape(total_x, total_y * Z4)
    basis_x = real_basis(total_x)
    basis_y = np.kron(real_basis(total_y), np.eye(Z4))
    span = X4[1]
    tail = up8(size_x)
    gather = np.zeros((total_x, 8 * size_x + tail))
    window = np.zeros((size_x, up8(span), total_x))
    for i in range(size_x):
        for a in range(span):
            place = (i * (CX // 8) + X4[0] + a) % total_x
            gather[:, i * 8 + a if a < 8 else 8 * size_x + i] = basis_x[:, place]
            window[i, a, :] = basis_x[:, place]
    return [t.astype(np.float32) for t in (gather, basis_y, spectrum, window)]


def spline_weights(frac):
    def near_weight(distance):
        return (1.0 - distance) * (1.0 + distance - 1.5 * distance * distance)

    def far_weight(distance):
        return -0.5 * (distance - 1.0) * (2.0 - distance) * (2.0 - distance)

    return [far_weight(1.0 + frac), near_weight(frac), near_weight(1.0 - frac), far_weight(2.0 - frac)]


def plane_rows(frac_ref, cell_ref, start, first_y, total_y):
    frac = frac_ref[0, 0, :, pl.ds(start, PER_PLANE)]
    cell = cell_ref[0, 0, :, pl.ds(start, PER_PLANE)]
    weights = spline_weights(frac)
    block_y = cell[0:1] - first_y
    block_y = jnp.where(block_y < 0, block_y + total_y, block_y)
    depth = []
    for tap in range(4):
        place = cell[1:2] + (tap - 1)
        place = jnp.where(place < 0, place + NZ, place)
        depth.append(jnp.where(place >= NZ, place - NZ, place))
    return weights, block_y, depth


def along_y(weights, block_y, lanes):
    places = lax.broadcasted_iota(jnp.int32, (YP1, LANES), 0)
    offset = places - block_y[:, lanes]
    table = jnp.zeros((YP1, LANES), jnp.float32)
    for tap in range(4):
        table = jnp.where(offset == tap, weights[tap][1:2, lanes], table)
    return table


def along_z(weights, depth, lanes):
    places = lax.broadcasted_iota(jnp.int32, (NZ, LANES), 0).astype(jnp.bfloat16).reshape(NZ // 16, 16, LANES)
    high = jnp.zeros((NZ // 16, 16, LANES), jnp.bfloat16)
    low = jnp.zeros((NZ // 16, 16, LANES), jnp.bfloat16)
    for tap in range(4):
        place = jnp.broadcast_to(depth[tap][:, lanes].astype(jnp.float32), (16, LANES)).astype(jnp.bfloat16)
        weight = jnp.broadcast_to(weights[tap][2:3, lanes], (16, LANES))
        weight_high = weight.astype(jnp.bfloat16)
        weight_low = (weight - weight_high.astype(jnp.float32)).astype(jnp.bfloat16)
        same = places == place[None]
        high = jnp.where(same, weight_high[None], high)
        low = jnp.where(same, weight_low[None], low)
    return high.reshape(NZ, LANES), low.reshape(NZ, LANES)


def halves(value):
    high = value.astype(jnp.bfloat16)
    low = (value - high.astype(jnp.float32)).astype(jnp.bfloat16)
    return high, low


def lane_index(shape):
    return lax.broadcasted_iota(jnp.int32, shape, len(shape) - 1)


def restrict_x(load, window_in, window_out):
    first, count = window_in
    outs = []
    for m in range(window_out[0], window_out[0] + window_out[1]):
        total = None
        for k, weight in RESTRICT_TAPS:
            place = 2 * m + k - first
            if 0 <= place < count:
                term = load(place) if weight == 1.0 else weight * load(place)
                total = term if total is None else total + term
        outs.append(total)
    return outs


def restrict_y(source, window_in, window_out, rows_out):
    total = None
    for k, weight in RESTRICT_TAPS:
        start = 2 * window_out[0] + k - window_in[0] + PAD
        term = source[:, pl.ds(start, rows_out, stride=2), :]
        term = term if weight == 1.0 else weight * term
        total = term if total is None else total + term
    places = lax.broadcasted_iota(jnp.int32, total.shape, 1)
    return jnp.where(places < window_out[1], total, 0.0)


def deposit_kernel(
    place_ref, charge_ref, frac_ref, cell_ref, depth_ref,
    raw_ref, part_ref, low_ref, high_ref, message_ref,
    grid, coarse, half2, half3, half4, last,
    *, total_y, devices,
):
    first_y = place_ref[1] * CY + 1
    grid[...] = jnp.zeros_like(grid)

    def step(plane, carry):
        start = pl.multiple_of(plane * PER_PLANE, PER_PLANE)
        weights, block_y, depth = plane_rows(frac_ref, cell_ref, start, first_y, total_y)
        charge = charge_ref[0, 0:1, pl.ds(start, PER_PLANE)]
        lefts, rights = [], []
        for chunk in range(CHUNKS):
            lanes = slice(chunk * LANES, (chunk + 1) * LANES)
            table = along_y(weights, block_y, lanes)
            spread = jnp.concatenate([table * (charge * weights[m][0:1])[:, lanes] for m in range(4)], axis=0)
            lefts.append(jnp.concatenate(halves(spread), axis=0))
            rights.append(jnp.concatenate(along_z(weights, depth, lanes), axis=0))
        left = jnp.concatenate(lefts, axis=1)
        right = jnp.concatenate(rights, axis=1)
        product = lax.dot_general(left, right, (((1,), (1,)), ((), ())), preferred_element_type=jnp.float32)
        rows = 4 * YP1
        layers = product[:rows, :NZ] + (product[:rows, NZ:] + product[rows:, :NZ] + product[rows:, NZ:])
        for m in range(4):
            grid[plane + m] = grid[plane + m] + layers[m * YP1 : (m + 1) * YP1]
        return carry

    lax.fori_loop(0, CX, step, 0)
    flat = grid[...].reshape(X1[1] * YP1, NZ)
    table = depth_ref[...]
    deep = (((1,), (1,)), ((), ()))
    raw = lax.dot_general(flat, table[:LANES], deep, precision=HIGHEST, preferred_element_type=jnp.float32)
    raw_ref[...] = raw.reshape(X1[1], YP1, LANES)
    below = lax.dot_general(flat, table[LANES:], deep, precision=HIGHEST, preferred_element_type=jnp.float32)
    coarse[...] = below.reshape(X1[1], YP1, LANES)

    def padded(half, outs, rows):
        half[...] = jnp.zeros_like(half)
        for i, value in enumerate(outs):
            half[i, PAD : PAD + rows, :] = value

    padded(half2, restrict_x(lambda i: coarse[i], X1, X2), YP1)
    level2 = restrict_y(half2, Y1, Y2, YP2)
    padded(half3, restrict_x(lambda i: level2[i], X2, X3), YP2)
    level3 = restrict_y(half3, Y2, Y3, YP3)
    padded(half4, restrict_x(lambda i: level3[i], X3, X4), YP3)
    last[...] = restrict_y(half4, Y3, Y4, YP4).reshape(X4[1] * YP4, LANES)

    lane2 = lane_index((YP2, LANES)) < Z2
    for i in range(X2[1]):
        other = level3[i] if i < X3[1] else jnp.zeros((YP2, LANES), jnp.float32)
        part_ref[i] = jnp.where(lane2, level2[i], other)
    for r in range(6):
        low_ref[r * YP1 : (r + 1) * YP1] = raw_ref[r]
        high_ref[r * YP1 : (r + 1) * YP1] = raw_ref[CX - 3 + r]
    for r in range(8):
        base = 6 * YP1 + r * YP2
        low_ref[base : base + YP2] = part_ref[r]
        two = part_ref[CX // 2 - 4 - X2[0] + r] if r < 7 else jnp.zeros((YP2, LANES), jnp.float32)
        high_ref[base : base + YP2] = jnp.where(lane2, two, part_ref[CX // 4 - 5 - X3[0] + r])
    lanes = lane_index((8, LANES))
    message = jnp.zeros((8, LANES), jnp.float32)
    for b in range(Y4[1]):
        rows = last[pl.ds(b, 8, stride=YP4), :]
        moved = pltpu.roll(rows, (b * Z4 - LANE4) % LANES, 1)
        message = jnp.where((lanes >= b * Z4) & (lanes < (b + 1) * Z4), moved, message)
    tail = pltpu.roll(last[8 * YP4 : 9 * YP4, :], Y4[1] * Z4 - LANE4, 1)
    message = jnp.where(lanes >= Y4[1] * Z4, tail, message)
    for d in range(devices):
        message_ref[d] = message


def merge_x_kernel(raw_ref, part_ref, below_ref, above_ref, fine_ref, pair_ref, up_ref, down_ref, up2_ref, down2_ref):
    lane2 = lane_index((YP2, LANES)) < Z2
    for r in range(X1[1]):
        fine_ref[3 + r] = raw_ref[r]
    for r in range(6):
        slab = slice(r * YP1, (r + 1) * YP1)
        if r < 3:
            fine_ref[r] = below_ref[slab]
            fine_ref[CX + 3 + r] = fine_ref[CX + 3 + r] + above_ref[slab]
        else:
            fine_ref[r] = fine_ref[r] + below_ref[slab]
            fine_ref[CX + 3 + r] = above_ref[slab]
    count = CX // 2 + 10
    pair_ref[...] = jnp.zeros_like(pair_ref)
    for r in range(X2[1]):
        pair_ref[3 + r] = part_ref[r]
    for r in range(8):
        slab = slice(6 * YP1 + r * YP2, 6 * YP1 + (r + 1) * YP2)
        pair_ref[r] = pair_ref[r] + below_ref[slab]
        at3 = CX // 4 + 3 + r
        pair_ref[at3] = pair_ref[at3] + jnp.where(lane2, 0.0, above_ref[slab])
        at2 = CX // 2 + 3 + r
        if at2 < count:
            pair_ref[at2] = pair_ref[at2] + jnp.where(lane2, above_ref[slab], 0.0)
    rows = X1[1] + 6
    narrow2 = lane_index((8, LANES)) < Z2
    for r in range(rows):
        up_ref[r] = fine_ref[r, CY - 3 : CY + 5, :]
        down_ref[r] = fine_ref[r, 0:8, :]
    row = lax.broadcasted_iota(jnp.int32, (8, LANES), 0)
    for r in range(count):
        two = jnp.where(row < 7, pair_ref[r, CY // 2 - 3 : CY // 2 + 5, :], 0.0)
        up_ref[rows + r] = jnp.where(narrow2, two, pair_ref[r, CY // 4 - 3 : CY // 4 + 5, :])
        down_ref[rows + r] = pair_ref[r, 0:8, :]
    span = CX // 4 + 11
    packed = (span + 1) // 2
    for r in range(span):
        at = slice(4 * (r // packed), 4 * (r // packed) + 4)
        up2_ref[r % packed, at, :] = pair_ref[r, CY // 2 - 3 : CY // 2 + 1, :]
        down2_ref[r % packed, at, :] = pair_ref[r, 0:4, :]
    if span % 2:
        up2_ref[packed - 1, 4:8, :] = jnp.zeros((4, LANES), jnp.float32)
        down2_ref[packed - 1, 4:8, :] = jnp.zeros((4, LANES), jnp.float32)


def stencil_rows(source, count, rows_out, table, out_ref, planes):
    total = count + 6

    def terms(i):
        sums = [source[i, 3 : 3 + rows_out, :]]
        for b in range(1, 4):
            sums.append(source[i, 3 - b : 3 - b + rows_out, :] + source[i, 3 + b : 3 + b + rows_out, :])
        for a in range(4):
            value = table[4 * a : 4 * a + 1] * sums[0]
            for b in range(1, 4):
                value = value + table[4 * a + b : 4 * a + b + 1] * sums[b]
            planes[a, i] = value

    def first(i, carry):
        terms(i)
        return carry

    lax.fori_loop(0, total, first, 0)

    def second(i, carry):
        value = planes[0, i + 3]
        for a in range(1, 4):
            value = value + (planes[a, i + 3 - a] + planes[a, i + 3 + a])
        out_ref[i] = value
        return carry

    lax.fori_loop(0, count, second, 0)


def stencil_kernel(
    fine_ref, pair_ref, below_ref, above_ref, below2_ref, above2_ref, spectrum_ref,
    smooth_ref, smooth_pair_ref,
    fine, pair, planes, planes_pair,
):
    rows = X1[1] + 6
    count = CX // 2 + 10
    fine[:, YP1 + 3 :, :] = jnp.zeros((rows, 32 - YP1 - 3, LANES), jnp.float32)
    fine[:, 0:3, :] = jnp.zeros((rows, 3, LANES), jnp.float32)
    fine[:, 3 : 3 + YP1, :] = fine_ref[...]
    fine[:, 0:6, :] = fine[:, 0:6, :] + below_ref[0:rows, 0:6, :]
    fine[:, CY + 3 : CY + 9, :] = fine[:, CY + 3 : CY + 9, :] + above_ref[0:rows, 0:6, :]
    pair[...] = jnp.zeros_like(pair)
    pair[:, 3 : 3 + YP2, :] = pair_ref[...]
    pair[:, 0:8, :] = pair[:, 0:8, :] + below_ref[rows:, :, :]
    lane2 = lane_index((count, 8, LANES)) < Z2
    above = above_ref[rows:, :, :]
    at2, at3 = (CY // 2 + 3, CY // 4 + 3)
    pair[:, at2 : at2 + 8, :] = pair[:, at2 : at2 + 8, :] + jnp.where(lane2, above, 0.0)
    pair[:, at3 : at3 + 8, :] = pair[:, at3 : at3 + 8, :] + jnp.where(lane2, 0.0, above)
    span = CX // 4 + 11
    packed = (span + 1) // 2
    lane3 = lane_index((4, LANES))
    lane3 = (lane3 >= LANE3) & (lane3 < LANE4)
    far = CY // 2 + 3
    for r in range(span):
        at = slice(4 * (r // packed), 4 * (r // packed) + 4)
        pair[r, 0:4, :] = pair[r, 0:4, :] + jnp.where(lane3, below2_ref[r % packed, at, :], 0.0)
        pair[r, far : far + 4, :] = pair[r, far : far + 4, :] + jnp.where(lane3, above2_ref[r % packed, at, :], 0.0)
    stencil_rows(fine, X1[1], YP1, spectrum_ref[0], smooth_ref, planes)
    stencil_rows(pair, X2[1], YP2, spectrum_ref[1], smooth_pair_ref, planes_pair)


def prolong_x(load, window_in, window_out):
    outs = []
    first = window_in[0]
    for n in range(window_out[0], window_out[0] + window_out[1]):
        if n % 2 == 0:
            outs.append(load(n // 2 - first))
        else:
            m = (n - 1) // 2 - first
            outs.append(0.5625 * (load(m) + load(m + 1)) - 0.0625 * (load(m - 1) + load(m + 2)))
    return outs


def prolong_y(source, window_in, window_out, target):
    first, count = window_out
    even = first % 2
    evens = (count - even + 1) // 2
    start = (first + even) // 2 - window_in[0]
    target[:, pl.ds(even, evens, stride=2), :] = source[:, start : start + evens, :]
    odds = count - evens
    m = (first + 1 - even - 1) // 2 - window_in[0]

    def taken(shift):
        return source[:, m + shift : m + shift + odds, :]

    target[:, pl.ds(1 - even, odds, stride=2), :] = 0.5625 * (taken(0) + taken(1)) - 0.0625 * (taken(-1) + taken(2))


def field_kernel(
    place_ref, message_ref, gather_ref, basis_ref, spectrum_ref, window_ref, smooth_ref, pair_ref, depth_ref,
    frac_ref, cell_ref,
    potential_ref, atom_ref,
    ninth, level4, half3, level3, half2, level2, half1, level1, field,
    *, size_x, size_y,
):
    total_y = CY * size_y
    devices = size_x * size_y
    width = CY // 8 * size_y * Z4
    blocks = width // LANES
    lanes8 = lane_index((8, LANES))
    used = Y4[1] * Z4
    tails = lane_index((devices, LANES))
    gathered = jnp.zeros((devices, LANES), jnp.float32)
    for b in range(Y4[1]):
        rows = message_ref[pl.ds(b, devices, stride=8), :]
        moved = pltpu.roll(rows, (b * Z4 - used) % LANES, 1)
        gathered = jnp.where((tails >= b * Z4) & (tails < (b + 1) * Z4), moved, gathered)
    ninth[...] = gathered

    def assemble(load, rows):
        total = [jnp.zeros((rows, LANES), jnp.float32) for _ in range(blocks)]
        lanes = lane_index((rows, LANES))
        for j in range(size_y):
            position = (j * (CY // 8) + Y4[0]) * Z4 % width
            block, offset = (position // LANES, position % LANES)
            value = jnp.where(lanes < used, load(j), 0.0)
            if offset == 0:
                total[block] = total[block] + value
                continue
            value = pltpu.roll(value, offset, 1)
            following = (block + 1) % blocks
            total[block] = total[block] + jnp.where(lanes >= offset, value, 0.0)
            total[following] = total[following] + jnp.where(lanes < offset, value, 0.0)
        return jnp.concatenate(total, axis=1)

    strips = []
    for i in range(size_x):
        strips.append(assemble(lambda j: message_ref[(i * size_y + j) * 8 : (i * size_y + j + 1) * 8, :], 8))
    tail = assemble(lambda j: ninth[pl.ds(j, size_x, stride=size_y), :], size_x)
    if size_x % 8:
        tail = jnp.concatenate([tail, jnp.zeros((8 - size_x % 8, width), jnp.float32)], axis=0)
    strips.append(tail)
    strips = jnp.concatenate(strips, axis=0)
    exact = dict(precision=HIGHEST, preferred_element_type=jnp.float32)
    modes = jnp.dot(gather_ref[...], strips, **exact)
    modes = lax.dot_general(modes, basis_ref[...], (((1,), (1,)), ((), ())), **exact)
    modes = jnp.dot(modes * spectrum_ref[...], basis_ref[...], **exact)
    shift = (width - (place_ref[1] * (CY // 8) + Y4[0]) * Z4) % width
    modes = pltpu.roll(modes, shift, 1)[:, :LANES]
    own = jnp.dot(window_ref[place_ref[0]], modes, **exact)
    lanes = lane_index(own.shape)
    inside4 = (lanes >= LANE4) & (lanes < LANE4 + Z4)
    level4[...] = jnp.zeros_like(level4)
    for b in range(Y4[1]):
        moved = jnp.where(inside4, pltpu.roll(own, (LANE4 - b * Z4) % LANES, 1), 0.0)
        level4[pl.ds(b, X4[1], stride=YP4), :] = moved[: X4[1]]

    def rise(load, window_in, window_out, wide_in, wide_out, half, target):
        target[...] = jnp.zeros_like(target)
        for r, value in enumerate(prolong_x(load, window_in, window_out)):
            half[r] = value
        prolong_y(half, wide_in, wide_out, target)

    rise(lambda i: level4[i * YP4 : (i + 1) * YP4, :], X4, X3, Y4, Y3, half3, level3)
    lanes3 = lane_index((YP3, LANES))
    inside3 = (lanes3 >= LANE3) & (lanes3 < LANE4)
    for r in range(X3[1]):
        level3[r] = level3[r] + jnp.where(inside3, pair_ref[r, 0:YP3, :], 0.0)
    rise(lambda i: level3[i], X3, X2, Y3, Y2, half2, level2)
    inside2 = lane_index((YP2, LANES)) < Z2
    for r in range(X2[1]):
        level2[r] = level2[r] + jnp.where(inside2, pair_ref[r], 0.0)
    rise(lambda i: level2[i], X2, X1, Y2, Y1, half1, level1)

    table = depth_ref[...]
    rows = X1[1] * YP1
    total = jnp.dot(smooth_ref[...].reshape(rows, LANES), table[:LANES], **exact)
    total = total + jnp.dot(level1[...].reshape(rows, LANES), table[LANES:], **exact)
    field[...] = total.reshape(X1[1], YP1, NZ)
    potential_ref[...] = field[0:CX, 0:CY, :]

    first_y = place_ref[1] * CY + 1

    def step(plane, carry):
        start = pl.multiple_of(plane * PER_PLANE, PER_PLANE)
        weights, block_y, depth = plane_rows(frac_ref, cell_ref, start, first_y, total_y)
        high, low = halves(jnp.concatenate([field[plane + m] for m in range(4)], axis=0))
        left = jnp.concatenate(
            [jnp.concatenate([high, high], axis=1), jnp.concatenate([low, low], axis=1)], axis=0
        )
        right = jnp.concatenate(
            [
                jnp.concatenate(along_z(weights, depth, slice(c * LANES, (c + 1) * LANES)), axis=0)
                for c in range(CHUNKS)
            ],
            axis=1,
        )
        product = jnp.dot(left, right, preferred_element_type=jnp.float32)
        sums = []
        for c in range(CHUNKS):
            lanes = slice(c * LANES, (c + 1) * LANES)
            total = jnp.zeros((YP1, LANES), jnp.float32)
            for m in range(4):
                layer = product[m * YP1 : (m + 1) * YP1, lanes] + product[(4 + m) * YP1 : (5 + m) * YP1, lanes]
                total = total + layer * weights[m][0:1, lanes]
            sums.append(jnp.sum(total * along_y(weights, block_y, lanes), axis=0, keepdims=True))
        atom_ref[0, 0:1, pl.ds(start, PER_PLANE)] = jnp.concatenate(sums, axis=1)
        return carry

    lax.fori_loop(0, CX, step, 0)


VM = pl.BlockSpec(memory_space=pltpu.VMEM)
SM = pl.BlockSpec(memory_space=pltpu.SMEM)


def f32(*shape):
    return jax.ShapeDtypeStruct(shape, jnp.float32)


def scratch(*shape):
    return pltpu.VMEM(shape, jnp.float32)


def shifted(value, axis, steps):
    count = lax.axis_size(axis)
    return lax.ppermute(value, axis, [(source, (source + steps) % count) for source in range(count)])


def local(charges, fractions, cells, interpret=False):
    size_x = lax.axis_size("gx")
    size_y = lax.axis_size("gy")
    devices = size_x * size_y
    place = jnp.stack([lax.axis_index("gx"), lax.axis_index("gy")]).astype(jnp.int32)
    depth = jnp.asarray(depth_matrix().astype(np.float32))
    gather, basis, coarse_spectrum, window = (jnp.asarray(t) for t in coarse_tables(size_x, size_y))
    slab = 6 * YP1 + 8 * YP2
    raw, part, low, high, message = pl.pallas_call(
        functools.partial(deposit_kernel, total_y=CY * size_y, devices=devices),
        in_specs=[SM, VM, VM, VM, VM],
        out_specs=[VM] * 5,
        out_shape=[
            f32(X1[1], YP1, LANES),
            f32(X2[1], YP2, LANES),
            f32(slab, LANES),
            f32(slab, LANES),
            f32(devices, 8, LANES),
        ],
        scratch_shapes=[
            scratch(X1[1], YP1, NZ),
            scratch(X1[1], YP1, LANES),
            scratch(X2[1], YP1 + 16, LANES),
            scratch(X3[1], YP2 + 24, LANES),
            scratch(X4[1], YP3 + 16, LANES),
            scratch(X4[1] * YP4, LANES),
        ],
        interpret=interpret,
        name="deposit",
    )(place, charges, fractions, cells, depth)
    everyone = lax.all_to_all(message, ("gx", "gy"), 0, 0)
    below = shifted(high, "gx", 1)
    above = shifted(low, "gx", -1)
    rows = X1[1] + 6
    count = CX // 2 + 10
    packed = (CX // 4 + 12) // 2
    fine, pair, up, down, up2, down2 = pl.pallas_call(
        merge_x_kernel,
        in_specs=[VM] * 4,
        out_specs=[VM] * 6,
        out_shape=[
            f32(rows, YP1, LANES),
            f32(count, YP2, LANES),
            f32(rows + count, 8, LANES),
            f32(rows + count, 8, LANES),
            f32(packed, 8, LANES),
            f32(packed, 8, LANES),
        ],
        interpret=interpret,
        name="merge_x",
    )(raw, part, below, above)
    below = shifted(up, "gy", 1)
    above = shifted(down, "gy", -1)
    below2 = shifted(up2, "gy", 2)
    above2 = shifted(down2, "gy", -2)
    smooth, smooth_pair = pl.pallas_call(
        stencil_kernel,
        in_specs=[VM] * 7,
        out_specs=[VM] * 2,
        out_shape=[f32(X1[1], YP1, LANES), f32(X2[1], YP2, LANES)],
        scratch_shapes=[
            scratch(rows, 32, LANES),
            scratch(count, 24, LANES),
            scratch(4, rows, YP1, LANES),
            scratch(4, count, YP2, LANES),
        ],
        interpret=interpret,
        name="stencils",
    )(fine, pair, below, above, below2, above2, jnp.asarray(spectra().astype(np.float32)))
    potential, atoms = pl.pallas_call(
        functools.partial(field_kernel, size_x=size_x, size_y=size_y),
        in_specs=[SM] + [VM] * 10,
        out_specs=[VM] * 2,
        out_shape=[f32(CX, CY, NZ), f32(1, 1, ATOMS_DEV)],
        scratch_shapes=[
            scratch(devices, LANES),
            scratch(X4[1] * YP4, LANES),
            scratch(X3[1], YP4, LANES),
            scratch(X3[1], YP3, LANES),
            scratch(X2[1], YP3, LANES),
            scratch(X2[1], YP2, LANES),
            scratch(X1[1], YP2, LANES),
            scratch(X1[1], YP1, LANES),
            scratch(X1[1], YP1, NZ),
        ],
        interpret=interpret,
        name="field",
    )(
        place, everyone.reshape(devices * 8, LANES), gather, basis, coarse_spectrum, window, smooth, smooth_pair, depth,
        fractions, cells,
    )
    return (potential, atoms)


def solution(mesh):
    placed = (P("gx", "gy", None), P("gx", "gy", None, None), P("gx", "gy", None, None))
    return jax.shard_map(
        local,
        mesh=mesh,
        in_specs=placed,
        out_specs=(P("gx", "gy", None), P("gx", "gy", None)),
        check_vma=False,
    )
```

```python
import functools

import jax
import jax.numpy as jnp
import numpy as np
from jax import lax
from jax.experimental import pallas as pl
from jax.experimental.pallas import tpu as pltpu
from jax.sharding import PartitionSpec as P

CX = 32
CY = 16
NZ = 128
ATOMS_DEV = 16384

HIGHEST = lax.Precision.HIGHEST
RESTRICT_TAPS = ((-3, -0.0625), (-1, 0.5625), (0, 1.0), (1, 0.5625), (3, -0.0625))
PER_PLANE = ATOMS_DEV // CX
LANES = 128
CHUNKS = PER_PLANE // LANES
Z2, Z3, Z4 = (NZ // 2, NZ // 4, NZ // 8)
LANE3 = Z2
LANE4 = Z2 + Z3

X1, Y1 = (0, CX + 3), (0, CY + 3)


def coarser(window):
    first, count = window
    last = first + count - 1
    starts = [m for m in range(first - 4, last + 4) if any(first <= 2 * m + k <= last for k, _ in RESTRICT_TAPS)]
    return (starts[0], starts[-1] - starts[0] + 1)


X2, Y2 = coarser(X1), coarser(Y1)
X3, Y3 = coarser(X2), coarser(Y2)
X4, Y4 = coarser(X3), coarser(Y3)


def up8(count):
    return -(-count // 8) * 8


SLAB2 = 6 * Y1[1]
SLAB3 = SLAB2 + 4 * Y2[1]
SLAB = up8(SLAB3 + 2 * Y3[1])
FINE_X = X1[1] + 6
PAIR_X = CX // 2 + 10
SPAN3 = CX // 4 + 11
PACK2 = (PAIR_X + 1) // 2
PACK3 = (SPAN3 + 3) // 4
EDGE2 = up8(6 * FINE_X)
EDGE3 = EDGE2 + 8 * PACK2
EDGE = EDGE3 + 8 * PACK3
FAR = up8(4 * PACK3)
YP1, YP2, YP3, YP4 = (up8(Y1[1]), up8(Y2[1]), up8(Y3[1]), up8(Y4[1]))
PAD = 8


def real_basis(count):
    places = np.arange(count)
    rows = [np.full(count, 1.0 / np.sqrt(count))]
    for k in range(1, count // 2):
        rows.append(np.sqrt(2.0 / count) * np.cos(2 * np.pi * k * places / count))
        rows.append(np.sqrt(2.0 / count) * np.sin(2 * np.pi * k * places / count))
    rows.append(np.where(places % 2 == 0, 1.0, -1.0) / np.sqrt(count))
    return np.stack(rows)


def basis_frequency(count):
    return np.array([0] + [k for k in range(1, count // 2) for _ in range(2)] + [count // 2])


def restrict_matrix(count):
    matrix = np.zeros((count // 2, count))
    for m in range(count // 2):
        for k, weight in RESTRICT_TAPS:
            matrix[m, (2 * m + k) % count] += weight
    return matrix


def depth_matrix():
    first = restrict_matrix(NZ)
    second = restrict_matrix(Z2) @ first
    third = restrict_matrix(Z3) @ second
    parts = [real_basis(NZ), real_basis(Z2) @ first, real_basis(Z3) @ second, real_basis(Z4) @ third]
    parts.append(np.zeros((2 * LANES - sum(p.shape[0] for p in parts), NZ)))
    return np.concatenate(parts, axis=0)


def split_numpy(value):
    high = value.astype(np.float32).astype(jnp.bfloat16)
    low = (value - high.astype(np.float64)).astype(np.float32).astype(jnp.bfloat16)
    return high, low


def depth_tables():
    high, low = split_numpy(depth_matrix())
    down = np.concatenate([high.T, high.T, low.T], axis=0)
    up = np.concatenate([high, high, low], axis=0)
    return jnp.asarray(down), jnp.asarray(up)


def smooth_numpy(rho):
    return np.where(rho < 1.0, 1.875 - 1.25 * rho * rho + 0.375 * rho**4, 1.0 / np.maximum(rho, 1.0))


def stencil_spectrum(level, count):
    offsets = np.arange(-3, 4) * 1.0
    near = np.arange(0, 4) * 1.0
    radius = np.sqrt(near[:, None, None] ** 2 + near[None, :, None] ** 2 + offsets[None, None, :] ** 2)
    stencil = (smooth_numpy(radius / 1.5) / 1.5 - smooth_numpy(radius / 3.0) / 3.0) / 2.0 ** (level - 1)
    waves = np.cos(2 * np.pi * offsets[:, None] * basis_frequency(count)[None, :] / count)
    return np.einsum("abd,dk->abk", stencil, waves)


def spectra():
    fine = stencil_spectrum(1, NZ).reshape(16, NZ)
    coarse = np.zeros((16, LANES))
    coarse[:, :Z2] = stencil_spectrum(2, Z2).reshape(16, Z2)
    coarse[:, LANE3:LANE4] = stencil_spectrum(3, Z3).reshape(16, Z3)
    return np.stack([fine, coarse])


def signed(count):
    places = np.arange(count)
    return np.where(places > count // 2, places - count, places) * 1.0


def coarse_tables(size_x, size_y):
    total_x = CX // 8 * size_x
    total_y = CY // 8 * size_y
    first = signed(total_x)[:, None, None]
    second = signed(total_y)[None, :, None]
    third = signed(Z4)[None, None, :]
    kernel = smooth_numpy(np.sqrt(first**2 + second**2 + third**2) / 1.5) / 12.0

    def cosines(count):
        return np.cos(2 * np.pi * basis_frequency(count)[:, None] * np.arange(count)[None, :] / count)

    spectrum = np.einsum("xyz,ax,by,cz->abc", kernel, cosines(total_x), cosines(total_y), cosines(Z4), optimize=True)
    spectrum = spectrum.reshape(total_x, total_y * Z4)
    basis_x = real_basis(total_x)
    basis_y = np.kron(real_basis(total_y), np.eye(Z4))
    span = X4[1]
    tail = up8(size_x)
    gather = np.zeros((total_x, 8 * size_x + tail))
    window = np.zeros((size_x, up8(span), total_x))
    for i in range(size_x):
        for a in range(span):
            place = (i * (CX // 8) + X4[0] + a) % total_x
            gather[:, i * 8 + a if a < 8 else 8 * size_x + i] = basis_x[:, place]
            window[i, a, :] = basis_x[:, place]
    return [t.astype(np.float32) for t in (gather, basis_y, spectrum, window)]


def spline_weights(frac):
    def near_weight(distance):
        return (1.0 - distance) * (1.0 + distance - 1.5 * distance * distance)

    def far_weight(distance):
        return -0.5 * (distance - 1.0) * (2.0 - distance) * (2.0 - distance)

    return [far_weight(1.0 + frac), near_weight(frac), near_weight(1.0 - frac), far_weight(2.0 - frac)]


ROWS = ATOMS_DEV // LANES
GROUP = 4
TILES_Y = YP1 // 8
TILES_Z = NZ // 16
REAL_X, REAL_Y, REAL_Z, REAL_TY, REAL_TZ = 0, 4, 8, 12, 14
REALS, PLACES = 16, 8


def fill_tables(reals, places, charge, frac_ref, cell_ref, total_y):
    first_y = lax.axis_index("gy") * CY + 1

    def put(ref, index, value):
        ref[index * ROWS : (index + 1) * ROWS, :] = value

    for dim, base in ((0, REAL_X), (1, REAL_Y), (2, REAL_Z)):
        weights = spline_weights(frac_ref[dim])
        for tap in range(4):
            put(reals, base + tap, weights[tap] if charge is None or dim else weights[tap] * charge)
    block_y = cell_ref[pl.ds(0, ROWS, stride=2), :] - first_y
    block_y = jnp.where(block_y < 0, block_y + total_y, block_y)
    block_z = (cell_ref[pl.ds(1, ROWS, stride=2), :] - 1) & (NZ - 1)
    for tap in range(4):
        put(places, tap, (block_y + tap) & 7)
        put(places, 4 + tap, (block_z + tap) & 15)
    tile_y = block_y >> 3
    tile_z = block_z >> 4
    put(reals, REAL_TY, tile_y.astype(jnp.float32))
    put(reals, REAL_TY + 1, (tile_y + 1).astype(jnp.float32))
    put(reals, REAL_TZ, tile_z.astype(jnp.float32))
    put(reals, REAL_TZ + 1, ((tile_z + 1) & (TILES_Z - 1)).astype(jnp.float32))


def spread_row(ref, index, row):
    return ref[pl.ds(index * ROWS + row, 8, stride=0), :]


def pattern_y(reals, places, row):
    index = lax.broadcasted_iota(jnp.int32, (8, LANES), 0)
    table = jnp.zeros((8, LANES), jnp.float32)
    for tap in range(4):
        place = spread_row(places, tap, row)
        table = jnp.where(index == place, spread_row(reals, REAL_Y + tap, row), table)
    start = spread_row(places, 0, row)
    tile = jnp.where(index >= start, spread_row(reals, REAL_TY, row), spread_row(reals, REAL_TY + 1, row))
    return table, tile


def along_z(reals, places, row):
    index = lax.broadcasted_iota(jnp.int32, (8, LANES), 0)
    parts, tiles = [], []
    for half in range(2):
        table = jnp.zeros((8, LANES), jnp.float32)
        for tap in range(4):
            place = spread_row(places, 4 + tap, row)
            table = jnp.where(index + 8 * half == place, spread_row(reals, REAL_Z + tap, row), table)
        start = spread_row(places, 4, row)
        tiles.append(
            jnp.where(index + 8 * half >= start, spread_row(reals, REAL_TZ, row), spread_row(reals, REAL_TZ + 1, row))
        )
        parts.append(table)
    high, low = halves(jnp.concatenate(parts, axis=0))
    tile = jnp.concatenate(tiles, axis=0).astype(jnp.bfloat16)
    zero = jnp.zeros((16, LANES), jnp.bfloat16)
    highs, lows = [], []
    for t in range(TILES_Z):
        same = tile == jnp.bfloat16(t)
        highs.append(jnp.where(same, high, zero))
        lows.append(jnp.where(same, low, zero))
    return highs, lows


def along_xy(reals, places, row):
    table, tile = pattern_y(reals, places, row)
    tile = jnp.concatenate([tile, tile], axis=0).astype(jnp.bfloat16)
    zero = jnp.zeros((16, LANES), jnp.bfloat16)
    same = [tile == jnp.bfloat16(t) for t in range(TILES_Y)]
    highs, lows = [], []
    for pair in range(2):
        both = [table * spread_row(reals, REAL_X + 2 * pair + m, row) for m in range(2)]
        high, low = halves(jnp.concatenate(both, axis=0))
        highs += [jnp.where(mask, high, zero) for mask in same]
        lows += [jnp.where(mask, low, zero) for mask in same]
    return highs + lows


def triple(value):
    high, low = halves(value)
    return jnp.concatenate([high, low, high], axis=1)


def halves(value):
    high = value.astype(jnp.bfloat16)
    low = (value - high.astype(jnp.float32)).astype(jnp.bfloat16)
    return high, low


def lane_index(shape):
    return lax.broadcasted_iota(jnp.int32, shape, len(shape) - 1)


def restrict_x(load, window_in, window_out):
    first, count = window_in
    outs = []
    for m in range(window_out[0], window_out[0] + window_out[1]):
        total = None
        for k, weight in RESTRICT_TAPS:
            place = 2 * m + k - first
            if 0 <= place < count:
                term = load(place) if weight == 1.0 else weight * load(place)
                total = term if total is None else total + term
        outs.append(total)
    return outs


def restrict_y(source, window_in, window_out, rows_out):
    total = None
    for k, weight in RESTRICT_TAPS:
        start = 2 * window_out[0] + k - window_in[0] + PAD
        term = source[:, pl.ds(start, rows_out, stride=2), :]
        term = term if weight == 1.0 else weight * term
        total = term if total is None else total + term
    places = lax.broadcasted_iota(jnp.int32, total.shape, 1)
    return jnp.where(places < window_out[1], total, 0.0)


def deposit_kernel(
    charge_ref, frac_ref, cell_ref, depth_ref,
    raw_ref, part_ref, low_ref, high_ref, message_ref,
    reals, places, grid, coarse, half2, half3, half4, last,
    *, total_y, devices,
):
    fill_tables(reals, places, charge_ref[...], frac_ref, cell_ref, total_y)
    grid[...] = jnp.zeros_like(grid)
    half_rows = 4 * YP1

    def step(group, carry):
        sums = [[None] * TILES_Y for _ in range(GROUP + 3)]
        for p in range(GROUP):
            lefts, rights = [], []
            for chunk in range(CHUNKS):
                row = (group * GROUP + p) * CHUNKS + chunk
                lefts.append(jnp.concatenate(along_xy(reals, places, row), axis=0))
                highs, lows = along_z(reals, places, row)
                rights.append(jnp.concatenate(highs + lows, axis=0))
            left = jnp.concatenate(lefts, axis=1)
            right = jnp.concatenate(rights, axis=1)
            product = lax.dot_general(left, right, (((1,), (1,)), ((), ())), preferred_element_type=jnp.float32)
            for m in range(4):
                for t in range(TILES_Y):
                    at = ((m // 2) * TILES_Y + t) * 16 + (m % 2) * 8
                    layer = product[at : at + 8, :NZ] + product[at : at + 8, NZ:]
                    layer = layer + product[half_rows + at : half_rows + at + 8, :NZ]
                    old = sums[p + m][t]
                    sums[p + m][t] = layer if old is None else old + layer
        for i in range(GROUP + 3):
            at = group * GROUP + i
            grid[at] = grid[at] + jnp.concatenate(sums[i], axis=0)
        return carry

    lax.fori_loop(0, CX // GROUP, step, 0)
    flat = triple(grid[...].reshape(X1[1] * YP1, NZ))
    below = jnp.dot(flat, depth_ref[...], preferred_element_type=jnp.float32)
    raw_ref[...] = below[:, :LANES].reshape(X1[1], YP1, LANES)
    coarse[...] = below[:, LANES:].reshape(X1[1], YP1, LANES)

    def padded(half, outs, rows):
        half[...] = jnp.zeros_like(half)
        for i, value in enumerate(outs):
            half[i, PAD : PAD + rows, :] = value

    padded(half2, restrict_x(lambda i: coarse[i], X1, X2), YP1)
    level2 = restrict_y(half2, Y1, Y2, YP2)
    padded(half3, restrict_x(lambda i: level2[i], X2, X3), YP2)
    level3 = restrict_y(half3, Y2, Y3, YP3)
    padded(half4, restrict_x(lambda i: level3[i], X3, X4), YP3)
    last[...] = restrict_y(half4, Y3, Y4, YP4).reshape(X4[1] * YP4, LANES)

    lane2 = lane_index((YP2, LANES)) < Z2
    for i in range(X2[1]):
        other = level3[i] if i < X3[1] else jnp.zeros((YP2, LANES), jnp.float32)
        part_ref[i] = jnp.where(lane2, level2[i], other)
    for r in range(6):
        at = slice(r * Y1[1], (r + 1) * Y1[1])
        low_ref[at, :] = raw_ref[r, 0 : Y1[1], :]
        high_ref[at, :] = raw_ref[CX - 3 + r, 0 : Y1[1], :]
    base2 = CX // 2 - 4 - X2[0]
    base3 = CX // 4 - 5 - X3[0]
    for ref, at2, at3 in ((low_ref, 0, 0), (high_ref, base2, base3)):
        for r in range(4):
            first = part_ref[at2 + r, 0 : Y2[1], :]
            if r < 3:
                second = pltpu.roll(part_ref[at2 + 4 + r, 0 : YP2, :], Z2, 1)[: Y2[1]]
            else:
                second = jnp.zeros((Y2[1], LANES), jnp.float32)
            at = SLAB2 + r * Y2[1]
            ref[at : at + Y2[1], :] = jnp.where(lane_index((Y2[1], LANES)) < Z2, first, second)
        for r in range(2):
            total = jnp.zeros((YP3, LANES), jnp.float32)
            lanes3 = lane_index((YP3, LANES))
            for g in range(4):
                moved = part_ref[at3 + 2 * g + r, 0:YP3, :]
                moved = pltpu.roll(moved, (g * Z3 - LANE3) % LANES, 1)
                total = jnp.where((lanes3 >= g * Z3) & (lanes3 < (g + 1) * Z3), moved, total)
            at = SLAB3 + r * Y3[1]
            ref[at : at + Y3[1], :] = total[: Y3[1]]
        ref[SLAB3 + 2 * Y3[1] :, :] = jnp.zeros((SLAB - SLAB3 - 2 * Y3[1], LANES), jnp.float32)
    lanes = lane_index((8, LANES))
    message = jnp.zeros((8, LANES), jnp.float32)
    for b in range(Y4[1]):
        rows = last[pl.ds(b, 8, stride=YP4), :]
        moved = pltpu.roll(rows, (b * Z4 - LANE4) % LANES, 1)
        message = jnp.where((lanes >= b * Z4) & (lanes < (b + 1) * Z4), moved, message)
    tail = pltpu.roll(last[8 * YP4 : 9 * YP4, :], Y4[1] * Z4 - LANE4, 1)
    message = jnp.where(lanes >= Y4[1] * Z4, tail, message)
    for d in range(devices):
        message_ref[d] = message


def merge_pair(part_ref, below_ref, above_ref, pair, row0):
    lane2 = lane_index((Y2[1], LANES)) < Z2
    lanes3 = lane_index((Y3[1], LANES))
    inside3 = (lanes3 >= LANE3) & (lanes3 < LANE4)

    def add(x, value):
        if x < PAIR_X:
            rows = slice(row0, row0 + value.shape[0])
            pair[x, rows, :] = pair[x, rows, :] + value

    for r in range(X2[1]):
        pair[3 + r, row0 : row0 + YP2, :] = part_ref[r]
    for ref, at2, at3 in ((below_ref, 0, 0), (above_ref, CX // 2 + 3, CX // 4 + 3)):
        for r in range(4):
            both = ref[SLAB2 + r * Y2[1] : SLAB2 + (r + 1) * Y2[1], :]
            add(at2 + r, jnp.where(lane2, both, 0.0))
            if r < 3:
                add(at2 + 4 + r, jnp.where(lane2, pltpu.roll(both, Z2, 1), 0.0))
        for r in range(2):
            four = ref[SLAB3 + r * Y3[1] : SLAB3 + (r + 1) * Y3[1], :]
            for g in range(4):
                moved = pltpu.roll(four, (LANE3 - g * Z3) % LANES, 1)
                add(at3 + 2 * g + r, jnp.where(inside3, moved, 0.0))


def edges_kernel(raw_ref, part_ref, below_ref, above_ref, up_ref, down_ref, up2_ref, down2_ref, pair):
    for x in range(FINE_X):
        for ref, start in ((up_ref, CY - 3), (down_ref, 0)):
            value = None
            if 3 <= x < FINE_X - 3:
                value = raw_ref[x - 3, start : start + 6, :]
            for slab, at in ((below_ref, x), (above_ref, x - CX - 3)):
                if 0 <= at < 6:
                    extra = slab[at * Y1[1] + start : at * Y1[1] + start + 6, :]
                    value = extra if value is None else value + extra
            ref[6 * x : 6 * x + 6, :] = value
    pair[...] = jnp.zeros_like(pair)
    merge_pair(part_ref, below_ref, above_ref, pair, 0)
    low2 = lane_index((8, LANES)) < Z2
    lanes = lane_index((8, LANES))
    keep = lax.broadcasted_iota(jnp.int32, (8, LANES), 0) < 7
    zero = jnp.zeros((8, LANES), jnp.float32)
    for ref, far, at2, at3, at_far in (
        (up_ref, up2_ref, CY // 2 - 3, CY // 4 - 3, CY // 2 - 3),
        (down_ref, down2_ref, 0, 0, 0),
    ):
        if EDGE2 > 6 * FINE_X:
            ref[6 * FINE_X : EDGE2, :] = jnp.zeros((EDGE2 - 6 * FINE_X, LANES), jnp.float32)
        for r in range(PACK2):
            first = pair[r, at2 : at2 + 8, :]
            second = zero
            if r + PACK2 < PAIR_X:
                second = pltpu.roll(pair[r + PACK2, at2 : at2 + 8, :], Z2, 1)
            ref[EDGE2 + 8 * r : EDGE2 + 8 * r + 8, :] = jnp.where(keep, jnp.where(low2, first, second), 0.0)
        for r in range(PACK3):
            total, total_far = zero, zero
            for g in range(4):
                x = g * PACK3 + r
                if x >= SPAN3:
                    continue
                inside = (lanes >= g * Z3) & (lanes < (g + 1) * Z3)
                turn = (g * Z3 - LANE3) % LANES
                total = jnp.where(inside, pltpu.roll(pair[x, at3 : at3 + 8, :], turn, 1), total)
                total_far = jnp.where(inside, pltpu.roll(pair[x, at_far : at_far + 8, :], turn, 1), total_far)
            ref[EDGE3 + 8 * r : EDGE3 + 8 * r + 8, :] = total
            far[4 * r : 4 * r + 4, :] = total_far[0:4]
        if FAR > 4 * PACK3:
            far[4 * PACK3 :, :] = jnp.zeros((FAR - 4 * PACK3, LANES), jnp.float32)


def merge_fine(raw_ref, below_ref, above_ref, south_ref, north_ref, fine):
    fine[...] = jnp.zeros_like(fine)
    for x in range(FINE_X):
        if 3 <= x < FINE_X - 3:
            fine[x, 3 : 3 + YP1, :] = raw_ref[x - 3]
        for slab, at in ((below_ref, x), (above_ref, x - CX - 3)):
            if 0 <= at < 6:
                rows = slice(3, 3 + Y1[1])
                fine[x, rows, :] = fine[x, rows, :] + slab[at * Y1[1] : (at + 1) * Y1[1], :]
        fine[x, 0:6, :] = fine[x, 0:6, :] + south_ref[6 * x : 6 * x + 6, :]
        fine[x, CY + 3 : CY + 9, :] = fine[x, CY + 3 : CY + 9, :] + north_ref[6 * x : 6 * x + 6, :]


def merge_coarse(part_ref, below_ref, above_ref, south_ref, north_ref, south2_ref, north2_ref, pair):
    pair[...] = jnp.zeros_like(pair)
    merge_pair(part_ref, below_ref, above_ref, pair, 3)
    low2 = lane_index((8, LANES)) < Z2
    lanes = lane_index((8, LANES))
    inside = (lanes >= LANE3) & (lanes < LANE4)
    for ref, far, at2, at3, at_far in (
        (south_ref, south2_ref, 0, 0, 0),
        (north_ref, north2_ref, CY // 2 + 3, CY // 4 + 3, CY // 2 + 3),
    ):
        for r in range(PACK2):
            both = ref[EDGE2 + 8 * r : EDGE2 + 8 * r + 8, :]
            pair[r, at2 : at2 + 8, :] = pair[r, at2 : at2 + 8, :] + jnp.where(low2, both, 0.0)
            x = r + PACK2
            if x < PAIR_X:
                moved = jnp.where(low2, pltpu.roll(both, Z2, 1), 0.0)
                pair[x, at2 : at2 + 8, :] = pair[x, at2 : at2 + 8, :] + moved
        for r in range(PACK3):
            four = ref[EDGE3 + 8 * r : EDGE3 + 8 * r + 8, :]
            four_far = far[4 * r : 4 * r + 4, :]
            for g in range(4):
                x = g * PACK3 + r
                if x >= SPAN3:
                    continue
                turn = (LANE3 - g * Z3) % LANES
                moved = jnp.where(inside, pltpu.roll(four, turn, 1), 0.0)
                pair[x, at3 : at3 + 8, :] = pair[x, at3 : at3 + 8, :] + moved
                moved = jnp.where(inside[0:4], pltpu.roll(four_far, turn, 1), 0.0)
                pair[x, at_far : at_far + 4, :] = pair[x, at_far : at_far + 4, :] + moved


def stencil_rows(source, count, rows_out, table, target, planes):
    for i in range(count + 6):
        sums = [source[i, 3 : 3 + rows_out, :]]
        for b in range(1, 4):
            sums.append(source[i, 3 - b : 3 - b + rows_out, :] + source[i, 3 + b : 3 + b + rows_out, :])
        for a in range(4):
            value = table[4 * a : 4 * a + 1] * sums[0]
            for b in range(1, 4):
                value = value + table[4 * a + b : 4 * a + b + 1] * sums[b]
            planes[a, i] = value
    for i in range(count):
        value = planes[0, i + 3]
        for a in range(1, 4):
            value = value + (planes[a, i + 3 - a] + planes[a, i + 3 + a])
        target[i] = value


def prolong_x(load, window_in, window_out):
    outs = []
    first = window_in[0]
    for n in range(window_out[0], window_out[0] + window_out[1]):
        if n % 2 == 0:
            outs.append(load(n // 2 - first))
        else:
            m = (n - 1) // 2 - first
            outs.append(0.5625 * (load(m) + load(m + 1)) - 0.0625 * (load(m - 1) + load(m + 2)))
    return outs


def prolong_y(source, window_in, window_out, target):
    first, count = window_out
    even = first % 2
    evens = (count - even + 1) // 2
    start = (first + even) // 2 - window_in[0]
    target[:, pl.ds(even, evens, stride=2), :] = source[:, start : start + evens, :]
    odds = count - evens
    m = (first + 1 - even - 1) // 2 - window_in[0]

    def taken(shift):
        return source[:, m + shift : m + shift + odds, :]

    target[:, pl.ds(1 - even, odds, stride=2), :] = 0.5625 * (taken(0) + taken(1)) - 0.0625 * (taken(-1) + taken(2))


def rise(load, window_in, window_out, wide_in, wide_out, half, target):
    target[...] = jnp.zeros_like(target)
    for r, value in enumerate(prolong_x(load, window_in, window_out)):
        half[r] = value
    prolong_y(half, wide_in, wide_out, target)


def coarse_kernel(
    message_ref, gather_ref, basis_ref, spectrum_ref, window_ref, level3_ref, ninth, level4, half3, *, size_x, size_y
):
    devices = size_x * size_y
    width = CY // 8 * size_y * Z4
    blocks = width // LANES
    used = Y4[1] * Z4
    tails = lane_index((devices, LANES))
    gathered = jnp.zeros((devices, LANES), jnp.float32)
    for b in range(Y4[1]):
        rows = message_ref[pl.ds(b, devices, stride=8), :]
        moved = pltpu.roll(rows, (b * Z4 - used) % LANES, 1)
        gathered = jnp.where((tails >= b * Z4) & (tails < (b + 1) * Z4), moved, gathered)
    ninth[...] = gathered

    def assemble(load, rows):
        total = [jnp.zeros((rows, LANES), jnp.float32) for _ in range(blocks)]
        lanes = lane_index((rows, LANES))
        for j in range(size_y):
            position = (j * (CY // 8) + Y4[0]) * Z4 % width
            block, offset = (position // LANES, position % LANES)
            value = jnp.where(lanes < used, load(j), 0.0)
            if offset == 0:
                total[block] = total[block] + value
                continue
            value = pltpu.roll(value, offset, 1)
            following = (block + 1) % blocks
            total[block] = total[block] + jnp.where(lanes >= offset, value, 0.0)
            total[following] = total[following] + jnp.where(lanes < offset, value, 0.0)
        return jnp.concatenate(total, axis=1)

    strips = []
    for i in range(size_x):
        strips.append(assemble(lambda j: message_ref[(i * size_y + j) * 8 : (i * size_y + j + 1) * 8, :], 8))
    tail = assemble(lambda j: ninth[pl.ds(j, size_x, stride=size_y), :], size_x)
    if size_x % 8:
        tail = jnp.concatenate([tail, jnp.zeros((8 - size_x % 8, width), jnp.float32)], axis=0)
    strips.append(tail)
    strips = jnp.concatenate(strips, axis=0)
    exact = dict(precision=HIGHEST, preferred_element_type=jnp.float32)
    modes = jnp.dot(gather_ref[...], strips, **exact)
    modes = lax.dot_general(modes, basis_ref[...], (((1,), (1,)), ((), ())), **exact)
    modes = jnp.dot(modes * spectrum_ref[...], basis_ref[...], **exact)
    shift = (width - (lax.axis_index("gy") * (CY // 8) + Y4[0]) * Z4) % width
    modes = pltpu.roll(modes, shift, 1)[:, :LANES]
    own = jnp.dot(window_ref[lax.axis_index("gx")], modes, **exact)
    lanes = lane_index(own.shape)
    inside4 = (lanes >= LANE4) & (lanes < LANE4 + Z4)
    level4[...] = jnp.zeros_like(level4)
    for b in range(Y4[1]):
        moved = jnp.where(inside4, pltpu.roll(own, (LANE4 - b * Z4) % LANES, 1), 0.0)
        level4[pl.ds(b, X4[1], stride=YP4), :] = moved[: X4[1]]

    rise(lambda i: level4[i * YP4 : (i + 1) * YP4, :], X4, X3, Y4, Y3, half3, level3_ref)


def field_kernel(
    raw_ref, part_ref, below_ref, above_ref, south_ref, north_ref, south2_ref, north2_ref,
    coarse_ref, spectrum_ref, depth_ref, frac_ref, cell_ref,
    potential_ref, atom_ref,
    reals, places, fine, pair, planes, planes_pair, smooth, smooth_pair,
    level3, half2, level2, half1, level1, field, partial,
    *, total_y,
):
    fill_tables(reals, places, None, frac_ref, cell_ref, total_y)
    merge_fine(raw_ref, below_ref, above_ref, south_ref, north_ref, fine)
    merge_coarse(part_ref, below_ref, above_ref, south_ref, north_ref, south2_ref, north2_ref, pair)
    stencil_rows(pair, X2[1], YP2, spectrum_ref[1], smooth_pair, planes_pair)
    lanes3 = lane_index((YP3, LANES))
    inside3 = (lanes3 >= LANE3) & (lanes3 < LANE4)
    for r in range(X3[1]):
        level3[r] = coarse_ref[r] + jnp.where(inside3, smooth_pair[r, 0:YP3, :], 0.0)
    rise(lambda i: level3[i], X3, X2, Y3, Y2, half2, level2)
    inside2 = lane_index((YP2, LANES)) < Z2
    for r in range(X2[1]):
        level2[r] = level2[r] + jnp.where(inside2, smooth_pair[r], 0.0)
    rise(lambda i: level2[i], X2, X1, Y2, Y1, half1, level1)
    stencil_rows(fine, X1[1], YP1, spectrum_ref[0], smooth, planes)

    rows = X1[1] * YP1
    modes = jnp.concatenate([smooth[...].reshape(rows, LANES), level1[...].reshape(rows, LANES)], axis=1)
    total = jnp.dot(triple(modes), depth_ref[...], preferred_element_type=jnp.float32)
    field[...] = total.reshape(X1[1], YP1, NZ)
    potential_ref[...] = field[0:CX, 0:CY, :]

    def step(group, carry):
        for p in range(GROUP):
            plane = group * GROUP + p
            high, low = halves(jnp.concatenate([field[plane + m] for m in range(4)], axis=0))
            left = jnp.concatenate([high, high, low], axis=1)
            rights = []
            for chunk in range(CHUNKS):
                highs, lows = along_z(reals, places, plane * CHUNKS + chunk)
                rights.append(jnp.concatenate(highs + lows + highs, axis=0))
            product = jnp.dot(left, jnp.concatenate(rights, axis=1), preferred_element_type=jnp.float32)
            for chunk in range(CHUNKS):
                row = plane * CHUNKS + chunk
                lanes = slice(chunk * LANES, (chunk + 1) * LANES)
                weights = [spread_row(reals, REAL_X + m, row) for m in range(4)]
                table, tile = pattern_y(reals, places, row)
                value = None
                for t in range(TILES_Y):
                    layer = None
                    for m in range(4):
                        at = m * YP1 + 8 * t
                        term = product[at : at + 8, lanes] * weights[m]
                        layer = term if layer is None else layer + term
                    value = layer if value is None else jnp.where(tile == t, layer, value)
                partial[pl.ds(row * 8, 8), :] = value * table
        return carry

    lax.fori_loop(0, CX // GROUP, step, 0)
    for g in range(ROWS // 8):
        total = partial[pl.ds(g * 64, 8, stride=8), :]
        for r in range(1, 8):
            total = total + partial[pl.ds(g * 64 + r, 8, stride=8), :]
        atom_ref[g * 8 : g * 8 + 8, :] = total


VM = pl.BlockSpec(memory_space=pltpu.VMEM)


def f32(*shape):
    return jax.ShapeDtypeStruct(shape, jnp.float32)


def scratch(*shape):
    return pltpu.VMEM(shape, jnp.float32)


def shifted(value, axis, steps):
    count = lax.axis_size(axis)
    return lax.ppermute(value, axis, [(source, (source + steps) % count) for source in range(count)])


def integers(*shape):
    return pltpu.VMEM(shape, jnp.int32)


def call(kernel, name, outs, scratches, *operands):
    return pl.pallas_call(
        kernel,
        in_specs=[VM] * len(operands),
        out_specs=[VM] * len(outs),
        out_shape=outs,
        scratch_shapes=scratches,
        name=name,
    )(*operands)


def local(charges, fractions, cells):
    size_x = lax.axis_size("gx")
    size_y = lax.axis_size("gy")
    devices = size_x * size_y
    total_y = CY * size_y
    down_table, up_table = depth_tables()
    gather, basis, coarse_spectrum, window = (jnp.asarray(t) for t in coarse_tables(size_x, size_y))
    charge = charges.reshape(ROWS, LANES)
    frac = fractions.reshape(3, ROWS, LANES)
    cell = cells.reshape(2, ROWS, LANES).transpose(1, 0, 2).reshape(2 * ROWS, LANES)
    raw, part, low, high, message = call(
        functools.partial(deposit_kernel, total_y=total_y, devices=devices),
        "deposit",
        [
            f32(X1[1], YP1, LANES),
            f32(X2[1], YP2, LANES),
            f32(SLAB, LANES),
            f32(SLAB, LANES),
            f32(devices, 8, LANES),
        ],
        [
            scratch(REALS * ROWS, LANES),
            integers(PLACES * ROWS, LANES),
            scratch(X1[1], YP1, NZ),
            scratch(X1[1], YP1, LANES),
            scratch(X2[1], YP1 + 16, LANES),
            scratch(X3[1], YP2 + 24, LANES),
            scratch(X4[1], YP3 + 16, LANES),
            scratch(X4[1] * YP4, LANES),
        ],
        charge, frac, cell, down_table,
    )
    everyone = lax.all_to_all(message, ("gx", "gy"), 0, 0)
    below = shifted(high, "gx", 1)
    above = shifted(low, "gx", -1)
    up, down, up2, down2 = call(
        edges_kernel,
        "edges",
        [f32(EDGE, LANES), f32(EDGE, LANES), f32(FAR, LANES), f32(FAR, LANES)],
        [scratch(PAIR_X, YP2, LANES)],
        raw, part, below, above,
    )
    south = shifted(up, "gy", 1)
    north = shifted(down, "gy", -1)
    south2 = shifted(up2, "gy", 2)
    north2 = shifted(down2, "gy", -2)
    (coarse,) = call(
        functools.partial(coarse_kernel, size_x=size_x, size_y=size_y),
        "coarse",
        [f32(X3[1], YP3, LANES)],
        [scratch(devices, LANES), scratch(X4[1] * YP4, LANES), scratch(X3[1], YP4, LANES)],
        everyone.reshape(devices * 8, LANES), gather, basis, coarse_spectrum, window,
    )
    potential, atoms = call(
        functools.partial(field_kernel, total_y=total_y),
        "field",
        [f32(CX, CY, NZ), f32(ROWS, LANES)],
        [
            scratch(REALS * ROWS, LANES),
            integers(PLACES * ROWS, LANES),
            scratch(FINE_X, 32, LANES),
            scratch(PAIR_X, 24, LANES),
            scratch(4, FINE_X, YP1, LANES),
            scratch(4, PAIR_X, YP2, LANES),
            scratch(X1[1], YP1, LANES),
            scratch(X2[1], YP2, LANES),
            scratch(X3[1], YP3, LANES),
            scratch(X2[1], YP3, LANES),
            scratch(X2[1], YP2, LANES),
            scratch(X1[1], YP2, LANES),
            scratch(X1[1], YP1, LANES),
            scratch(X1[1], YP1, NZ),
            scratch(8 * ROWS, LANES),
        ],
        raw, part, below, above, south, north, south2, north2,
        coarse, jnp.asarray(spectra().astype(np.float32)), up_table, frac, cell,
    )
    return (potential, atoms.reshape(1, 1, ATOMS_DEV))


def solution(mesh):
    placed = (P("gx", "gy", None), P("gx", "gy", None, None), P("gx", "gy", None, None))
    return jax.shard_map(
        local,
        mesh=mesh,
        in_specs=placed,
        out_specs=(P("gx", "gy", None), P("gx", "gy", None)),
        check_vma=False,
    )
```

```python
import functools

import jax
import jax.numpy as jnp
import numpy as np
from jax import lax
from jax.experimental import pallas as pl
from jax.experimental.pallas import tpu as pltpu
from jax.sharding import PartitionSpec as P

CX = 32
CY = 16
NZ = 128
ATOMS_DEV = 16384

HIGHEST = lax.Precision.HIGHEST
RESTRICT_TAPS = ((-3, -0.0625), (-1, 0.5625), (0, 1.0), (1, 0.5625), (3, -0.0625))
PER_PLANE = ATOMS_DEV // CX
LANES = 128
CHUNKS = PER_PLANE // LANES
Z2, Z3, Z4 = (NZ // 2, NZ // 4, NZ // 8)
LANE3 = Z2
LANE4 = Z2 + Z3

X1, Y1 = (0, CX + 3), (0, CY + 3)


def coarser(window):
    first, count = window
    last = first + count - 1
    starts = [m for m in range(first - 4, last + 4) if any(first <= 2 * m + k <= last for k, _ in RESTRICT_TAPS)]
    return (starts[0], starts[-1] - starts[0] + 1)


X2, Y2 = coarser(X1), coarser(Y1)
X3, Y3 = coarser(X2), coarser(Y2)
X4, Y4 = coarser(X3), coarser(Y3)


def up8(count):
    return -(-count // 8) * 8


SLAB2 = 6 * Y1[1]
SLAB3 = SLAB2 + 4 * Y2[1]
SLAB = up8(SLAB3 + 2 * Y3[1])
FINE_X = X1[1] + 6
PAIR_X = CX // 2 + 10
SPAN3 = CX // 4 + 11
PACK2 = (PAIR_X + 1) // 2
PACK3 = (SPAN3 + 3) // 4
EDGE2 = up8(6 * FINE_X)
EDGE3 = EDGE2 + 8 * PACK2
EDGE = EDGE3 + 8 * PACK3
FAR = up8(4 * PACK3)
YP1, YP2, YP3, YP4 = (up8(Y1[1]), up8(Y2[1]), up8(Y3[1]), up8(Y4[1]))
PAD = 8


def real_basis(count):
    places = np.arange(count)
    rows = [np.full(count, 1.0 / np.sqrt(count))]
    for k in range(1, count // 2):
        rows.append(np.sqrt(2.0 / count) * np.cos(2 * np.pi * k * places / count))
        rows.append(np.sqrt(2.0 / count) * np.sin(2 * np.pi * k * places / count))
    rows.append(np.where(places % 2 == 0, 1.0, -1.0) / np.sqrt(count))
    return np.stack(rows)


def basis_frequency(count):
    return np.array([0] + [k for k in range(1, count // 2) for _ in range(2)] + [count // 2])


def restrict_matrix(count):
    matrix = np.zeros((count // 2, count))
    for m in range(count // 2):
        for k, weight in RESTRICT_TAPS:
            matrix[m, (2 * m + k) % count] += weight
    return matrix


def depth_matrix():
    first = restrict_matrix(NZ)
    second = restrict_matrix(Z2) @ first
    third = restrict_matrix(Z3) @ second
    parts = [real_basis(NZ), real_basis(Z2) @ first, real_basis(Z3) @ second, real_basis(Z4) @ third]
    parts.append(np.zeros((2 * LANES - sum(p.shape[0] for p in parts), NZ)))
    return np.concatenate(parts, axis=0)


def split_numpy(value):
    high = value.astype(np.float32).astype(jnp.bfloat16)
    low = (value - high.astype(np.float64)).astype(np.float32).astype(jnp.bfloat16)
    return high, low


def depth_tables():
    high, low = split_numpy(depth_matrix())
    down = np.concatenate([high.T, high.T, low.T], axis=0)
    up = np.concatenate([high, high, low], axis=0)
    return jnp.asarray(down), jnp.asarray(up)


def smooth_numpy(rho):
    return np.where(rho < 1.0, 1.875 - 1.25 * rho * rho + 0.375 * rho**4, 1.0 / np.maximum(rho, 1.0))


def stencil_spectrum(level, count):
    offsets = np.arange(-3, 4) * 1.0
    near = np.arange(0, 4) * 1.0
    radius = np.sqrt(near[:, None, None] ** 2 + near[None, :, None] ** 2 + offsets[None, None, :] ** 2)
    stencil = (smooth_numpy(radius / 1.5) / 1.5 - smooth_numpy(radius / 3.0) / 3.0) / 2.0 ** (level - 1)
    waves = np.cos(2 * np.pi * offsets[:, None] * basis_frequency(count)[None, :] / count)
    return np.einsum("abd,dk->abk", stencil, waves)


def spectra():
    fine = stencil_spectrum(1, NZ).reshape(16, NZ)
    coarse = np.zeros((16, LANES))
    coarse[:, :Z2] = stencil_spectrum(2, Z2).reshape(16, Z2)
    coarse[:, LANE3:LANE4] = stencil_spectrum(3, Z3).reshape(16, Z3)
    return np.stack([fine, coarse])


def signed(count):
    places = np.arange(count)
    return np.where(places > count // 2, places - count, places) * 1.0


def coarse_tables(size_x, size_y):
    total_x = CX // 8 * size_x
    total_y = CY // 8 * size_y
    first = signed(total_x)[:, None, None]
    second = signed(total_y)[None, :, None]
    third = signed(Z4)[None, None, :]
    kernel = smooth_numpy(np.sqrt(first**2 + second**2 + third**2) / 1.5) / 12.0

    def cosines(count):
        return np.cos(2 * np.pi * basis_frequency(count)[:, None] * np.arange(count)[None, :] / count)

    spectrum = np.einsum("xyz,ax,by,cz->abc", kernel, cosines(total_x), cosines(total_y), cosines(Z4), optimize=True)
    spectrum = spectrum.reshape(total_x, total_y * Z4)
    basis_x = real_basis(total_x)
    basis_y = np.kron(real_basis(total_y), np.eye(Z4))
    span = X4[1]
    tail = up8(size_x)
    gather = np.zeros((total_x, 8 * size_x + tail))
    window = np.zeros((size_x, up8(span), total_x))
    for i in range(size_x):
        for a in range(span):
            place = (i * (CX // 8) + X4[0] + a) % total_x
            gather[:, i * 8 + a if a < 8 else 8 * size_x + i] = basis_x[:, place]
            window[i, a, :] = basis_x[:, place]
    return [t.astype(np.float32) for t in (gather, basis_y, spectrum, window)]


def spline_weights(frac):
    def near_weight(distance):
        return (1.0 - distance) * (1.0 + distance - 1.5 * distance * distance)

    def far_weight(distance):
        return -0.5 * (distance - 1.0) * (2.0 - distance) * (2.0 - distance)

    return [far_weight(1.0 + frac), near_weight(frac), near_weight(1.0 - frac), far_weight(2.0 - frac)]


ROWS = ATOMS_DEV // LANES
GROUP = 16
TILES_Y = YP1 // 8
TILES_Z = NZ // 16
REAL_X, REAL_Y, REAL_Z, REAL_TY, REAL_TZ = 0, 4, 8, 12, 14
REALS, PLACES = 16, 8


def fill_tables(reals, places, charge, frac_ref, cell_ref, total_y):
    first_y = lax.axis_index("gy") * CY + 1

    def put(ref, index, value):
        ref[index * ROWS : (index + 1) * ROWS, :] = value

    for dim, base in ((0, REAL_X), (1, REAL_Y), (2, REAL_Z)):
        weights = spline_weights(frac_ref[dim])
        for tap in range(4):
            put(reals, base + tap, weights[tap] if charge is None or dim else weights[tap] * charge)
    block_y = cell_ref[pl.ds(0, ROWS, stride=2), :] - first_y
    block_y = jnp.where(block_y < 0, block_y + total_y, block_y)
    block_z = (cell_ref[pl.ds(1, ROWS, stride=2), :] - 1) & (NZ - 1)
    for tap in range(4):
        put(places, tap, (block_y + tap) & 7)
        put(places, 4 + tap, (block_z + tap) & 15)
    tile_y = block_y >> 3
    tile_z = block_z >> 4
    put(reals, REAL_TY, tile_y.astype(jnp.float32))
    put(reals, REAL_TY + 1, (tile_y + 1).astype(jnp.float32))
    put(reals, REAL_TZ, tile_z.astype(jnp.float32))
    put(reals, REAL_TZ + 1, ((tile_z + 1) & (TILES_Z - 1)).astype(jnp.float32))


def spread_row(ref, index, row):
    return ref[pl.ds(index * ROWS + row, 8, stride=0), :]


def pattern_y(reals, places, row):
    index = lax.broadcasted_iota(jnp.int32, (8, LANES), 0)
    table = jnp.zeros((8, LANES), jnp.float32)
    for tap in range(4):
        place = spread_row(places, tap, row)
        table = jnp.where(index == place, spread_row(reals, REAL_Y + tap, row), table)
    start = spread_row(places, 0, row)
    tile = jnp.where(index >= start, spread_row(reals, REAL_TY, row), spread_row(reals, REAL_TY + 1, row))
    return table, tile


def along_z(reals, places, row):
    index = lax.broadcasted_iota(jnp.int32, (8, LANES), 0)
    parts, tiles = [], []
    for half in range(2):
        table = jnp.zeros((8, LANES), jnp.float32)
        for tap in range(4):
            place = spread_row(places, 4 + tap, row)
            table = jnp.where(index + 8 * half == place, spread_row(reals, REAL_Z + tap, row), table)
        start = spread_row(places, 4, row)
        tiles.append(
            jnp.where(index + 8 * half >= start, spread_row(reals, REAL_TZ, row), spread_row(reals, REAL_TZ + 1, row))
        )
        parts.append(table)
    high, low = halves(jnp.concatenate(parts, axis=0))
    tile = jnp.concatenate(tiles, axis=0).astype(jnp.bfloat16)
    zero = jnp.zeros((16, LANES), jnp.bfloat16)
    highs, lows = [], []
    for t in range(TILES_Z):
        same = tile == jnp.bfloat16(t)
        highs.append(jnp.where(same, high, zero))
        lows.append(jnp.where(same, low, zero))
    return highs, lows


def along_xy(reals, places, row):
    table, tile = pattern_y(reals, places, row)
    tile = jnp.concatenate([tile, tile], axis=0).astype(jnp.bfloat16)
    zero = jnp.zeros((16, LANES), jnp.bfloat16)
    same = [tile == jnp.bfloat16(t) for t in range(TILES_Y)]
    highs, lows = [], []
    for pair in range(2):
        both = [table * spread_row(reals, REAL_X + 2 * pair + m, row) for m in range(2)]
        high, low = halves(jnp.concatenate(both, axis=0))
        highs += [jnp.where(mask, high, zero) for mask in same]
        lows += [jnp.where(mask, low, zero) for mask in same]
    return highs + lows


def triple(value):
    high, low = halves(value)
    return jnp.concatenate([high, low, high], axis=1)


def halves(value):
    high = value.astype(jnp.bfloat16)
    low = (value - high.astype(jnp.float32)).astype(jnp.bfloat16)
    return high, low


def lane_index(shape):
    return lax.broadcasted_iota(jnp.int32, shape, len(shape) - 1)


def restrict_x(load, window_in, window_out):
    first, count = window_in
    outs = []
    for m in range(window_out[0], window_out[0] + window_out[1]):
        total = None
        for k, weight in RESTRICT_TAPS:
            place = 2 * m + k - first
            if 0 <= place < count:
                term = load(place) if weight == 1.0 else weight * load(place)
                total = term if total is None else total + term
        outs.append(total)
    return outs


def restrict_y(source, window_in, window_out, rows_out):
    total = None
    for k, weight in RESTRICT_TAPS:
        start = 2 * window_out[0] + k - window_in[0] + PAD
        term = source[:, pl.ds(start, rows_out, stride=2), :]
        term = term if weight == 1.0 else weight * term
        total = term if total is None else total + term
    places = lax.broadcasted_iota(jnp.int32, total.shape, 1)
    return jnp.where(places < window_out[1], total, 0.0)


def deposit_kernel(
    charge_ref, frac_ref, cell_ref, depth_ref,
    raw_ref, part_ref, low_ref, high_ref, message_ref,
    reals, places, grid, coarse, half2, half3, half4, last,
    *, total_y, devices,
):
    fill_tables(reals, places, charge_ref[...], frac_ref, cell_ref, total_y)
    grid[...] = jnp.zeros_like(grid)
    half_rows = 4 * YP1

    def step(group, carry):
        sums = [[None] * TILES_Y for _ in range(GROUP + 3)]
        for p in range(GROUP):
            lefts, rights = [], []
            for chunk in range(CHUNKS):
                row = (group * GROUP + p) * CHUNKS + chunk
                lefts.append(jnp.concatenate(along_xy(reals, places, row), axis=0))
                highs, lows = along_z(reals, places, row)
                rights.append(jnp.concatenate(highs + lows, axis=0))
            left = jnp.concatenate(lefts, axis=1)
            right = jnp.concatenate(rights, axis=1)
            product = lax.dot_general(left, right, (((1,), (1,)), ((), ())), preferred_element_type=jnp.float32)
            for m in range(4):
                for t in range(TILES_Y):
                    at = ((m // 2) * TILES_Y + t) * 16 + (m % 2) * 8
                    layer = product[at : at + 8, :NZ] + product[at : at + 8, NZ:]
                    layer = layer + product[half_rows + at : half_rows + at + 8, :NZ]
                    old = sums[p + m][t]
                    sums[p + m][t] = layer if old is None else old + layer
        for i in range(GROUP + 3):
            at = group * GROUP + i
            grid[at] = grid[at] + jnp.concatenate(sums[i], axis=0)
        return carry

    lax.fori_loop(0, CX // GROUP, step, 0)
    flat = triple(grid[...].reshape(X1[1] * YP1, NZ))
    below = jnp.dot(flat, depth_ref[...], preferred_element_type=jnp.float32)
    raw_ref[...] = below[:, :LANES].reshape(X1[1], YP1, LANES)
    coarse[...] = below[:, LANES:].reshape(X1[1], YP1, LANES)

    def padded(half, outs, rows):
        half[...] = jnp.zeros_like(half)
        for i, value in enumerate(outs):
            half[i, PAD : PAD + rows, :] = value

    padded(half2, restrict_x(lambda i: coarse[i], X1, X2), YP1)
    level2 = restrict_y(half2, Y1, Y2, YP2)
    padded(half3, restrict_x(lambda i: level2[i], X2, X3), YP2)
    level3 = restrict_y(half3, Y2, Y3, YP3)
    padded(half4, restrict_x(lambda i: level3[i], X3, X4), YP3)
    last[...] = restrict_y(half4, Y3, Y4, YP4).reshape(X4[1] * YP4, LANES)

    lane2 = lane_index((YP2, LANES)) < Z2
    for i in range(X2[1]):
        other = level3[i] if i < X3[1] else jnp.zeros((YP2, LANES), jnp.float32)
        part_ref[i] = jnp.where(lane2, level2[i], other)
    for r in range(6):
        at = slice(r * Y1[1], (r + 1) * Y1[1])
        low_ref[at, :] = raw_ref[r, 0 : Y1[1], :]
        high_ref[at, :] = raw_ref[CX - 3 + r, 0 : Y1[1], :]
    base2 = CX // 2 - 4 - X2[0]
    base3 = CX // 4 - 5 - X3[0]
    for ref, at2, at3 in ((low_ref, 0, 0), (high_ref, base2, base3)):
        for r in range(4):
            first = part_ref[at2 + r, 0 : Y2[1], :]
            if r < 3:
                second = pltpu.roll(part_ref[at2 + 4 + r, 0 : YP2, :], Z2, 1)[: Y2[1]]
            else:
                second = jnp.zeros((Y2[1], LANES), jnp.float32)
            at = SLAB2 + r * Y2[1]
            ref[at : at + Y2[1], :] = jnp.where(lane_index((Y2[1], LANES)) < Z2, first, second)
        for r in range(2):
            total = jnp.zeros((YP3, LANES), jnp.float32)
            lanes3 = lane_index((YP3, LANES))
            for g in range(4):
                moved = part_ref[at3 + 2 * g + r, 0:YP3, :]
                moved = pltpu.roll(moved, (g * Z3 - LANE3) % LANES, 1)
                total = jnp.where((lanes3 >= g * Z3) & (lanes3 < (g + 1) * Z3), moved, total)
            at = SLAB3 + r * Y3[1]
            ref[at : at + Y3[1], :] = total[: Y3[1]]
        ref[SLAB3 + 2 * Y3[1] :, :] = jnp.zeros((SLAB - SLAB3 - 2 * Y3[1], LANES), jnp.float32)
    lanes = lane_index((8, LANES))
    message = jnp.zeros((8, LANES), jnp.float32)
    for b in range(Y4[1]):
        rows = last[pl.ds(b, 8, stride=YP4), :]
        moved = pltpu.roll(rows, (b * Z4 - LANE4) % LANES, 1)
        message = jnp.where((lanes >= b * Z4) & (lanes < (b + 1) * Z4), moved, message)
    tail = pltpu.roll(last[8 * YP4 : 9 * YP4, :], Y4[1] * Z4 - LANE4, 1)
    message = jnp.where(lanes >= Y4[1] * Z4, tail, message)
    for d in range(devices):
        message_ref[d] = message


def merge_pair(part_ref, below_ref, above_ref, pair, row0):
    lane2 = lane_index((Y2[1], LANES)) < Z2
    lanes3 = lane_index((Y3[1], LANES))
    inside3 = (lanes3 >= LANE3) & (lanes3 < LANE4)

    def add(x, value):
        if x < PAIR_X:
            rows = slice(row0, row0 + value.shape[0])
            pair[x, rows, :] = pair[x, rows, :] + value

    for r in range(X2[1]):
        pair[3 + r, row0 : row0 + YP2, :] = part_ref[r]
    for ref, at2, at3 in ((below_ref, 0, 0), (above_ref, CX // 2 + 3, CX // 4 + 3)):
        for r in range(4):
            both = ref[SLAB2 + r * Y2[1] : SLAB2 + (r + 1) * Y2[1], :]
            add(at2 + r, jnp.where(lane2, both, 0.0))
            if r < 3:
                add(at2 + 4 + r, jnp.where(lane2, pltpu.roll(both, Z2, 1), 0.0))
        for r in range(2):
            four = ref[SLAB3 + r * Y3[1] : SLAB3 + (r + 1) * Y3[1], :]
            for g in range(4):
                moved = pltpu.roll(four, (LANE3 - g * Z3) % LANES, 1)
                add(at3 + 2 * g + r, jnp.where(inside3, moved, 0.0))


def edges_kernel(raw_ref, part_ref, below_ref, above_ref, up_ref, down_ref, up2_ref, down2_ref, pair):
    for x in range(FINE_X):
        for ref, start in ((up_ref, CY - 3), (down_ref, 0)):
            value = None
            if 3 <= x < FINE_X - 3:
                value = raw_ref[x - 3, start : start + 6, :]
            for slab, at in ((below_ref, x), (above_ref, x - CX - 3)):
                if 0 <= at < 6:
                    extra = slab[at * Y1[1] + start : at * Y1[1] + start + 6, :]
                    value = extra if value is None else value + extra
            ref[6 * x : 6 * x + 6, :] = value
    pair[...] = jnp.zeros_like(pair)
    merge_pair(part_ref, below_ref, above_ref, pair, 0)
    low2 = lane_index((8, LANES)) < Z2
    lanes = lane_index((8, LANES))
    keep = lax.broadcasted_iota(jnp.int32, (8, LANES), 0) < 7
    zero = jnp.zeros((8, LANES), jnp.float32)
    for ref, far, at2, at3, at_far in (
        (up_ref, up2_ref, CY // 2 - 3, CY // 4 - 3, CY // 2 - 3),
        (down_ref, down2_ref, 0, 0, 0),
    ):
        if EDGE2 > 6 * FINE_X:
            ref[6 * FINE_X : EDGE2, :] = jnp.zeros((EDGE2 - 6 * FINE_X, LANES), jnp.float32)
        for r in range(PACK2):
            first = pair[r, at2 : at2 + 8, :]
            second = zero
            if r + PACK2 < PAIR_X:
                second = pltpu.roll(pair[r + PACK2, at2 : at2 + 8, :], Z2, 1)
            ref[EDGE2 + 8 * r : EDGE2 + 8 * r + 8, :] = jnp.where(keep, jnp.where(low2, first, second), 0.0)
        for r in range(PACK3):
            total, total_far = zero, zero
            for g in range(4):
                x = g * PACK3 + r
                if x >= SPAN3:
                    continue
                inside = (lanes >= g * Z3) & (lanes < (g + 1) * Z3)
                turn = (g * Z3 - LANE3) % LANES
                total = jnp.where(inside, pltpu.roll(pair[x, at3 : at3 + 8, :], turn, 1), total)
                total_far = jnp.where(inside, pltpu.roll(pair[x, at_far : at_far + 8, :], turn, 1), total_far)
            ref[EDGE3 + 8 * r : EDGE3 + 8 * r + 8, :] = total
            far[4 * r : 4 * r + 4, :] = total_far[0:4]
        if FAR > 4 * PACK3:
            far[4 * PACK3 :, :] = jnp.zeros((FAR - 4 * PACK3, LANES), jnp.float32)


def merge_fine(raw_ref, below_ref, above_ref, south_ref, north_ref, fine):
    fine[...] = jnp.zeros_like(fine)
    for x in range(FINE_X):
        if 3 <= x < FINE_X - 3:
            fine[x, 3 : 3 + YP1, :] = raw_ref[x - 3]
        for slab, at in ((below_ref, x), (above_ref, x - CX - 3)):
            if 0 <= at < 6:
                rows = slice(3, 3 + Y1[1])
                fine[x, rows, :] = fine[x, rows, :] + slab[at * Y1[1] : (at + 1) * Y1[1], :]
        fine[x, 0:6, :] = fine[x, 0:6, :] + south_ref[6 * x : 6 * x + 6, :]
        fine[x, CY + 3 : CY + 9, :] = fine[x, CY + 3 : CY + 9, :] + north_ref[6 * x : 6 * x + 6, :]


def merge_coarse(part_ref, below_ref, above_ref, south_ref, north_ref, south2_ref, north2_ref, pair):
    pair[...] = jnp.zeros_like(pair)
    merge_pair(part_ref, below_ref, above_ref, pair, 3)
    low2 = lane_index((8, LANES)) < Z2
    lanes = lane_index((8, LANES))
    inside = (lanes >= LANE3) & (lanes < LANE4)
    for ref, far, at2, at3, at_far in (
        (south_ref, south2_ref, 0, 0, 0),
        (north_ref, north2_ref, CY // 2 + 3, CY // 4 + 3, CY // 2 + 3),
    ):
        for r in range(PACK2):
            both = ref[EDGE2 + 8 * r : EDGE2 + 8 * r + 8, :]
            pair[r, at2 : at2 + 8, :] = pair[r, at2 : at2 + 8, :] + jnp.where(low2, both, 0.0)
            x = r + PACK2
            if x < PAIR_X:
                moved = jnp.where(low2, pltpu.roll(both, Z2, 1), 0.0)
                pair[x, at2 : at2 + 8, :] = pair[x, at2 : at2 + 8, :] + moved
        for r in range(PACK3):
            four = ref[EDGE3 + 8 * r : EDGE3 + 8 * r + 8, :]
            four_far = far[4 * r : 4 * r + 4, :]
            for g in range(4):
                x = g * PACK3 + r
                if x >= SPAN3:
                    continue
                turn = (LANE3 - g * Z3) % LANES
                moved = jnp.where(inside, pltpu.roll(four, turn, 1), 0.0)
                pair[x, at3 : at3 + 8, :] = pair[x, at3 : at3 + 8, :] + moved
                moved = jnp.where(inside[0:4], pltpu.roll(four_far, turn, 1), 0.0)
                pair[x, at_far : at_far + 4, :] = pair[x, at_far : at_far + 4, :] + moved


def stencil_rows(source, count, rows_out, table, target, planes):
    for i in range(count + 6):
        sums = [source[i, 3 : 3 + rows_out, :]]
        for b in range(1, 4):
            sums.append(source[i, 3 - b : 3 - b + rows_out, :] + source[i, 3 + b : 3 + b + rows_out, :])
        for a in range(4):
            value = table[4 * a : 4 * a + 1] * sums[0]
            for b in range(1, 4):
                value = value + table[4 * a + b : 4 * a + b + 1] * sums[b]
            planes[a, i] = value
    for i in range(count):
        value = planes[0, i + 3]
        for a in range(1, 4):
            value = value + (planes[a, i + 3 - a] + planes[a, i + 3 + a])
        target[i] = value


def prolong_x(load, window_in, window_out):
    outs = []
    first = window_in[0]
    for n in range(window_out[0], window_out[0] + window_out[1]):
        if n % 2 == 0:
            outs.append(load(n // 2 - first))
        else:
            m = (n - 1) // 2 - first
            outs.append(0.5625 * (load(m) + load(m + 1)) - 0.0625 * (load(m - 1) + load(m + 2)))
    return outs


def prolong_y(source, window_in, window_out, target):
    first, count = window_out
    even = first % 2
    evens = (count - even + 1) // 2
    start = (first + even) // 2 - window_in[0]
    target[:, pl.ds(even, evens, stride=2), :] = source[:, start : start + evens, :]
    odds = count - evens
    m = (first + 1 - even - 1) // 2 - window_in[0]

    def taken(shift):
        return source[:, m + shift : m + shift + odds, :]

    target[:, pl.ds(1 - even, odds, stride=2), :] = 0.5625 * (taken(0) + taken(1)) - 0.0625 * (taken(-1) + taken(2))


def rise(load, window_in, window_out, wide_in, wide_out, half, target):
    target[...] = jnp.zeros_like(target)
    for r, value in enumerate(prolong_x(load, window_in, window_out)):
        half[r] = value
    prolong_y(half, wide_in, wide_out, target)


def coarse_kernel(
    message_ref, gather_ref, basis_ref, spectrum_ref, window_ref, level3_ref, ninth, level4, half3, *, size_x, size_y
):
    devices = size_x * size_y
    width = CY // 8 * size_y * Z4
    blocks = width // LANES
    used = Y4[1] * Z4
    tails = lane_index((devices, LANES))
    gathered = jnp.zeros((devices, LANES), jnp.float32)
    for b in range(Y4[1]):
        rows = message_ref[pl.ds(b, devices, stride=8), :]
        moved = pltpu.roll(rows, (b * Z4 - used) % LANES, 1)
        gathered = jnp.where((tails >= b * Z4) & (tails < (b + 1) * Z4), moved, gathered)
    ninth[...] = gathered

    def assemble(load, rows):
        total = [jnp.zeros((rows, LANES), jnp.float32) for _ in range(blocks)]
        lanes = lane_index((rows, LANES))
        for j in range(size_y):
            position = (j * (CY // 8) + Y4[0]) * Z4 % width
            block, offset = (position // LANES, position % LANES)
            value = jnp.where(lanes < used, load(j), 0.0)
            if offset == 0:
                total[block] = total[block] + value
                continue
            value = pltpu.roll(value, offset, 1)
            following = (block + 1) % blocks
            total[block] = total[block] + jnp.where(lanes >= offset, value, 0.0)
            total[following] = total[following] + jnp.where(lanes < offset, value, 0.0)
        return jnp.concatenate(total, axis=1)

    strips = []
    for i in range(size_x):
        strips.append(assemble(lambda j: message_ref[(i * size_y + j) * 8 : (i * size_y + j + 1) * 8, :], 8))
    tail = assemble(lambda j: ninth[pl.ds(j, size_x, stride=size_y), :], size_x)
    if size_x % 8:
        tail = jnp.concatenate([tail, jnp.zeros((8 - size_x % 8, width), jnp.float32)], axis=0)
    strips.append(tail)
    strips = jnp.concatenate(strips, axis=0)
    exact = dict(precision=HIGHEST, preferred_element_type=jnp.float32)
    modes = jnp.dot(gather_ref[...], strips, **exact)
    modes = lax.dot_general(modes, basis_ref[...], (((1,), (1,)), ((), ())), **exact)
    modes = jnp.dot(modes * spectrum_ref[...], basis_ref[...], **exact)
    shift = (width - (lax.axis_index("gy") * (CY // 8) + Y4[0]) * Z4) % width
    modes = pltpu.roll(modes, shift, 1)[:, :LANES]
    own = jnp.dot(window_ref[lax.axis_index("gx")], modes, **exact)
    lanes = lane_index(own.shape)
    inside4 = (lanes >= LANE4) & (lanes < LANE4 + Z4)
    level4[...] = jnp.zeros_like(level4)
    for b in range(Y4[1]):
        moved = jnp.where(inside4, pltpu.roll(own, (LANE4 - b * Z4) % LANES, 1), 0.0)
        level4[pl.ds(b, X4[1], stride=YP4), :] = moved[: X4[1]]

    rise(lambda i: level4[i * YP4 : (i + 1) * YP4, :], X4, X3, Y4, Y3, half3, level3_ref)


def field_kernel(
    raw_ref, part_ref, below_ref, above_ref, south_ref, north_ref, south2_ref, north2_ref,
    coarse_ref, spectrum_ref, depth_ref, frac_ref, cell_ref,
    potential_ref, atom_ref,
    reals, places, fine, pair, planes, planes_pair, smooth, smooth_pair,
    level3, half2, level2, half1, level1, field, partial,
    *, total_y,
):
    fill_tables(reals, places, None, frac_ref, cell_ref, total_y)
    merge_fine(raw_ref, below_ref, above_ref, south_ref, north_ref, fine)
    merge_coarse(part_ref, below_ref, above_ref, south_ref, north_ref, south2_ref, north2_ref, pair)
    stencil_rows(pair, X2[1], YP2, spectrum_ref[1], smooth_pair, planes_pair)
    lanes3 = lane_index((YP3, LANES))
    inside3 = (lanes3 >= LANE3) & (lanes3 < LANE4)
    for r in range(X3[1]):
        level3[r] = coarse_ref[r] + jnp.where(inside3, smooth_pair[r, 0:YP3, :], 0.0)
    rise(lambda i: level3[i], X3, X2, Y3, Y2, half2, level2)
    inside2 = lane_index((YP2, LANES)) < Z2
    for r in range(X2[1]):
        level2[r] = level2[r] + jnp.where(inside2, smooth_pair[r], 0.0)
    rise(lambda i: level2[i], X2, X1, Y2, Y1, half1, level1)
    stencil_rows(fine, X1[1], YP1, spectrum_ref[0], smooth, planes)

    rows = X1[1] * YP1
    modes = jnp.concatenate([smooth[...].reshape(rows, LANES), level1[...].reshape(rows, LANES)], axis=1)
    total = jnp.dot(triple(modes), depth_ref[...], preferred_element_type=jnp.float32)
    field[...] = total.reshape(X1[1], YP1, NZ)
    potential_ref[...] = field[0:CX, 0:CY, :]

    def step(group, carry):
        for p in range(GROUP):
            plane = group * GROUP + p
            high, low = halves(jnp.concatenate([field[plane + m] for m in range(4)], axis=0))
            left = jnp.concatenate([high, high, low], axis=1)
            rights = []
            for chunk in range(CHUNKS):
                highs, lows = along_z(reals, places, plane * CHUNKS + chunk)
                rights.append(jnp.concatenate(highs + lows + highs, axis=0))
            product = jnp.dot(left, jnp.concatenate(rights, axis=1), preferred_element_type=jnp.float32)
            for chunk in range(CHUNKS):
                row = plane * CHUNKS + chunk
                lanes = slice(chunk * LANES, (chunk + 1) * LANES)
                weights = [spread_row(reals, REAL_X + m, row) for m in range(4)]
                table, tile = pattern_y(reals, places, row)
                value = None
                for t in range(TILES_Y):
                    layer = None
                    for m in range(4):
                        at = m * YP1 + 8 * t
                        term = product[at : at + 8, lanes] * weights[m]
                        layer = term if layer is None else layer + term
                    value = layer if value is None else jnp.where(tile == t, layer, value)
                partial[pl.ds(row * 8, 8), :] = value * table
        return carry

    lax.fori_loop(0, CX // GROUP, step, 0)
    for g in range(ROWS // 8):
        total = partial[pl.ds(g * 64, 8, stride=8), :]
        for r in range(1, 8):
            total = total + partial[pl.ds(g * 64 + r, 8, stride=8), :]
        atom_ref[g * 8 : g * 8 + 8, :] = total


VM = pl.BlockSpec(memory_space=pltpu.VMEM)


RESIDENT = 2**19


def f32(*shape):
    if 4 * int(np.prod(shape)) <= RESIDENT:
        return pltpu.VMEM(shape, jnp.float32)
    return jax.ShapeDtypeStruct(shape, jnp.float32)


def scratch(*shape):
    return pltpu.VMEM(shape, jnp.float32)


def shifted(value, axis, steps):
    count = lax.axis_size(axis)
    return lax.ppermute(value, axis, [(source, (source + steps) % count) for source in range(count)])


def integers(*shape):
    return pltpu.VMEM(shape, jnp.int32)


def call(kernel, name, outs, scratches, *operands):
    return pl.pallas_call(
        kernel,
        in_specs=[VM] * len(operands),
        out_specs=[VM] * len(outs),
        out_shape=outs,
        scratch_shapes=scratches,
        name=name,
    )(*operands)


def resident(*values):
    return [
        pltpu.with_memory_space_constraint(value, pltpu.VMEM) if value.nbytes <= RESIDENT else value
        for value in values
    ]


def local(charges, fractions, cells):
    size_x = lax.axis_size("gx")
    size_y = lax.axis_size("gy")
    devices = size_x * size_y
    total_y = CY * size_y
    down_table, up_table = depth_tables()
    gather, basis, coarse_spectrum, window = (jnp.asarray(t) for t in coarse_tables(size_x, size_y))
    charge = charges.reshape(ROWS, LANES)
    frac = fractions.reshape(3, ROWS, LANES)
    cell = cells.reshape(2, ROWS, LANES).transpose(1, 0, 2).reshape(2 * ROWS, LANES)
    raw, part, low, high, message = call(
        functools.partial(deposit_kernel, total_y=total_y, devices=devices),
        "deposit",
        [
            f32(X1[1], YP1, LANES),
            f32(X2[1], YP2, LANES),
            f32(SLAB, LANES),
            f32(SLAB, LANES),
            f32(devices, 8, LANES),
        ],
        [
            scratch(REALS * ROWS, LANES),
            integers(PLACES * ROWS, LANES),
            scratch(X1[1], YP1, NZ),
            scratch(X1[1], YP1, LANES),
            scratch(X2[1], YP1 + 16, LANES),
            scratch(X3[1], YP2 + 24, LANES),
            scratch(X4[1], YP3 + 16, LANES),
            scratch(X4[1] * YP4, LANES),
        ],
        charge, frac, cell, down_table,
    )
    everyone = lax.all_to_all(message, ("gx", "gy"), 0, 0)
    below = shifted(high, "gx", 1)
    above = shifted(low, "gx", -1)
    up, down, up2, down2 = call(
        edges_kernel,
        "edges",
        [f32(EDGE, LANES), f32(EDGE, LANES), f32(FAR, LANES), f32(FAR, LANES)],
        [scratch(PAIR_X, YP2, LANES)],
        *resident(raw, part, below, above),
    )
    south = shifted(up, "gy", 1)
    north = shifted(down, "gy", -1)
    south2 = shifted(up2, "gy", 2)
    north2 = shifted(down2, "gy", -2)
    (coarse,) = call(
        functools.partial(coarse_kernel, size_x=size_x, size_y=size_y),
        "coarse",
        [f32(X3[1], YP3, LANES)],
        [scratch(devices, LANES), scratch(X4[1] * YP4, LANES), scratch(X3[1], YP4, LANES)],
        *resident(everyone.reshape(devices * 8, LANES), gather, basis, coarse_spectrum, window),
    )
    potential, atoms = call(
        functools.partial(field_kernel, total_y=total_y),
        "field",
        [jax.ShapeDtypeStruct((CX, CY, NZ), jnp.float32), jax.ShapeDtypeStruct((ROWS, LANES), jnp.float32)],
        [
            scratch(REALS * ROWS, LANES),
            integers(PLACES * ROWS, LANES),
            scratch(FINE_X, 32, LANES),
            scratch(PAIR_X, 24, LANES),
            scratch(4, FINE_X, YP1, LANES),
            scratch(4, PAIR_X, YP2, LANES),
            scratch(X1[1], YP1, LANES),
            scratch(X2[1], YP2, LANES),
            scratch(X3[1], YP3, LANES),
            scratch(X2[1], YP3, LANES),
            scratch(X2[1], YP2, LANES),
            scratch(X1[1], YP2, LANES),
            scratch(X1[1], YP1, LANES),
            scratch(X1[1], YP1, NZ),
            scratch(8 * ROWS, LANES),
        ],
        *resident(raw, part, below, above, south, north, south2, north2),
        *resident(coarse, jnp.asarray(spectra().astype(np.float32)), up_table, frac, cell),
    )
    return (potential, atoms.reshape(1, 1, ATOMS_DEV))


def solution(mesh):
    placed = (P("gx", "gy", None), P("gx", "gy", None, None), P("gx", "gy", None, None))
    return jax.shard_map(
        local,
        mesh=mesh,
        in_specs=placed,
        out_specs=(P("gx", "gy", None), P("gx", "gy", None)),
        check_vma=False,
    )
```

```python
import functools

import jax
import jax.numpy as jnp
import numpy as np
from jax import lax
from jax.experimental import pallas as pl
from jax.experimental.pallas import tpu as pltpu
from jax.sharding import PartitionSpec as P

CX = 32
CY = 16
NZ = 128
ATOMS_DEV = 16384

HIGHEST = lax.Precision.HIGHEST
RESTRICT_TAPS = ((-3, -0.0625), (-1, 0.5625), (0, 1.0), (1, 0.5625), (3, -0.0625))
PER_PLANE = ATOMS_DEV // CX
LANES = 128
CHUNKS = PER_PLANE // LANES
Z2, Z3, Z4 = (NZ // 2, NZ // 4, NZ // 8)
LANE3 = Z2
LANE4 = Z2 + Z3

X1, Y1 = (0, CX + 3), (0, CY + 3)


def coarser(window):
    first, count = window
    last = first + count - 1
    starts = [m for m in range(first - 4, last + 4) if any(first <= 2 * m + k <= last for k, _ in RESTRICT_TAPS)]
    return (starts[0], starts[-1] - starts[0] + 1)


X2, Y2 = coarser(X1), coarser(Y1)
X3, Y3 = coarser(X2), coarser(Y2)
X4, Y4 = coarser(X3), coarser(Y3)


def up8(count):
    return -(-count // 8) * 8


SLAB2 = 6 * Y1[1]
SLAB3 = SLAB2 + 4 * Y2[1]
SLAB = up8(SLAB3 + 2 * Y3[1])
FINE_X = X1[1] + 6
PAIR_X = CX // 2 + 10
SPAN3 = CX // 4 + 11
PACK2 = (PAIR_X + 1) // 2
PACK3 = (SPAN3 + 3) // 4
EDGE2 = up8(6 * FINE_X)
EDGE3 = EDGE2 + 8 * PACK2
EDGE = EDGE3 + 8 * PACK3
FAR = up8(4 * PACK3)
YP1, YP2, YP3, YP4 = (up8(Y1[1]), up8(Y2[1]), up8(Y3[1]), up8(Y4[1]))
PAD = 8


def real_basis(count):
    places = np.arange(count)
    rows = [np.full(count, 1.0 / np.sqrt(count))]
    for k in range(1, count // 2):
        rows.append(np.sqrt(2.0 / count) * np.cos(2 * np.pi * k * places / count))
        rows.append(np.sqrt(2.0 / count) * np.sin(2 * np.pi * k * places / count))
    rows.append(np.where(places % 2 == 0, 1.0, -1.0) / np.sqrt(count))
    return np.stack(rows)


def basis_frequency(count):
    return np.array([0] + [k for k in range(1, count // 2) for _ in range(2)] + [count // 2])


def restrict_matrix(count):
    matrix = np.zeros((count // 2, count))
    for m in range(count // 2):
        for k, weight in RESTRICT_TAPS:
            matrix[m, (2 * m + k) % count] += weight
    return matrix


def depth_matrix():
    first = restrict_matrix(NZ)
    second = restrict_matrix(Z2) @ first
    third = restrict_matrix(Z3) @ second
    parts = [real_basis(NZ), real_basis(Z2) @ first, real_basis(Z3) @ second, real_basis(Z4) @ third]
    parts.append(np.zeros((2 * LANES - sum(p.shape[0] for p in parts), NZ)))
    return np.concatenate(parts, axis=0)


def split_numpy(value):
    high = value.astype(np.float32).astype(jnp.bfloat16)
    low = (value - high.astype(np.float64)).astype(np.float32).astype(jnp.bfloat16)
    return high, low


def depth_tables():
    high, low = split_numpy(depth_matrix())
    down = np.concatenate([high.T, high.T, low.T, np.zeros_like(low.T)], axis=0)
    up = np.concatenate([high, high, low], axis=0)
    return jnp.asarray(down), jnp.asarray(up)


def smooth_numpy(rho):
    return np.where(rho < 1.0, 1.875 - 1.25 * rho * rho + 0.375 * rho**4, 1.0 / np.maximum(rho, 1.0))


def stencil_spectrum(level, count):
    offsets = np.arange(-3, 4) * 1.0
    near = np.arange(0, 4) * 1.0
    radius = np.sqrt(near[:, None, None] ** 2 + near[None, :, None] ** 2 + offsets[None, None, :] ** 2)
    stencil = (smooth_numpy(radius / 1.5) / 1.5 - smooth_numpy(radius / 3.0) / 3.0) / 2.0 ** (level - 1)
    waves = np.cos(2 * np.pi * offsets[:, None] * basis_frequency(count)[None, :] / count)
    return np.einsum("abd,dk->abk", stencil, waves)


def spectra():
    fine = stencil_spectrum(1, NZ).reshape(16, NZ)
    coarse = np.zeros((16, LANES))
    coarse[:, :Z2] = stencil_spectrum(2, Z2).reshape(16, Z2)
    coarse[:, LANE3:LANE4] = stencil_spectrum(3, Z3).reshape(16, Z3)
    return np.stack([fine, coarse])


def signed(count):
    places = np.arange(count)
    return np.where(places > count // 2, places - count, places) * 1.0


def coarse_tables(size_x, size_y):
    total_x = CX // 8 * size_x
    total_y = CY // 8 * size_y
    first = signed(total_x)[:, None, None]
    second = signed(total_y)[None, :, None]
    third = signed(Z4)[None, None, :]
    kernel = smooth_numpy(np.sqrt(first**2 + second**2 + third**2) / 1.5) / 12.0

    def cosines(count):
        return np.cos(2 * np.pi * basis_frequency(count)[:, None] * np.arange(count)[None, :] / count)

    spectrum = np.einsum("xyz,ax,by,cz->abc", kernel, cosines(total_x), cosines(total_y), cosines(Z4), optimize=True)
    spectrum = spectrum.reshape(total_x, total_y * Z4)
    basis_x = real_basis(total_x)
    basis_y = np.kron(real_basis(total_y), np.eye(Z4))
    span = X4[1]
    tail = up8(size_x)
    gather = np.zeros((total_x, 8 * size_x + tail))
    window = np.zeros((size_x, up8(span), total_x))
    for i in range(size_x):
        for a in range(span):
            place = (i * (CX // 8) + X4[0] + a) % total_x
            gather[:, i * 8 + a if a < 8 else 8 * size_x + i] = basis_x[:, place]
            window[i, a, :] = basis_x[:, place]
    return [t.astype(np.float32) for t in (gather, basis_y, spectrum, window)]


def spline_weights(frac):
    def near_weight(distance):
        return (1.0 - distance) * (1.0 + distance - 1.5 * distance * distance)

    def far_weight(distance):
        return -0.5 * (distance - 1.0) * (2.0 - distance) * (2.0 - distance)

    return [far_weight(1.0 + frac), near_weight(frac), near_weight(1.0 - frac), far_weight(2.0 - frac)]


ROWS = ATOMS_DEV // LANES
GROUP = 16
UNITS = 2
SHARE = GROUP // UNITS
GRID_X = X1[1] + X1[1] % 2
TILES_Y = YP1 // 8
TILES_Z = NZ // 8
REAL_X, REAL_Y, REAL_Z, REAL_TY, REAL_TZ = 0, 4, 8, 12, 14
REALS, PLACES = 16, 8
PARTS = 4


def fill_tables(reals, places, charge, frac_ref, cell_ref, total_y):
    first_y = lax.axis_index("gy") * CY + 1

    def put(ref, index, value):
        ref[index * ROWS : (index + 1) * ROWS, :] = value

    for dim, base in ((0, REAL_X), (1, REAL_Y), (2, REAL_Z)):
        weights = spline_weights(frac_ref[dim])
        for tap in range(4):
            put(reals, base + tap, weights[tap] if charge is None or dim else weights[tap] * charge)
    block_y = cell_ref[pl.ds(0, ROWS, stride=2), :] - first_y
    block_y = jnp.where(block_y < 0, block_y + total_y, block_y)
    block_z = (cell_ref[pl.ds(1, ROWS, stride=2), :] - 1) & (NZ - 1)
    for tap in range(4):
        put(places, tap, (block_y + tap) & 7)
        put(places, 4 + tap, (block_z + tap) & 7)
    tile_y = block_y >> 3
    tile_z = block_z >> 3
    put(reals, REAL_TY, tile_y.astype(jnp.float32))
    put(reals, REAL_TY + 1, (tile_y + 1).astype(jnp.float32))
    put(reals, REAL_TZ, tile_z.astype(jnp.float32))
    put(reals, REAL_TZ + 1, ((tile_z + 1) & (TILES_Z - 1)).astype(jnp.float32))


def spread_row(ref, index, row):
    return ref[pl.ds(index * ROWS + row, 8, stride=0), :]


def pattern_y(reals, places, row):
    index = lax.broadcasted_iota(jnp.int32, (8, LANES), 0)
    table = jnp.zeros((8, LANES), jnp.float32)
    for tap in range(4):
        place = spread_row(places, tap, row)
        table = jnp.where(index == place, spread_row(reals, REAL_Y + tap, row), table)
    start = spread_row(places, 0, row)
    tile = jnp.where(index >= start, spread_row(reals, REAL_TY, row), spread_row(reals, REAL_TY + 1, row))
    return table, tile


def along_z(reals, places, row):
    index = lax.broadcasted_iota(jnp.int32, (8, LANES), 0)
    table = jnp.zeros((8, LANES), jnp.float32)
    for tap in range(4):
        table = jnp.where(index == spread_row(places, 4 + tap, row), spread_row(reals, REAL_Z + tap, row), table)
    start = spread_row(places, 4, row)
    tile = jnp.where(index >= start, spread_row(reals, REAL_TZ, row), spread_row(reals, REAL_TZ + 1, row))
    high = jnp.concatenate([table, table], axis=0).astype(jnp.bfloat16)
    low = table - high.astype(jnp.float32)[0:8]
    low = jnp.concatenate([low, low], axis=0).astype(jnp.bfloat16)
    tile = jnp.concatenate([tile, tile - 1.0], axis=0).astype(jnp.bfloat16)
    zero = jnp.zeros((16, LANES), jnp.bfloat16)
    highs, lows = [], []
    for t in range(0, TILES_Z, 2):
        same = tile == jnp.bfloat16(t)
        highs.append(jnp.where(same, high, zero))
        lows.append(jnp.where(same, low, zero))
    return highs, lows


def along_xy(reals, places, row):
    table, tile = pattern_y(reals, places, row)
    tile = jnp.concatenate([tile, tile], axis=0).astype(jnp.bfloat16)
    zero = jnp.zeros((16, LANES), jnp.bfloat16)
    same = [tile == jnp.bfloat16(t) for t in range(TILES_Y)]
    taps = []
    for pair in range(2):
        both = jnp.concatenate([table * spread_row(reals, REAL_X + 2 * pair + m, row) for m in range(2)], axis=0)
        high = both.astype(jnp.bfloat16).astype(jnp.float32)
        low = both - high
        for at in (slice(0, 8), slice(8, 16)):
            value = jnp.concatenate([high[at], low[at]], axis=0).astype(jnp.bfloat16)
            taps.append(jnp.concatenate([jnp.where(mask, value, zero) for mask in same], axis=0))
    return taps


def triple(value):
    high, low = halves(value)
    return jnp.concatenate([high, low, high], axis=1)


def halves(value):
    high = value.astype(jnp.bfloat16)
    low = (value - high.astype(jnp.float32)).astype(jnp.bfloat16)
    return high, low


def lane_index(shape):
    return lax.broadcasted_iota(jnp.int32, shape, len(shape) - 1)


def restrict_x(load, window_in, window_out):
    first, count = window_in
    outs = []
    for m in range(window_out[0], window_out[0] + window_out[1]):
        total = None
        for k, weight in RESTRICT_TAPS:
            place = 2 * m + k - first
            if 0 <= place < count:
                term = load(place) if weight == 1.0 else weight * load(place)
                total = term if total is None else total + term
        outs.append(total)
    return outs


def restrict_y(source, window_in, window_out, rows_out):
    total = None
    for k, weight in RESTRICT_TAPS:
        start = 2 * window_out[0] + k - window_in[0] + PAD
        term = source[:, pl.ds(start, rows_out, stride=2), :]
        term = term if weight == 1.0 else weight * term
        total = term if total is None else total + term
    places = lax.broadcasted_iota(jnp.int32, total.shape, 1)
    return jnp.where(places < window_out[1], total, 0.0)


def deposit_kernel(
    charge_ref, frac_ref, cell_ref, depth_ref,
    raw_ref, part_ref, low_ref, high_ref, message_ref,
    reals, places, grid, coarse, half2, half3, half4, last,
    *, total_y, devices,
):
    fill_tables(reals, places, charge_ref[...], frac_ref, cell_ref, total_y)
    grid[...] = jnp.zeros_like(grid)

    def planes(group, *accs):
        sums = [None] * (GROUP + 3)

        def pop(unit, i):
            value = pltpu.matmul_pop(accs[unit * (SHARE + 3) + i])
            parts = []
            for t in range(TILES_Y):
                upper = value[16 * t : 16 * t + 8, :NZ] + value[16 * t : 16 * t + 8, NZ:]
                parts.append(upper + value[16 * t + 8 : 16 * t + 16, :NZ])
            layer = jnp.concatenate(parts, axis=0)
            at = unit * SHARE + i
            sums[at] = layer if sums[at] is None else sums[at] + layer

        for q in range(SHARE):
            for unit in range(UNITS):
                taps, tables = [], []
                for chunk in range(CHUNKS):
                    row = (group * GROUP + unit * SHARE + q) * CHUNKS + chunk
                    taps.append(along_xy(reals, places, row))
                    highs, lows = along_z(reals, places, row)
                    tables.append(jnp.concatenate(highs + lows, axis=0))
                for half in range(CHUNKS // 2):
                    both = (2 * half, 2 * half + 1)
                    table = jnp.concatenate([tables[c] for c in both], axis=1)
                    pltpu.matmul_push_rhs(table, half, unit, transpose=True)
                    for m in range(4):
                        left = jnp.concatenate([taps[c][m] for c in both], axis=1)
                        target = accs[unit * (SHARE + 3) + q + m]
                        pltpu.matmul_acc_lhs(target, left, half if m == 0 else None)
                pop(unit, q)
        for unit in range(UNITS):
            for i in range(SHARE, SHARE + 3):
                pop(unit, i)
        for i in range(GROUP + 3):
            at = group * GROUP + i
            grid[at] = grid[at] + sums[i]

    def step(group, carry):
        shape = (2 * YP1, 2 * NZ)
        units = [unit for unit in range(UNITS) for _ in range(SHARE + 3)]
        pl.run_scoped(functools.partial(planes, group), *(pltpu.ACC(mxu_id=u)(shape, jnp.float32) for u in units))
        return carry

    lax.fori_loop(0, CX // GROUP, step, 0)

    def transform(*accs):
        span = GRID_X // UNITS
        for unit, acc in enumerate(accs):
            rows = grid[unit * span : (unit + 1) * span].reshape(span * YP1, NZ)
            left = jnp.concatenate(halves(rows), axis=1)
            for part in range(2):
                pltpu.matmul_push_rhs(depth_ref[part * 2 * NZ : (part + 1) * 2 * NZ, :], part, unit)
                pltpu.matmul_acc_lhs(acc, left, part)
        for unit, acc in enumerate(accs):
            value = pltpu.matmul_pop(acc).reshape(span, YP1, 2 * LANES)
            count = min(span, X1[1] - unit * span)
            raw_ref[unit * span : unit * span + count] = value[:count, :, :LANES]
            coarse[unit * span : unit * span + count] = value[:count, :, LANES:]

    shape = (GRID_X // UNITS * YP1, 2 * LANES)
    pl.run_scoped(transform, *(pltpu.ACC(mxu_id=unit)(shape, jnp.float32) for unit in range(UNITS)))

    def padded(half, outs, rows):
        half[...] = jnp.zeros_like(half)
        for i, value in enumerate(outs):
            half[i, PAD : PAD + rows, :] = value

    padded(half2, restrict_x(lambda i: coarse[i], X1, X2), YP1)
    level2 = restrict_y(half2, Y1, Y2, YP2)
    padded(half3, restrict_x(lambda i: level2[i], X2, X3), YP2)
    level3 = restrict_y(half3, Y2, Y3, YP3)
    padded(half4, restrict_x(lambda i: level3[i], X3, X4), YP3)
    last[...] = restrict_y(half4, Y3, Y4, YP4).reshape(X4[1] * YP4, LANES)

    lane2 = lane_index((YP2, LANES)) < Z2
    for i in range(X2[1]):
        other = level3[i] if i < X3[1] else jnp.zeros((YP2, LANES), jnp.float32)
        part_ref[i] = jnp.where(lane2, level2[i], other)
    for r in range(6):
        at = slice(r * Y1[1], (r + 1) * Y1[1])
        low_ref[at, :] = raw_ref[r, 0 : Y1[1], :]
        high_ref[at, :] = raw_ref[CX - 3 + r, 0 : Y1[1], :]
    base2 = CX // 2 - 4 - X2[0]
    base3 = CX // 4 - 5 - X3[0]
    for ref, at2, at3 in ((low_ref, 0, 0), (high_ref, base2, base3)):
        for r in range(4):
            first = part_ref[at2 + r, 0 : Y2[1], :]
            if r < 3:
                second = pltpu.roll(part_ref[at2 + 4 + r, 0 : YP2, :], Z2, 1)[: Y2[1]]
            else:
                second = jnp.zeros((Y2[1], LANES), jnp.float32)
            at = SLAB2 + r * Y2[1]
            ref[at : at + Y2[1], :] = jnp.where(lane_index((Y2[1], LANES)) < Z2, first, second)
        for r in range(2):
            total = jnp.zeros((YP3, LANES), jnp.float32)
            lanes3 = lane_index((YP3, LANES))
            for g in range(4):
                moved = part_ref[at3 + 2 * g + r, 0:YP3, :]
                moved = pltpu.roll(moved, (g * Z3 - LANE3) % LANES, 1)
                total = jnp.where((lanes3 >= g * Z3) & (lanes3 < (g + 1) * Z3), moved, total)
            at = SLAB3 + r * Y3[1]
            ref[at : at + Y3[1], :] = total[: Y3[1]]
        ref[SLAB3 + 2 * Y3[1] :, :] = jnp.zeros((SLAB - SLAB3 - 2 * Y3[1], LANES), jnp.float32)
    lanes = lane_index((8, LANES))
    message = jnp.zeros((8, LANES), jnp.float32)
    for b in range(Y4[1]):
        rows = last[pl.ds(b, 8, stride=YP4), :]
        moved = pltpu.roll(rows, (b * Z4 - LANE4) % LANES, 1)
        message = jnp.where((lanes >= b * Z4) & (lanes < (b + 1) * Z4), moved, message)
    tail = pltpu.roll(last[8 * YP4 : 9 * YP4, :], Y4[1] * Z4 - LANE4, 1)
    message = jnp.where(lanes >= Y4[1] * Z4, tail, message)
    for d in range(devices):
        message_ref[d] = message


def merge_pair(part_ref, below_ref, above_ref, pair, row0):
    lane2 = lane_index((Y2[1], LANES)) < Z2
    lanes3 = lane_index((Y3[1], LANES))
    inside3 = (lanes3 >= LANE3) & (lanes3 < LANE4)

    def add(x, value):
        if x < PAIR_X:
            rows = slice(row0, row0 + value.shape[0])
            pair[x, rows, :] = pair[x, rows, :] + value

    for r in range(X2[1]):
        pair[3 + r, row0 : row0 + YP2, :] = part_ref[r]
    for ref, at2, at3 in ((below_ref, 0, 0), (above_ref, CX // 2 + 3, CX // 4 + 3)):
        for r in range(4):
            both = ref[SLAB2 + r * Y2[1] : SLAB2 + (r + 1) * Y2[1], :]
            add(at2 + r, jnp.where(lane2, both, 0.0))
            if r < 3:
                add(at2 + 4 + r, jnp.where(lane2, pltpu.roll(both, Z2, 1), 0.0))
        for r in range(2):
            four = ref[SLAB3 + r * Y3[1] : SLAB3 + (r + 1) * Y3[1], :]
            for g in range(4):
                moved = pltpu.roll(four, (LANE3 - g * Z3) % LANES, 1)
                add(at3 + 2 * g + r, jnp.where(inside3, moved, 0.0))


def edges_kernel(raw_ref, part_ref, below_ref, above_ref, up_ref, down_ref, up2_ref, down2_ref, pair):
    for x in range(FINE_X):
        for ref, start in ((up_ref, CY - 3), (down_ref, 0)):
            value = None
            if 3 <= x < FINE_X - 3:
                value = raw_ref[x - 3, start : start + 6, :]
            for slab, at in ((below_ref, x), (above_ref, x - CX - 3)):
                if 0 <= at < 6:
                    extra = slab[at * Y1[1] + start : at * Y1[1] + start + 6, :]
                    value = extra if value is None else value + extra
            ref[6 * x : 6 * x + 6, :] = value
    pair[...] = jnp.zeros_like(pair)
    merge_pair(part_ref, below_ref, above_ref, pair, 0)
    low2 = lane_index((8, LANES)) < Z2
    lanes = lane_index((8, LANES))
    keep = lax.broadcasted_iota(jnp.int32, (8, LANES), 0) < 7
    zero = jnp.zeros((8, LANES), jnp.float32)
    for ref, far, at2, at3, at_far in (
        (up_ref, up2_ref, CY // 2 - 3, CY // 4 - 3, CY // 2 - 3),
        (down_ref, down2_ref, 0, 0, 0),
    ):
        if EDGE2 > 6 * FINE_X:
            ref[6 * FINE_X : EDGE2, :] = jnp.zeros((EDGE2 - 6 * FINE_X, LANES), jnp.float32)
        for r in range(PACK2):
            first = pair[r, at2 : at2 + 8, :]
            second = zero
            if r + PACK2 < PAIR_X:
                second = pltpu.roll(pair[r + PACK2, at2 : at2 + 8, :], Z2, 1)
            ref[EDGE2 + 8 * r : EDGE2 + 8 * r + 8, :] = jnp.where(keep, jnp.where(low2, first, second), 0.0)
        for r in range(PACK3):
            total, total_far = zero, zero
            for g in range(4):
                x = g * PACK3 + r
                if x >= SPAN3:
                    continue
                inside = (lanes >= g * Z3) & (lanes < (g + 1) * Z3)
                turn = (g * Z3 - LANE3) % LANES
                total = jnp.where(inside, pltpu.roll(pair[x, at3 : at3 + 8, :], turn, 1), total)
                total_far = jnp.where(inside, pltpu.roll(pair[x, at_far : at_far + 8, :], turn, 1), total_far)
            ref[EDGE3 + 8 * r : EDGE3 + 8 * r + 8, :] = total
            far[4 * r : 4 * r + 4, :] = total_far[0:4]
        if FAR > 4 * PACK3:
            far[4 * PACK3 :, :] = jnp.zeros((FAR - 4 * PACK3, LANES), jnp.float32)


def merge_fine(raw_ref, below_ref, above_ref, south_ref, north_ref, fine):
    fine[...] = jnp.zeros_like(fine)
    for x in range(FINE_X):
        if 3 <= x < FINE_X - 3:
            fine[x, 3 : 3 + YP1, :] = raw_ref[x - 3]
        for slab, at in ((below_ref, x), (above_ref, x - CX - 3)):
            if 0 <= at < 6:
                rows = slice(3, 3 + Y1[1])
                fine[x, rows, :] = fine[x, rows, :] + slab[at * Y1[1] : (at + 1) * Y1[1], :]
        fine[x, 0:6, :] = fine[x, 0:6, :] + south_ref[6 * x : 6 * x + 6, :]
        fine[x, CY + 3 : CY + 9, :] = fine[x, CY + 3 : CY + 9, :] + north_ref[6 * x : 6 * x + 6, :]


def merge_coarse(part_ref, below_ref, above_ref, south_ref, north_ref, south2_ref, north2_ref, pair):
    pair[...] = jnp.zeros_like(pair)
    merge_pair(part_ref, below_ref, above_ref, pair, 3)
    low2 = lane_index((8, LANES)) < Z2
    lanes = lane_index((8, LANES))
    inside = (lanes >= LANE3) & (lanes < LANE4)
    for ref, far, at2, at3, at_far in (
        (south_ref, south2_ref, 0, 0, 0),
        (north_ref, north2_ref, CY // 2 + 3, CY // 4 + 3, CY // 2 + 3),
    ):
        for r in range(PACK2):
            both = ref[EDGE2 + 8 * r : EDGE2 + 8 * r + 8, :]
            pair[r, at2 : at2 + 8, :] = pair[r, at2 : at2 + 8, :] + jnp.where(low2, both, 0.0)
            x = r + PACK2
            if x < PAIR_X:
                moved = jnp.where(low2, pltpu.roll(both, Z2, 1), 0.0)
                pair[x, at2 : at2 + 8, :] = pair[x, at2 : at2 + 8, :] + moved
        for r in range(PACK3):
            four = ref[EDGE3 + 8 * r : EDGE3 + 8 * r + 8, :]
            four_far = far[4 * r : 4 * r + 4, :]
            for g in range(4):
                x = g * PACK3 + r
                if x >= SPAN3:
                    continue
                turn = (LANE3 - g * Z3) % LANES
                moved = jnp.where(inside, pltpu.roll(four, turn, 1), 0.0)
                pair[x, at3 : at3 + 8, :] = pair[x, at3 : at3 + 8, :] + moved
                moved = jnp.where(inside[0:4], pltpu.roll(four_far, turn, 1), 0.0)
                pair[x, at_far : at_far + 4, :] = pair[x, at_far : at_far + 4, :] + moved


def stencil_rows(source, count, rows_out, table, target, planes):
    for i in range(count + 6):
        sums = [source[i, 3 : 3 + rows_out, :]]
        for b in range(1, 4):
            sums.append(source[i, 3 - b : 3 - b + rows_out, :] + source[i, 3 + b : 3 + b + rows_out, :])
        for a in range(4):
            value = table[4 * a : 4 * a + 1] * sums[0]
            for b in range(1, 4):
                value = value + table[4 * a + b : 4 * a + b + 1] * sums[b]
            planes[a, i] = value
    for i in range(count):
        value = planes[0, i + 3]
        for a in range(1, 4):
            value = value + (planes[a, i + 3 - a] + planes[a, i + 3 + a])
        target[i] = value


def prolong_x(load, window_in, window_out):
    outs = []
    first = window_in[0]
    for n in range(window_out[0], window_out[0] + window_out[1]):
        if n % 2 == 0:
            outs.append(load(n // 2 - first))
        else:
            m = (n - 1) // 2 - first
            outs.append(0.5625 * (load(m) + load(m + 1)) - 0.0625 * (load(m - 1) + load(m + 2)))
    return outs


def prolong_y(source, window_in, window_out, target):
    first, count = window_out
    even = first % 2
    evens = (count - even + 1) // 2
    start = (first + even) // 2 - window_in[0]
    target[:, pl.ds(even, evens, stride=2), :] = source[:, start : start + evens, :]
    odds = count - evens
    m = (first + 1 - even - 1) // 2 - window_in[0]

    def taken(shift):
        return source[:, m + shift : m + shift + odds, :]

    target[:, pl.ds(1 - even, odds, stride=2), :] = 0.5625 * (taken(0) + taken(1)) - 0.0625 * (taken(-1) + taken(2))


def rise(load, window_in, window_out, wide_in, wide_out, half, target):
    target[...] = jnp.zeros_like(target)
    for r, value in enumerate(prolong_x(load, window_in, window_out)):
        half[r] = value
    prolong_y(half, wide_in, wide_out, target)


def coarse_kernel(
    message_ref, gather_ref, basis_ref, spectrum_ref, window_ref, level3_ref, ninth, level4, half3, *, size_x, size_y
):
    devices = size_x * size_y
    width = CY // 8 * size_y * Z4
    blocks = width // LANES
    used = Y4[1] * Z4
    tails = lane_index((devices, LANES))
    gathered = jnp.zeros((devices, LANES), jnp.float32)
    for b in range(Y4[1]):
        rows = message_ref[pl.ds(b, devices, stride=8), :]
        moved = pltpu.roll(rows, (b * Z4 - used) % LANES, 1)
        gathered = jnp.where((tails >= b * Z4) & (tails < (b + 1) * Z4), moved, gathered)
    ninth[...] = gathered

    def assemble(load, rows):
        total = [jnp.zeros((rows, LANES), jnp.float32) for _ in range(blocks)]
        lanes = lane_index((rows, LANES))
        for j in range(size_y):
            position = (j * (CY // 8) + Y4[0]) * Z4 % width
            block, offset = (position // LANES, position % LANES)
            value = jnp.where(lanes < used, load(j), 0.0)
            if offset == 0:
                total[block] = total[block] + value
                continue
            value = pltpu.roll(value, offset, 1)
            following = (block + 1) % blocks
            total[block] = total[block] + jnp.where(lanes >= offset, value, 0.0)
            total[following] = total[following] + jnp.where(lanes < offset, value, 0.0)
        return jnp.concatenate(total, axis=1)

    strips = []
    for i in range(size_x):
        strips.append(assemble(lambda j: message_ref[(i * size_y + j) * 8 : (i * size_y + j + 1) * 8, :], 8))
    tail = assemble(lambda j: ninth[pl.ds(j, size_x, stride=size_y), :], size_x)
    if size_x % 8:
        tail = jnp.concatenate([tail, jnp.zeros((8 - size_x % 8, width), jnp.float32)], axis=0)
    strips.append(tail)
    strips = jnp.concatenate(strips, axis=0)
    exact = dict(precision=HIGHEST, preferred_element_type=jnp.float32)
    modes = jnp.dot(gather_ref[...], strips, **exact)
    modes = lax.dot_general(modes, basis_ref[...], (((1,), (1,)), ((), ())), **exact)
    modes = jnp.dot(modes * spectrum_ref[...], basis_ref[...], **exact)
    shift = (width - (lax.axis_index("gy") * (CY // 8) + Y4[0]) * Z4) % width
    modes = pltpu.roll(modes, shift, 1)[:, :LANES]
    own = jnp.dot(window_ref[lax.axis_index("gx")], modes, **exact)
    lanes = lane_index(own.shape)
    inside4 = (lanes >= LANE4) & (lanes < LANE4 + Z4)
    level4[...] = jnp.zeros_like(level4)
    for b in range(Y4[1]):
        moved = jnp.where(inside4, pltpu.roll(own, (LANE4 - b * Z4) % LANES, 1), 0.0)
        level4[pl.ds(b, X4[1], stride=YP4), :] = moved[: X4[1]]

    rise(lambda i: level4[i * YP4 : (i + 1) * YP4, :], X4, X3, Y4, Y3, half3, level3_ref)


def part_copies(pairs, sems, part):
    copies = []
    for i, (source, target) in enumerate(pairs):
        rows = source.shape[0] // PARTS
        at = pl.ds(pl.multiple_of(part * rows, 8), rows)
        copies.append(pltpu.make_async_copy(source.at[at], target.at[at], sems.at[i, part]))
    return copies


def atoms_kernel(frac_ref, cell_ref, token_ref, real_ref, place_ref, reals, places, sems, *, total_y):
    fill_tables(reals, places, None, frac_ref, cell_ref, total_y)
    pairs = ((reals, real_ref), (places, place_ref))
    for part in range(PARTS):
        for copy in part_copies(pairs, sems, part):
            copy.start()
    for part in range(PARTS):
        for copy in part_copies(pairs, sems, part):
            copy.wait()


def field_kernel(
    raw_ref, part_ref, below_ref, above_ref, south_ref, north_ref, south2_ref, north2_ref,
    coarse_ref, spectrum_ref, depth_ref, real_ref, place_ref,
    potential_ref, atom_ref,
    reals, places, sems, fine, pair, planes, planes_pair, smooth, smooth_pair,
    level3, half2, level2, half1, level1, field, partial,
):
    pairs = ((real_ref, reals), (place_ref, places))

    def fetch(part, carry):
        for copy in part_copies(pairs, sems, part):
            copy.start()
        return carry

    lax.fori_loop(0, PARTS, fetch, 0)
    merge_fine(raw_ref, below_ref, above_ref, south_ref, north_ref, fine)
    merge_coarse(part_ref, below_ref, above_ref, south_ref, north_ref, south2_ref, north2_ref, pair)
    stencil_rows(pair, X2[1], YP2, spectrum_ref[1], smooth_pair, planes_pair)
    lanes3 = lane_index((YP3, LANES))
    inside3 = (lanes3 >= LANE3) & (lanes3 < LANE4)
    for r in range(X3[1]):
        level3[r] = coarse_ref[r] + jnp.where(inside3, smooth_pair[r, 0:YP3, :], 0.0)
    rise(lambda i: level3[i], X3, X2, Y3, Y2, half2, level2)
    inside2 = lane_index((YP2, LANES)) < Z2
    for r in range(X2[1]):
        level2[r] = level2[r] + jnp.where(inside2, smooth_pair[r], 0.0)
    rise(lambda i: level2[i], X2, X1, Y2, Y1, half1, level1)
    stencil_rows(fine, X1[1], YP1, spectrum_ref[0], smooth, planes)

    rows = X1[1] * YP1
    modes = jnp.concatenate([smooth[...].reshape(rows, LANES), level1[...].reshape(rows, LANES)], axis=1)
    total = jnp.dot(triple(modes), depth_ref[...], preferred_element_type=jnp.float32)
    field[...] = total.reshape(X1[1], YP1, NZ)
    potential_ref[...] = field[0:CX, 0:CY, :]
    for part in range(PARTS):
        for copy in part_copies(pairs, sems, part):
            copy.wait()

    def step(group, carry):
        for p in range(GROUP):
            plane = group * GROUP + p
            high, low = halves(jnp.concatenate([field[plane + m] for m in range(4)], axis=0))
            left = jnp.concatenate([high, high, low], axis=1)
            rights = []
            for chunk in range(CHUNKS):
                highs, lows = along_z(reals, places, plane * CHUNKS + chunk)
                rights.append(jnp.concatenate(highs + lows + highs, axis=0))
            product = jnp.dot(left, jnp.concatenate(rights, axis=1), preferred_element_type=jnp.float32)
            for chunk in range(CHUNKS):
                row = plane * CHUNKS + chunk
                lanes = slice(chunk * LANES, (chunk + 1) * LANES)
                weights = [spread_row(reals, REAL_X + m, row) for m in range(4)]
                table, tile = pattern_y(reals, places, row)
                value = None
                for t in range(TILES_Y):
                    layer = None
                    for m in range(4):
                        at = m * YP1 + 8 * t
                        term = product[at : at + 8, lanes] * weights[m]
                        layer = term if layer is None else layer + term
                    value = layer if value is None else jnp.where(tile == t, layer, value)
                partial[pl.ds(row * 8, 8), :] = value * table
        return carry

    lax.fori_loop(0, CX // GROUP, step, 0)
    for g in range(ROWS // 8):
        total = partial[pl.ds(g * 64, 8, stride=8), :]
        for r in range(1, 8):
            total = total + partial[pl.ds(g * 64 + r, 8, stride=8), :]
        atom_ref[g * 8 : g * 8 + 8, :] = total


VM = pl.BlockSpec(memory_space=pltpu.VMEM)
HB = pl.BlockSpec(memory_space=pl.ANY)


RESIDENT = 2**19


def f32(*shape):
    if 4 * int(np.prod(shape)) <= RESIDENT:
        return pltpu.VMEM(shape, jnp.float32)
    return jax.ShapeDtypeStruct(shape, jnp.float32)


def scratch(*shape):
    return pltpu.VMEM(shape, jnp.float32)


def shifted(value, axis, steps):
    count = lax.axis_size(axis)
    return lax.ppermute(value, axis, [(source, (source + steps) % count) for source in range(count)])


def integers(*shape):
    return pltpu.VMEM(shape, jnp.int32)


def call(kernel, name, outs, scratches, *operands, far_in=(), far_out=()):
    return pl.pallas_call(
        kernel,
        in_specs=[VM] * len(operands) + [HB] * len(far_in),
        out_specs=[VM] * len(outs) + [HB] * len(far_out),
        out_shape=[*outs, *far_out],
        scratch_shapes=scratches,
        name=name,
    )(*operands, *far_in)


def resident(*values):
    return [
        pltpu.with_memory_space_constraint(value, pltpu.VMEM) if value.nbytes <= RESIDENT else value
        for value in values
    ]


def local(charges, fractions, cells):
    size_x = lax.axis_size("gx")
    size_y = lax.axis_size("gy")
    devices = size_x * size_y
    total_y = CY * size_y
    down_table, up_table = depth_tables()
    gather, basis, coarse_spectrum, window = (jnp.asarray(t) for t in coarse_tables(size_x, size_y))
    charge = charges.reshape(ROWS, LANES)
    frac = fractions.reshape(3, ROWS, LANES)
    cell = cells.reshape(2, ROWS, LANES).transpose(1, 0, 2).reshape(2 * ROWS, LANES)
    raw, part, low, high, message = call(
        functools.partial(deposit_kernel, total_y=total_y, devices=devices),
        "deposit",
        [
            f32(X1[1], YP1, LANES),
            f32(X2[1], YP2, LANES),
            f32(SLAB, LANES),
            f32(SLAB, LANES),
            f32(devices, 8, LANES),
        ],
        [
            scratch(REALS * ROWS, LANES),
            integers(PLACES * ROWS, LANES),
            scratch(GRID_X, YP1, NZ),
            scratch(X1[1], YP1, LANES),
            scratch(X2[1], YP1 + 16, LANES),
            scratch(X3[1], YP2 + 24, LANES),
            scratch(X4[1], YP3 + 16, LANES),
            scratch(X4[1] * YP4, LANES),
        ],
        charge, frac, cell, down_table,
    )
    everyone = lax.all_to_all(message, ("gx", "gy"), 0, 0)
    below = shifted(high, "gx", 1)
    above = shifted(low, "gx", -1)
    up, down, up2, down2 = call(
        edges_kernel,
        "edges",
        [f32(EDGE, LANES), f32(EDGE, LANES), f32(FAR, LANES), f32(FAR, LANES)],
        [scratch(PAIR_X, YP2, LANES)],
        *resident(raw, part, below, above),
    )
    south = shifted(up, "gy", 1)
    north = shifted(down, "gy", -1)
    south2 = shifted(up2, "gy", 2)
    north2 = shifted(down2, "gy", -2)
    (coarse,) = call(
        functools.partial(coarse_kernel, size_x=size_x, size_y=size_y),
        "coarse",
        [f32(X3[1], YP3, LANES)],
        [scratch(devices, LANES), scratch(X4[1] * YP4, LANES), scratch(X3[1], YP4, LANES)],
        *resident(everyone.reshape(devices * 8, LANES), gather, basis, coarse_spectrum, window),
    )
    sems = pltpu.SemaphoreType.DMA((2, PARTS))
    tables = call(
        functools.partial(atoms_kernel, total_y=total_y),
        "atoms",
        [],
        [scratch(REALS * ROWS, LANES), integers(PLACES * ROWS, LANES), sems],
        *resident(frac, cell),
        far_in=[up2],
        far_out=[pltpu.HBM((REALS * ROWS, LANES), jnp.float32), pltpu.HBM((PLACES * ROWS, LANES), jnp.int32)],
    )
    potential, atoms = call(
        field_kernel,
        "field",
        [jax.ShapeDtypeStruct((CX, CY, NZ), jnp.float32), jax.ShapeDtypeStruct((ROWS, LANES), jnp.float32)],
        [
            scratch(REALS * ROWS, LANES),
            integers(PLACES * ROWS, LANES),
            sems,
            scratch(FINE_X, 32, LANES),
            scratch(PAIR_X, 24, LANES),
            scratch(4, FINE_X, YP1, LANES),
            scratch(4, PAIR_X, YP2, LANES),
            scratch(X1[1], YP1, LANES),
            scratch(X2[1], YP2, LANES),
            scratch(X3[1], YP3, LANES),
            scratch(X2[1], YP3, LANES),
            scratch(X2[1], YP2, LANES),
            scratch(X1[1], YP2, LANES),
            scratch(X1[1], YP1, LANES),
            scratch(X1[1], YP1, NZ),
            scratch(8 * ROWS, LANES),
        ],
        *resident(raw, part, below, above, south, north, south2, north2),
        *resident(coarse, jnp.asarray(spectra().astype(np.float32)), up_table),
        far_in=tables,
    )
    return (potential, atoms.reshape(1, 1, ATOMS_DEV))


def solution(mesh):
    placed = (P("gx", "gy", None), P("gx", "gy", None, None), P("gx", "gy", None, None))
    return jax.shard_map(
        local,
        mesh=mesh,
        in_specs=placed,
        out_specs=(P("gx", "gy", None), P("gx", "gy", None)),
        check_vma=False,
    )
```

```python
import functools

import jax
import jax.numpy as jnp
import numpy as np
from jax import lax
from jax.experimental import pallas as pl
from jax.experimental.pallas import tpu as pltpu
from jax.sharding import PartitionSpec as P

CX = 32
CY = 16
NZ = 128
ATOMS_DEV = 16384

HIGHEST = lax.Precision.HIGHEST
RESTRICT_TAPS = ((-3, -0.0625), (-1, 0.5625), (0, 1.0), (1, 0.5625), (3, -0.0625))
PER_PLANE = ATOMS_DEV // CX
LANES = 128
CHUNKS = PER_PLANE // LANES
Z2, Z3, Z4 = (NZ // 2, NZ // 4, NZ // 8)
LANE3 = Z2
LANE4 = Z2 + Z3

X1, Y1 = (0, CX + 3), (0, CY + 3)


def coarser(window):
    first, count = window
    last = first + count - 1
    starts = [m for m in range(first - 4, last + 4) if any(first <= 2 * m + k <= last for k, _ in RESTRICT_TAPS)]
    return (starts[0], starts[-1] - starts[0] + 1)


X2, Y2 = coarser(X1), coarser(Y1)
X3, Y3 = coarser(X2), coarser(Y2)
X4, Y4 = coarser(X3), coarser(Y3)


def up8(count):
    return -(-count // 8) * 8


SLAB2 = 6 * Y1[1]
SLAB3 = SLAB2 + 4 * Y2[1]
SLAB = up8(SLAB3 + 2 * Y3[1])
FINE_X = X1[1] + 6
PAIR_X = CX // 2 + 10
SPAN3 = CX // 4 + 11
PACK2 = (PAIR_X + 1) // 2
PACK3 = (SPAN3 + 3) // 4
EDGE2 = up8(6 * FINE_X)
EDGE3 = EDGE2 + 8 * PACK2
EDGE = EDGE3 + 8 * PACK3
FAR = up8(4 * PACK3)
YP1, YP2, YP3, YP4 = (up8(Y1[1]), up8(Y2[1]), up8(Y3[1]), up8(Y4[1]))
PAD = 8


def real_basis(count):
    places = np.arange(count)
    rows = [np.full(count, 1.0 / np.sqrt(count))]
    for k in range(1, count // 2):
        rows.append(np.sqrt(2.0 / count) * np.cos(2 * np.pi * k * places / count))
        rows.append(np.sqrt(2.0 / count) * np.sin(2 * np.pi * k * places / count))
    rows.append(np.where(places % 2 == 0, 1.0, -1.0) / np.sqrt(count))
    return np.stack(rows)


def basis_frequency(count):
    return np.array([0] + [k for k in range(1, count // 2) for _ in range(2)] + [count // 2])


def restrict_matrix(count):
    matrix = np.zeros((count // 2, count))
    for m in range(count // 2):
        for k, weight in RESTRICT_TAPS:
            matrix[m, (2 * m + k) % count] += weight
    return matrix


def depth_matrix():
    first = restrict_matrix(NZ)
    second = restrict_matrix(Z2) @ first
    third = restrict_matrix(Z3) @ second
    parts = [real_basis(NZ), real_basis(Z2) @ first, real_basis(Z3) @ second, real_basis(Z4) @ third]
    parts.append(np.zeros((2 * LANES - sum(p.shape[0] for p in parts), NZ)))
    return np.concatenate(parts, axis=0)


def split_numpy(value):
    high = value.astype(np.float32).astype(jnp.bfloat16)
    low = (value - high.astype(np.float64)).astype(np.float32).astype(jnp.bfloat16)
    return high, low


def depth_tables():
    high, low = split_numpy(depth_matrix())
    down = np.concatenate([high.T, high.T, low.T, np.zeros_like(low.T)], axis=0)
    up = np.concatenate([high, low], axis=1)
    return jnp.asarray(down), jnp.asarray(up)


def smooth_numpy(rho):
    return np.where(rho < 1.0, 1.875 - 1.25 * rho * rho + 0.375 * rho**4, 1.0 / np.maximum(rho, 1.0))


def stencil_spectrum(level, count):
    offsets = np.arange(-3, 4) * 1.0
    near = np.arange(0, 4) * 1.0
    radius = np.sqrt(near[:, None, None] ** 2 + near[None, :, None] ** 2 + offsets[None, None, :] ** 2)
    stencil = (smooth_numpy(radius / 1.5) / 1.5 - smooth_numpy(radius / 3.0) / 3.0) / 2.0 ** (level - 1)
    waves = np.cos(2 * np.pi * offsets[:, None] * basis_frequency(count)[None, :] / count)
    return np.einsum("abd,dk->abk", stencil, waves)


def spectra():
    fine = stencil_spectrum(1, NZ).reshape(16, NZ)
    coarse = np.zeros((16, LANES))
    coarse[:, :Z2] = stencil_spectrum(2, Z2).reshape(16, Z2)
    coarse[:, LANE3:LANE4] = stencil_spectrum(3, Z3).reshape(16, Z3)
    return np.stack([fine, coarse])


def signed(count):
    places = np.arange(count)
    return np.where(places > count // 2, places - count, places) * 1.0


def coarse_tables(size_x, size_y):
    total_x = CX // 8 * size_x
    total_y = CY // 8 * size_y
    first = signed(total_x)[:, None, None]
    second = signed(total_y)[None, :, None]
    third = signed(Z4)[None, None, :]
    kernel = smooth_numpy(np.sqrt(first**2 + second**2 + third**2) / 1.5) / 12.0

    def cosines(count):
        return np.cos(2 * np.pi * basis_frequency(count)[:, None] * np.arange(count)[None, :] / count)

    spectrum = np.einsum("xyz,ax,by,cz->abc", kernel, cosines(total_x), cosines(total_y), cosines(Z4), optimize=True)
    spectrum = spectrum.reshape(total_x, total_y * Z4)
    basis_x = real_basis(total_x)
    basis_y = np.kron(real_basis(total_y), np.eye(Z4))
    span = X4[1]
    tail = up8(size_x)
    gather = np.zeros((total_x, 8 * size_x + tail))
    window = np.zeros((size_x, up8(span), total_x))
    for i in range(size_x):
        for a in range(span):
            place = (i * (CX // 8) + X4[0] + a) % total_x
            gather[:, i * 8 + a if a < 8 else 8 * size_x + i] = basis_x[:, place]
            window[i, a, :] = basis_x[:, place]
    return [t.astype(np.float32) for t in (gather, basis_y, spectrum, window)]


def spline_weights(frac):
    def near_weight(distance):
        return (1.0 - distance) * (1.0 + distance - 1.5 * distance * distance)

    def far_weight(distance):
        return -0.5 * (distance - 1.0) * (2.0 - distance) * (2.0 - distance)

    return [far_weight(1.0 + frac), near_weight(frac), near_weight(1.0 - frac), far_weight(2.0 - frac)]


ROWS = ATOMS_DEV // LANES
GROUP = 16
UNITS = 2
SHARE = GROUP // UNITS
GRID_X = X1[1] + X1[1] % 2
TILES_Y = YP1 // 8
TILES_Z = NZ // 8
REAL_X, REAL_Y, REAL_Z, REAL_TY, REAL_TZ = 0, 4, 8, 12, 14
REALS, PLACES = 16, 8
PARTS = 4


def fill_tables(reals, places, charge, frac_ref, cell_ref, total_y):
    first_y = lax.axis_index("gy") * CY + 1

    def put(ref, index, value):
        ref[index * ROWS : (index + 1) * ROWS, :] = value

    for dim, base in ((0, REAL_X), (1, REAL_Y), (2, REAL_Z)):
        weights = spline_weights(frac_ref[dim])
        for tap in range(4):
            put(reals, base + tap, weights[tap] if charge is None or dim else weights[tap] * charge)
    block_y = cell_ref[pl.ds(0, ROWS, stride=2), :] - first_y
    block_y = jnp.where(block_y < 0, block_y + total_y, block_y)
    block_z = (cell_ref[pl.ds(1, ROWS, stride=2), :] - 1) & (NZ - 1)
    for tap in range(4):
        put(places, tap, (block_y + tap) & 7)
        put(places, 4 + tap, (block_z + tap) & 7)
    tile_y = block_y >> 3
    tile_z = block_z >> 3
    put(reals, REAL_TY, tile_y.astype(jnp.float32))
    put(reals, REAL_TY + 1, (tile_y + 1).astype(jnp.float32))
    put(reals, REAL_TZ, tile_z.astype(jnp.float32))
    put(reals, REAL_TZ + 1, ((tile_z + 1) & (TILES_Z - 1)).astype(jnp.float32))


def spread_row(ref, index, row):
    return ref[pl.ds(index * ROWS + row, 8, stride=0), :]


def pattern_y(reals, places, row):
    index = lax.broadcasted_iota(jnp.int32, (8, LANES), 0)
    table = jnp.zeros((8, LANES), jnp.float32)
    for tap in range(4):
        place = spread_row(places, tap, row)
        table = jnp.where(index == place, spread_row(reals, REAL_Y + tap, row), table)
    start = spread_row(places, 0, row)
    tile = jnp.where(index >= start, spread_row(reals, REAL_TY, row), spread_row(reals, REAL_TY + 1, row))
    return table, tile


def along_z(reals, places, row):
    index = lax.broadcasted_iota(jnp.int32, (8, LANES), 0)
    table = jnp.zeros((8, LANES), jnp.float32)
    for tap in range(4):
        table = jnp.where(index == spread_row(places, 4 + tap, row), spread_row(reals, REAL_Z + tap, row), table)
    start = spread_row(places, 4, row)
    tile = jnp.where(index >= start, spread_row(reals, REAL_TZ, row), spread_row(reals, REAL_TZ + 1, row))
    high = jnp.concatenate([table, table], axis=0).astype(jnp.bfloat16)
    low = table - high.astype(jnp.float32)[0:8]
    low = jnp.concatenate([low, low], axis=0).astype(jnp.bfloat16)
    tile = jnp.concatenate([tile, tile - 1.0], axis=0).astype(jnp.bfloat16)
    zero = jnp.zeros((16, LANES), jnp.bfloat16)
    highs, lows = [], []
    for t in range(0, TILES_Z, 2):
        same = tile == jnp.bfloat16(t)
        highs.append(jnp.where(same, high, zero))
        lows.append(jnp.where(same, low, zero))
    return highs, lows


def along_xy(reals, places, row):
    table, tile = pattern_y(reals, places, row)
    tile = jnp.concatenate([tile, tile], axis=0).astype(jnp.bfloat16)
    zero = jnp.zeros((16, LANES), jnp.bfloat16)
    same = [tile == jnp.bfloat16(t) for t in range(TILES_Y)]
    taps = []
    for pair in range(2):
        both = jnp.concatenate([table * spread_row(reals, REAL_X + 2 * pair + m, row) for m in range(2)], axis=0)
        high = both.astype(jnp.bfloat16).astype(jnp.float32)
        low = both - high
        for at in (slice(0, 8), slice(8, 16)):
            value = jnp.concatenate([high[at], low[at]], axis=0).astype(jnp.bfloat16)
            taps.append(jnp.concatenate([jnp.where(mask, value, zero) for mask in same], axis=0))
    return taps


def halves(value):
    high = value.astype(jnp.bfloat16)
    low = (value - high.astype(jnp.float32)).astype(jnp.bfloat16)
    return high, low


def lane_index(shape):
    return lax.broadcasted_iota(jnp.int32, shape, len(shape) - 1)


def restrict_x(load, window_in, window_out):
    first, count = window_in
    outs = []
    for m in range(window_out[0], window_out[0] + window_out[1]):
        total = None
        for k, weight in RESTRICT_TAPS:
            place = 2 * m + k - first
            if 0 <= place < count:
                term = load(place) if weight == 1.0 else weight * load(place)
                total = term if total is None else total + term
        outs.append(total)
    return outs


def restrict_y(source, window_in, window_out, rows_out):
    total = None
    for k, weight in RESTRICT_TAPS:
        start = 2 * window_out[0] + k - window_in[0] + PAD
        term = source[:, pl.ds(start, rows_out, stride=2), :]
        term = term if weight == 1.0 else weight * term
        total = term if total is None else total + term
    places = lax.broadcasted_iota(jnp.int32, total.shape, 1)
    return jnp.where(places < window_out[1], total, 0.0)


def deposit_kernel(
    charge_ref, frac_ref, cell_ref, depth_ref,
    raw_ref, part_ref, low_ref, high_ref, message_ref,
    reals, places, grid, coarse, half2, half3, half4, last,
    *, total_y, devices,
):
    fill_tables(reals, places, charge_ref[...], frac_ref, cell_ref, total_y)
    grid[...] = jnp.zeros_like(grid)

    def planes(group, *accs):
        sums = [None] * (GROUP + 3)

        def pop(unit, i):
            value = pltpu.matmul_pop(accs[unit * (SHARE + 3) + i])
            parts = []
            for t in range(TILES_Y):
                upper = value[16 * t : 16 * t + 8, :NZ] + value[16 * t : 16 * t + 8, NZ:]
                parts.append(upper + value[16 * t + 8 : 16 * t + 16, :NZ])
            layer = jnp.concatenate(parts, axis=0)
            at = unit * SHARE + i
            sums[at] = layer if sums[at] is None else sums[at] + layer

        for q in range(SHARE):
            for unit in range(UNITS):
                taps, tables = [], []
                for chunk in range(CHUNKS):
                    row = (group * GROUP + unit * SHARE + q) * CHUNKS + chunk
                    taps.append(along_xy(reals, places, row))
                    highs, lows = along_z(reals, places, row)
                    tables.append(jnp.concatenate(highs + lows, axis=0))
                for half in range(CHUNKS // 2):
                    both = (2 * half, 2 * half + 1)
                    table = jnp.concatenate([tables[c] for c in both], axis=1)
                    pltpu.matmul_push_rhs(table, half, unit, transpose=True)
                    for m in range(4):
                        left = jnp.concatenate([taps[c][m] for c in both], axis=1)
                        target = accs[unit * (SHARE + 3) + q + m]
                        pltpu.matmul_acc_lhs(target, left, half if m == 0 else None)
                pop(unit, q)
        for unit in range(UNITS):
            for i in range(SHARE, SHARE + 3):
                pop(unit, i)
        for i in range(GROUP + 3):
            at = group * GROUP + i
            grid[at] = grid[at] + sums[i]

    def step(group, carry):
        shape = (2 * YP1, 2 * NZ)
        units = [unit for unit in range(UNITS) for _ in range(SHARE + 3)]
        pl.run_scoped(functools.partial(planes, group), *(pltpu.ACC(mxu_id=u)(shape, jnp.float32) for u in units))
        return carry

    lax.fori_loop(0, CX // GROUP, step, 0)

    def transform(*accs):
        span = GRID_X // UNITS
        for unit, acc in enumerate(accs):
            rows = grid[unit * span : (unit + 1) * span].reshape(span * YP1, NZ)
            left = jnp.concatenate(halves(rows), axis=1)
            for part in range(2):
                pltpu.matmul_push_rhs(depth_ref[part * 2 * NZ : (part + 1) * 2 * NZ, :], part, unit)
                pltpu.matmul_acc_lhs(acc, left, part)
        for unit, acc in enumerate(accs):
            value = pltpu.matmul_pop(acc).reshape(span, YP1, 2 * LANES)
            count = min(span, X1[1] - unit * span)
            raw_ref[unit * span : unit * span + count] = value[:count, :, :LANES]
            coarse[unit * span : unit * span + count] = value[:count, :, LANES:]

    shape = (GRID_X // UNITS * YP1, 2 * LANES)
    pl.run_scoped(transform, *(pltpu.ACC(mxu_id=unit)(shape, jnp.float32) for unit in range(UNITS)))

    def padded(half, outs, rows):
        half[...] = jnp.zeros_like(half)
        for i, value in enumerate(outs):
            half[i, PAD : PAD + rows, :] = value

    padded(half2, restrict_x(lambda i: coarse[i], X1, X2), YP1)
    level2 = restrict_y(half2, Y1, Y2, YP2)
    padded(half3, restrict_x(lambda i: level2[i], X2, X3), YP2)
    level3 = restrict_y(half3, Y2, Y3, YP3)
    padded(half4, restrict_x(lambda i: level3[i], X3, X4), YP3)
    last[...] = restrict_y(half4, Y3, Y4, YP4).reshape(X4[1] * YP4, LANES)

    lane2 = lane_index((YP2, LANES)) < Z2
    for i in range(X2[1]):
        other = level3[i] if i < X3[1] else jnp.zeros((YP2, LANES), jnp.float32)
        part_ref[i] = jnp.where(lane2, level2[i], other)
    for r in range(6):
        at = slice(r * Y1[1], (r + 1) * Y1[1])
        low_ref[at, :] = raw_ref[r, 0 : Y1[1], :]
        high_ref[at, :] = raw_ref[CX - 3 + r, 0 : Y1[1], :]
    base2 = CX // 2 - 4 - X2[0]
    base3 = CX // 4 - 5 - X3[0]
    for ref, at2, at3 in ((low_ref, 0, 0), (high_ref, base2, base3)):
        for r in range(4):
            first = part_ref[at2 + r, 0 : Y2[1], :]
            if r < 3:
                second = pltpu.roll(part_ref[at2 + 4 + r, 0 : YP2, :], Z2, 1)[: Y2[1]]
            else:
                second = jnp.zeros((Y2[1], LANES), jnp.float32)
            at = SLAB2 + r * Y2[1]
            ref[at : at + Y2[1], :] = jnp.where(lane_index((Y2[1], LANES)) < Z2, first, second)
        for r in range(2):
            total = jnp.zeros((YP3, LANES), jnp.float32)
            lanes3 = lane_index((YP3, LANES))
            for g in range(4):
                moved = part_ref[at3 + 2 * g + r, 0:YP3, :]
                moved = pltpu.roll(moved, (g * Z3 - LANE3) % LANES, 1)
                total = jnp.where((lanes3 >= g * Z3) & (lanes3 < (g + 1) * Z3), moved, total)
            at = SLAB3 + r * Y3[1]
            ref[at : at + Y3[1], :] = total[: Y3[1]]
        ref[SLAB3 + 2 * Y3[1] :, :] = jnp.zeros((SLAB - SLAB3 - 2 * Y3[1], LANES), jnp.float32)
    lanes = lane_index((8, LANES))
    message = jnp.zeros((8, LANES), jnp.float32)
    for b in range(Y4[1]):
        rows = last[pl.ds(b, 8, stride=YP4), :]
        moved = pltpu.roll(rows, (b * Z4 - LANE4) % LANES, 1)
        message = jnp.where((lanes >= b * Z4) & (lanes < (b + 1) * Z4), moved, message)
    tail = pltpu.roll(last[8 * YP4 : 9 * YP4, :], Y4[1] * Z4 - LANE4, 1)
    message = jnp.where(lanes >= Y4[1] * Z4, tail, message)
    for d in range(devices):
        message_ref[d] = message


def merge_pair(part_ref, below_ref, above_ref, pair, row0):
    lane2 = lane_index((Y2[1], LANES)) < Z2
    lanes3 = lane_index((Y3[1], LANES))
    inside3 = (lanes3 >= LANE3) & (lanes3 < LANE4)

    def add(x, value):
        if x < PAIR_X:
            rows = slice(row0, row0 + value.shape[0])
            pair[x, rows, :] = pair[x, rows, :] + value

    for r in range(X2[1]):
        pair[3 + r, row0 : row0 + YP2, :] = part_ref[r]
    for ref, at2, at3 in ((below_ref, 0, 0), (above_ref, CX // 2 + 3, CX // 4 + 3)):
        for r in range(4):
            both = ref[SLAB2 + r * Y2[1] : SLAB2 + (r + 1) * Y2[1], :]
            add(at2 + r, jnp.where(lane2, both, 0.0))
            if r < 3:
                add(at2 + 4 + r, jnp.where(lane2, pltpu.roll(both, Z2, 1), 0.0))
        for r in range(2):
            four = ref[SLAB3 + r * Y3[1] : SLAB3 + (r + 1) * Y3[1], :]
            for g in range(4):
                moved = pltpu.roll(four, (LANE3 - g * Z3) % LANES, 1)
                add(at3 + 2 * g + r, jnp.where(inside3, moved, 0.0))


def edges_kernel(raw_ref, part_ref, below_ref, above_ref, up_ref, down_ref, up2_ref, down2_ref, pair):
    for x in range(FINE_X):
        for ref, start in ((up_ref, CY - 3), (down_ref, 0)):
            value = None
            if 3 <= x < FINE_X - 3:
                value = raw_ref[x - 3, start : start + 6, :]
            for slab, at in ((below_ref, x), (above_ref, x - CX - 3)):
                if 0 <= at < 6:
                    extra = slab[at * Y1[1] + start : at * Y1[1] + start + 6, :]
                    value = extra if value is None else value + extra
            ref[6 * x : 6 * x + 6, :] = value
    pair[...] = jnp.zeros_like(pair)
    merge_pair(part_ref, below_ref, above_ref, pair, 0)
    low2 = lane_index((8, LANES)) < Z2
    lanes = lane_index((8, LANES))
    keep = lax.broadcasted_iota(jnp.int32, (8, LANES), 0) < 7
    zero = jnp.zeros((8, LANES), jnp.float32)
    for ref, far, at2, at3, at_far in (
        (up_ref, up2_ref, CY // 2 - 3, CY // 4 - 3, CY // 2 - 3),
        (down_ref, down2_ref, 0, 0, 0),
    ):
        if EDGE2 > 6 * FINE_X:
            ref[6 * FINE_X : EDGE2, :] = jnp.zeros((EDGE2 - 6 * FINE_X, LANES), jnp.float32)
        for r in range(PACK2):
            first = pair[r, at2 : at2 + 8, :]
            second = zero
            if r + PACK2 < PAIR_X:
                second = pltpu.roll(pair[r + PACK2, at2 : at2 + 8, :], Z2, 1)
            ref[EDGE2 + 8 * r : EDGE2 + 8 * r + 8, :] = jnp.where(keep, jnp.where(low2, first, second), 0.0)
        for r in range(PACK3):
            total, total_far = zero, zero
            for g in range(4):
                x = g * PACK3 + r
                if x >= SPAN3:
                    continue
                inside = (lanes >= g * Z3) & (lanes < (g + 1) * Z3)
                turn = (g * Z3 - LANE3) % LANES
                total = jnp.where(inside, pltpu.roll(pair[x, at3 : at3 + 8, :], turn, 1), total)
                total_far = jnp.where(inside, pltpu.roll(pair[x, at_far : at_far + 8, :], turn, 1), total_far)
            ref[EDGE3 + 8 * r : EDGE3 + 8 * r + 8, :] = total
            far[4 * r : 4 * r + 4, :] = total_far[0:4]
        if FAR > 4 * PACK3:
            far[4 * PACK3 :, :] = jnp.zeros((FAR - 4 * PACK3, LANES), jnp.float32)


def merge_fine(raw_ref, below_ref, above_ref, south_ref, north_ref, fine):
    fine[...] = jnp.zeros_like(fine)
    for x in range(FINE_X):
        if 3 <= x < FINE_X - 3:
            fine[x, 3 : 3 + YP1, :] = raw_ref[x - 3]
        for slab, at in ((below_ref, x), (above_ref, x - CX - 3)):
            if 0 <= at < 6:
                rows = slice(3, 3 + Y1[1])
                fine[x, rows, :] = fine[x, rows, :] + slab[at * Y1[1] : (at + 1) * Y1[1], :]
        fine[x, 0:6, :] = fine[x, 0:6, :] + south_ref[6 * x : 6 * x + 6, :]
        fine[x, CY + 3 : CY + 9, :] = fine[x, CY + 3 : CY + 9, :] + north_ref[6 * x : 6 * x + 6, :]


def merge_coarse(part_ref, below_ref, above_ref, south_ref, north_ref, south2_ref, north2_ref, pair):
    pair[...] = jnp.zeros_like(pair)
    merge_pair(part_ref, below_ref, above_ref, pair, 3)
    low2 = lane_index((8, LANES)) < Z2
    lanes = lane_index((8, LANES))
    inside = (lanes >= LANE3) & (lanes < LANE4)
    for ref, far, at2, at3, at_far in (
        (south_ref, south2_ref, 0, 0, 0),
        (north_ref, north2_ref, CY // 2 + 3, CY // 4 + 3, CY // 2 + 3),
    ):
        for r in range(PACK2):
            both = ref[EDGE2 + 8 * r : EDGE2 + 8 * r + 8, :]
            pair[r, at2 : at2 + 8, :] = pair[r, at2 : at2 + 8, :] + jnp.where(low2, both, 0.0)
            x = r + PACK2
            if x < PAIR_X:
                moved = jnp.where(low2, pltpu.roll(both, Z2, 1), 0.0)
                pair[x, at2 : at2 + 8, :] = pair[x, at2 : at2 + 8, :] + moved
        for r in range(PACK3):
            four = ref[EDGE3 + 8 * r : EDGE3 + 8 * r + 8, :]
            four_far = far[4 * r : 4 * r + 4, :]
            for g in range(4):
                x = g * PACK3 + r
                if x >= SPAN3:
                    continue
                turn = (LANE3 - g * Z3) % LANES
                moved = jnp.where(inside, pltpu.roll(four, turn, 1), 0.0)
                pair[x, at3 : at3 + 8, :] = pair[x, at3 : at3 + 8, :] + moved
                moved = jnp.where(inside[0:4], pltpu.roll(four_far, turn, 1), 0.0)
                pair[x, at_far : at_far + 4, :] = pair[x, at_far : at_far + 4, :] + moved


def stencil_rows(source, count, rows_out, table, target, planes):
    for i in range(count + 6):
        sums = [source[i, 3 : 3 + rows_out, :]]
        for b in range(1, 4):
            sums.append(source[i, 3 - b : 3 - b + rows_out, :] + source[i, 3 + b : 3 + b + rows_out, :])
        for a in range(4):
            value = table[4 * a : 4 * a + 1] * sums[0]
            for b in range(1, 4):
                value = value + table[4 * a + b : 4 * a + b + 1] * sums[b]
            planes[a, i] = value
    for i in range(count):
        value = planes[0, i + 3]
        for a in range(1, 4):
            value = value + (planes[a, i + 3 - a] + planes[a, i + 3 + a])
        target[i] = value


def prolong_x(load, window_in, window_out):
    outs = []
    first = window_in[0]
    for n in range(window_out[0], window_out[0] + window_out[1]):
        if n % 2 == 0:
            outs.append(load(n // 2 - first))
        else:
            m = (n - 1) // 2 - first
            outs.append(0.5625 * (load(m) + load(m + 1)) - 0.0625 * (load(m - 1) + load(m + 2)))
    return outs


def prolong_y(source, window_in, window_out, target):
    first, count = window_out
    even = first % 2
    evens = (count - even + 1) // 2
    start = (first + even) // 2 - window_in[0]
    target[:, pl.ds(even, evens, stride=2), :] = source[:, start : start + evens, :]
    odds = count - evens
    m = (first + 1 - even - 1) // 2 - window_in[0]

    def taken(shift):
        return source[:, m + shift : m + shift + odds, :]

    target[:, pl.ds(1 - even, odds, stride=2), :] = 0.5625 * (taken(0) + taken(1)) - 0.0625 * (taken(-1) + taken(2))


def rise(load, window_in, window_out, wide_in, wide_out, half, target):
    target[...] = jnp.zeros_like(target)
    for r, value in enumerate(prolong_x(load, window_in, window_out)):
        half[r] = value
    prolong_y(half, wide_in, wide_out, target)


def coarse_kernel(
    message_ref, gather_ref, basis_ref, spectrum_ref, window_ref, level3_ref, ninth, level4, half3, *, size_x, size_y
):
    devices = size_x * size_y
    width = CY // 8 * size_y * Z4
    blocks = width // LANES
    used = Y4[1] * Z4
    tails = lane_index((devices, LANES))
    gathered = jnp.zeros((devices, LANES), jnp.float32)
    for b in range(Y4[1]):
        rows = message_ref[pl.ds(b, devices, stride=8), :]
        moved = pltpu.roll(rows, (b * Z4 - used) % LANES, 1)
        gathered = jnp.where((tails >= b * Z4) & (tails < (b + 1) * Z4), moved, gathered)
    ninth[...] = gathered

    def assemble(load, rows):
        total = [jnp.zeros((rows, LANES), jnp.float32) for _ in range(blocks)]
        lanes = lane_index((rows, LANES))
        for j in range(size_y):
            position = (j * (CY // 8) + Y4[0]) * Z4 % width
            block, offset = (position // LANES, position % LANES)
            value = jnp.where(lanes < used, load(j), 0.0)
            if offset == 0:
                total[block] = total[block] + value
                continue
            value = pltpu.roll(value, offset, 1)
            following = (block + 1) % blocks
            total[block] = total[block] + jnp.where(lanes >= offset, value, 0.0)
            total[following] = total[following] + jnp.where(lanes < offset, value, 0.0)
        return jnp.concatenate(total, axis=1)

    strips = []
    for i in range(size_x):
        strips.append(assemble(lambda j: message_ref[(i * size_y + j) * 8 : (i * size_y + j + 1) * 8, :], 8))
    tail = assemble(lambda j: ninth[pl.ds(j, size_x, stride=size_y), :], size_x)
    if size_x % 8:
        tail = jnp.concatenate([tail, jnp.zeros((8 - size_x % 8, width), jnp.float32)], axis=0)
    strips.append(tail)
    strips = jnp.concatenate(strips, axis=0)
    exact = dict(precision=HIGHEST, preferred_element_type=jnp.float32)
    modes = jnp.dot(gather_ref[...], strips, **exact)
    modes = lax.dot_general(modes, basis_ref[...], (((1,), (1,)), ((), ())), **exact)
    modes = jnp.dot(modes * spectrum_ref[...], basis_ref[...], **exact)
    shift = (width - (lax.axis_index("gy") * (CY // 8) + Y4[0]) * Z4) % width
    modes = pltpu.roll(modes, shift, 1)[:, :LANES]
    own = jnp.dot(window_ref[lax.axis_index("gx")], modes, **exact)
    lanes = lane_index(own.shape)
    inside4 = (lanes >= LANE4) & (lanes < LANE4 + Z4)
    level4[...] = jnp.zeros_like(level4)
    for b in range(Y4[1]):
        moved = jnp.where(inside4, pltpu.roll(own, (LANE4 - b * Z4) % LANES, 1), 0.0)
        level4[pl.ds(b, X4[1], stride=YP4), :] = moved[: X4[1]]

    rise(lambda i: level4[i * YP4 : (i + 1) * YP4, :], X4, X3, Y4, Y3, half3, level3_ref)


def part_copies(pairs, sems, part):
    copies = []
    for i, (source, target) in enumerate(pairs):
        rows = source.shape[0] // PARTS
        at = pl.ds(pl.multiple_of(part * rows, 8), rows)
        copies.append(pltpu.make_async_copy(source.at[at], target.at[at], sems.at[i, part]))
    return copies


def atoms_kernel(frac_ref, cell_ref, token_ref, real_ref, place_ref, reals, places, sems, *, total_y):
    fill_tables(reals, places, None, frac_ref, cell_ref, total_y)
    pairs = ((reals, real_ref), (places, place_ref))
    for part in range(PARTS):
        for copy in part_copies(pairs, sems, part):
            copy.start()
    for part in range(PARTS):
        for copy in part_copies(pairs, sems, part):
            copy.wait()


def field_kernel(
    raw_ref, part_ref, below_ref, above_ref, south_ref, north_ref, south2_ref, north2_ref,
    coarse_ref, spectrum_ref, depth_ref, real_ref, place_ref,
    potential_ref, atom_ref,
    reals, places, sems, fine, pair, planes, planes_pair, smooth, smooth_pair,
    level3, half2, level2, half1, level1, field, partial,
):
    pairs = ((real_ref, reals), (place_ref, places))

    def fetch(part, carry):
        for copy in part_copies(pairs, sems, part):
            copy.start()
        return carry

    lax.fori_loop(0, PARTS, fetch, 0)
    merge_fine(raw_ref, below_ref, above_ref, south_ref, north_ref, fine)
    merge_coarse(part_ref, below_ref, above_ref, south_ref, north_ref, south2_ref, north2_ref, pair)
    stencil_rows(pair, X2[1], YP2, spectrum_ref[1], smooth_pair, planes_pair)
    lanes3 = lane_index((YP3, LANES))
    inside3 = (lanes3 >= LANE3) & (lanes3 < LANE4)
    for r in range(X3[1]):
        level3[r] = coarse_ref[r] + jnp.where(inside3, smooth_pair[r, 0:YP3, :], 0.0)
    rise(lambda i: level3[i], X3, X2, Y3, Y2, half2, level2)
    inside2 = lane_index((YP2, LANES)) < Z2
    for r in range(X2[1]):
        level2[r] = level2[r] + jnp.where(inside2, smooth_pair[r], 0.0)
    rise(lambda i: level2[i], X2, X1, Y2, Y1, half1, level1)
    stencil_rows(fine, X1[1], YP1, spectrum_ref[0], smooth, planes)


    def transform(*accs):
        span = GRID_X // UNITS
        for unit, acc in enumerate(accs):
            at = slice(unit * span, (unit + 1) * span)
            parts = [value[at].reshape(span * YP1, LANES) for value in (smooth, level1)]
            high, low = halves(jnp.concatenate(parts, axis=1))
            pltpu.matmul_push_rhs(depth_ref[...], 0, unit)
            pltpu.matmul_acc_lhs(acc, high, 0)
            pltpu.matmul_acc_lhs(acc, low, None)
        for unit, acc in enumerate(accs):
            value = pltpu.matmul_pop(acc)
            field[unit * span : (unit + 1) * span] = (value[:, :NZ] + value[:, NZ:]).reshape(span, YP1, NZ)

    shape = (GRID_X // UNITS * YP1, 2 * NZ)
    pl.run_scoped(transform, *(pltpu.ACC(mxu_id=unit)(shape, jnp.float32) for unit in range(UNITS)))
    potential_ref[...] = field[0:CX, 0:CY, :]
    for part in range(PARTS):
        for copy in part_copies(pairs, sems, part):
            copy.wait()

    half = CHUNKS // UNITS
    rows = 4 * YP1

    def sample(plane, unit, acc):
        product = pltpu.matmul_pop(acc)
        for c in range(half):
            row = plane * CHUNKS + unit * half + c
            lanes = slice(c * LANES, (c + 1) * LANES)
            weights = [spread_row(reals, REAL_X + m, row) for m in range(4)]
            table, tile = pattern_y(reals, places, row)
            value = None
            for t in range(TILES_Y):
                layer = None
                for m in range(4):
                    at = m * YP1 + 8 * t
                    term = product[at : at + 8, lanes] * weights[m]
                    layer = term if layer is None else layer + term
                value = layer if value is None else jnp.where(tile == t, layer, value)
            partial[pl.ds(row * 8, 8), :] = value * table

    def planes_of(group, *accs):
        depth = len(accs) // UNITS
        for p in range(GROUP):
            plane = group * GROUP + p
            high, low = halves(jnp.concatenate([field[plane + m] for m in range(4)], axis=0))
            first = jnp.concatenate([high, high], axis=1)
            second = jnp.concatenate([low, jnp.zeros_like(low)], axis=1)
            for unit in range(UNITS):
                tables = []
                for c in range(half):
                    highs, lows = along_z(reals, places, plane * CHUNKS + unit * half + c)
                    tables.append(jnp.concatenate(highs + lows, axis=0))
                acc = accs[unit * depth + p % depth]
                pltpu.matmul_push_rhs(jnp.concatenate(tables, axis=1), p % 2, unit)
                pltpu.matmul_acc_lhs(acc, first, p % 2)
                pltpu.matmul_acc_lhs(acc, second, None)
            if p > 0:
                for unit in range(UNITS):
                    sample(plane - 1, unit, accs[unit * depth + (p - 1) % depth])
        for unit in range(UNITS):
            sample(group * GROUP + GROUP - 1, unit, accs[unit * depth + (GROUP - 1) % depth])

    def step(group, carry):
        units = [unit for unit in range(UNITS) for _ in range(4)]
        accs = (pltpu.ACC(mxu_id=u)((rows, half * LANES), jnp.float32) for u in units)
        pl.run_scoped(functools.partial(planes_of, group), *accs)
        return carry

    lax.fori_loop(0, CX // GROUP, step, 0)
    for g in range(ROWS // 8):
        total = partial[pl.ds(g * 64, 8, stride=8), :]
        for r in range(1, 8):
            total = total + partial[pl.ds(g * 64 + r, 8, stride=8), :]
        atom_ref[g * 8 : g * 8 + 8, :] = total


VM = pl.BlockSpec(memory_space=pltpu.VMEM)
HB = pl.BlockSpec(memory_space=pl.ANY)


RESIDENT = 2**19


def f32(*shape):
    if 4 * int(np.prod(shape)) <= RESIDENT:
        return pltpu.VMEM(shape, jnp.float32)
    return jax.ShapeDtypeStruct(shape, jnp.float32)


def scratch(*shape):
    return pltpu.VMEM(shape, jnp.float32)


def shifted(value, axis, steps):
    count = lax.axis_size(axis)
    return lax.ppermute(value, axis, [(source, (source + steps) % count) for source in range(count)])


def integers(*shape):
    return pltpu.VMEM(shape, jnp.int32)


def call(kernel, name, outs, scratches, *operands, far_in=(), far_out=()):
    return pl.pallas_call(
        kernel,
        in_specs=[VM] * len(operands) + [HB] * len(far_in),
        out_specs=[VM] * len(outs) + [HB] * len(far_out),
        out_shape=[*outs, *far_out],
        scratch_shapes=scratches,
        name=name,
    )(*operands, *far_in)


def resident(*values):
    return [
        pltpu.with_memory_space_constraint(value, pltpu.VMEM) if value.nbytes <= RESIDENT else value
        for value in values
    ]


def local(charges, fractions, cells):
    size_x = lax.axis_size("gx")
    size_y = lax.axis_size("gy")
    devices = size_x * size_y
    total_y = CY * size_y
    down_table, up_table = depth_tables()
    gather, basis, coarse_spectrum, window = (jnp.asarray(t) for t in coarse_tables(size_x, size_y))
    charge = charges.reshape(ROWS, LANES)
    frac = fractions.reshape(3, ROWS, LANES)
    cell = cells.reshape(2, ROWS, LANES).transpose(1, 0, 2).reshape(2 * ROWS, LANES)
    raw, part, low, high, message = call(
        functools.partial(deposit_kernel, total_y=total_y, devices=devices),
        "deposit",
        [
            f32(X1[1], YP1, LANES),
            f32(X2[1], YP2, LANES),
            f32(SLAB, LANES),
            f32(SLAB, LANES),
            f32(devices, 8, LANES),
        ],
        [
            scratch(REALS * ROWS, LANES),
            integers(PLACES * ROWS, LANES),
            scratch(GRID_X, YP1, NZ),
            scratch(X1[1], YP1, LANES),
            scratch(X2[1], YP1 + 16, LANES),
            scratch(X3[1], YP2 + 24, LANES),
            scratch(X4[1], YP3 + 16, LANES),
            scratch(X4[1] * YP4, LANES),
        ],
        charge, frac, cell, down_table,
    )
    everyone = lax.all_to_all(message, ("gx", "gy"), 0, 0)
    below = shifted(high, "gx", 1)
    above = shifted(low, "gx", -1)
    up, down, up2, down2 = call(
        edges_kernel,
        "edges",
        [f32(EDGE, LANES), f32(EDGE, LANES), f32(FAR, LANES), f32(FAR, LANES)],
        [scratch(PAIR_X, YP2, LANES)],
        *resident(raw, part, below, above),
    )
    south = shifted(up, "gy", 1)
    north = shifted(down, "gy", -1)
    south2 = shifted(up2, "gy", 2)
    north2 = shifted(down2, "gy", -2)
    (coarse,) = call(
        functools.partial(coarse_kernel, size_x=size_x, size_y=size_y),
        "coarse",
        [f32(X3[1], YP3, LANES)],
        [scratch(devices, LANES), scratch(X4[1] * YP4, LANES), scratch(X3[1], YP4, LANES)],
        *resident(everyone.reshape(devices * 8, LANES), gather, basis, coarse_spectrum, window),
    )
    sems = pltpu.SemaphoreType.DMA((2, PARTS))
    tables = call(
        functools.partial(atoms_kernel, total_y=total_y),
        "atoms",
        [],
        [scratch(REALS * ROWS, LANES), integers(PLACES * ROWS, LANES), sems],
        *resident(frac, cell),
        far_in=[up2],
        far_out=[pltpu.HBM((REALS * ROWS, LANES), jnp.float32), pltpu.HBM((PLACES * ROWS, LANES), jnp.int32)],
    )
    potential, atoms = call(
        field_kernel,
        "field",
        [jax.ShapeDtypeStruct((CX, CY, NZ), jnp.float32), jax.ShapeDtypeStruct((ROWS, LANES), jnp.float32)],
        [
            scratch(REALS * ROWS, LANES),
            integers(PLACES * ROWS, LANES),
            sems,
            scratch(FINE_X, 32, LANES),
            scratch(PAIR_X, 24, LANES),
            scratch(4, FINE_X, YP1, LANES),
            scratch(4, PAIR_X, YP2, LANES),
            scratch(GRID_X, YP1, LANES),
            scratch(X2[1], YP2, LANES),
            scratch(X3[1], YP3, LANES),
            scratch(X2[1], YP3, LANES),
            scratch(X2[1], YP2, LANES),
            scratch(GRID_X, YP2, LANES),
            scratch(GRID_X, YP1, LANES),
            scratch(GRID_X, YP1, NZ),
            scratch(8 * ROWS, LANES),
        ],
        *resident(raw, part, below, above, south, north, south2, north2),
        *resident(coarse, jnp.asarray(spectra().astype(np.float32)), up_table),
        far_in=tables,
    )
    return (potential, atoms.reshape(1, 1, ATOMS_DEV))


def solution(mesh):
    placed = (P("gx", "gy", None), P("gx", "gy", None, None), P("gx", "gy", None, None))
    return jax.shard_map(
        local,
        mesh=mesh,
        in_specs=placed,
        out_specs=(P("gx", "gy", None), P("gx", "gy", None)),
        check_vma=False,
    )
```

```python
import functools

import jax
import jax.numpy as jnp
import numpy as np
from jax import lax
from jax.experimental import pallas as pl
from jax.experimental.pallas import tpu as pltpu
from jax.sharding import PartitionSpec as P

CX = 32
CY = 16
NZ = 128
ATOMS_DEV = 16384

HIGHEST = lax.Precision.HIGHEST
RESTRICT_TAPS = ((-3, -0.0625), (-1, 0.5625), (0, 1.0), (1, 0.5625), (3, -0.0625))
PER_PLANE = ATOMS_DEV // CX
LANES = 128
CHUNKS = PER_PLANE // LANES
Z2, Z3, Z4 = (NZ // 2, NZ // 4, NZ // 8)
LANE3 = Z2
LANE4 = Z2 + Z3

X1, Y1 = (0, CX + 3), (0, CY + 3)


def coarser(window):
    first, count = window
    last = first + count - 1
    starts = [m for m in range(first - 4, last + 4) if any(first <= 2 * m + k <= last for k, _ in RESTRICT_TAPS)]
    return (starts[0], starts[-1] - starts[0] + 1)


X2, Y2 = coarser(X1), coarser(Y1)
X3, Y3 = coarser(X2), coarser(Y2)
X4, Y4 = coarser(X3), coarser(Y3)


def up8(count):
    return -(-count // 8) * 8


SLAB2 = 6 * Y1[1]
SLAB3 = SLAB2 + 4 * Y2[1]
SLAB = up8(SLAB3 + 2 * Y3[1])
FINE_X = X1[1] + 6
PAIR_X = CX // 2 + 10
SPAN3 = CX // 4 + 11
PACK2 = (PAIR_X + 1) // 2
PACK3 = (SPAN3 + 3) // 4
EDGE2 = up8(6 * FINE_X)
EDGE3 = EDGE2 + 8 * PACK2
EDGE = EDGE3 + 8 * PACK3
FAR = up8(4 * PACK3)
YP1, YP2, YP3, YP4 = (up8(Y1[1]), up8(Y2[1]), up8(Y3[1]), up8(Y4[1]))
PAD = 8


def real_basis(count):
    places = np.arange(count)
    rows = [np.full(count, 1.0 / np.sqrt(count))]
    for k in range(1, count // 2):
        rows.append(np.sqrt(2.0 / count) * np.cos(2 * np.pi * k * places / count))
        rows.append(np.sqrt(2.0 / count) * np.sin(2 * np.pi * k * places / count))
    rows.append(np.where(places % 2 == 0, 1.0, -1.0) / np.sqrt(count))
    return np.stack(rows)


def basis_frequency(count):
    return np.array([0] + [k for k in range(1, count // 2) for _ in range(2)] + [count // 2])


def restrict_matrix(count):
    matrix = np.zeros((count // 2, count))
    for m in range(count // 2):
        for k, weight in RESTRICT_TAPS:
            matrix[m, (2 * m + k) % count] += weight
    return matrix


def depth_matrix():
    first = restrict_matrix(NZ)
    second = restrict_matrix(Z2) @ first
    third = restrict_matrix(Z3) @ second
    parts = [real_basis(NZ), real_basis(Z2) @ first, real_basis(Z3) @ second, real_basis(Z4) @ third]
    parts.append(np.zeros((2 * LANES - sum(p.shape[0] for p in parts), NZ)))
    return np.concatenate(parts, axis=0)


def split_numpy(value):
    high = value.astype(np.float32).astype(jnp.bfloat16)
    low = (value - high.astype(np.float64)).astype(np.float32).astype(jnp.bfloat16)
    return high, low


def depth_tables():
    high, low = split_numpy(depth_matrix())
    down = np.concatenate([high.T, high.T, low.T, np.zeros_like(low.T)], axis=0)
    up = np.concatenate([high, low], axis=1)
    return jnp.asarray(down), jnp.asarray(up)


def smooth_numpy(rho):
    return np.where(rho < 1.0, 1.875 - 1.25 * rho * rho + 0.375 * rho**4, 1.0 / np.maximum(rho, 1.0))


def stencil_spectrum(level, count):
    offsets = np.arange(-3, 4) * 1.0
    near = np.arange(0, 4) * 1.0
    radius = np.sqrt(near[:, None, None] ** 2 + near[None, :, None] ** 2 + offsets[None, None, :] ** 2)
    stencil = (smooth_numpy(radius / 1.5) / 1.5 - smooth_numpy(radius / 3.0) / 3.0) / 2.0 ** (level - 1)
    waves = np.cos(2 * np.pi * offsets[:, None] * basis_frequency(count)[None, :] / count)
    return np.einsum("abd,dk->abk", stencil, waves)


def spectra():
    fine = stencil_spectrum(1, NZ).reshape(16, NZ)
    coarse = np.zeros((16, LANES))
    coarse[:, :Z2] = stencil_spectrum(2, Z2).reshape(16, Z2)
    coarse[:, LANE3:LANE4] = stencil_spectrum(3, Z3).reshape(16, Z3)
    return np.stack([fine, coarse])


def signed(count):
    places = np.arange(count)
    return np.where(places > count // 2, places - count, places) * 1.0


def coarse_tables(size_x, size_y):
    total_x = CX // 8 * size_x
    total_y = CY // 8 * size_y
    first = signed(total_x)[:, None, None]
    second = signed(total_y)[None, :, None]
    third = signed(Z4)[None, None, :]
    kernel = smooth_numpy(np.sqrt(first**2 + second**2 + third**2) / 1.5) / 12.0

    def cosines(count):
        return np.cos(2 * np.pi * basis_frequency(count)[:, None] * np.arange(count)[None, :] / count)

    spectrum = np.einsum("xyz,ax,by,cz->abc", kernel, cosines(total_x), cosines(total_y), cosines(Z4), optimize=True)
    spectrum = spectrum.reshape(total_x, total_y * Z4)
    basis_x = real_basis(total_x)
    basis_y = np.kron(real_basis(total_y), np.eye(Z4))
    span = X4[1]
    tail = up8(size_x)
    gather = np.zeros((total_x, 8 * size_x + tail))
    window = np.zeros((size_x, up8(span), total_x))
    for i in range(size_x):
        for a in range(span):
            place = (i * (CX // 8) + X4[0] + a) % total_x
            gather[:, i * 8 + a if a < 8 else 8 * size_x + i] = basis_x[:, place]
            window[i, a, :] = basis_x[:, place]
    return [t.astype(np.float32) for t in (gather, basis_y, spectrum, window)]


def spline_weights(frac):
    def near_weight(distance):
        return (1.0 - distance) * (1.0 + distance - 1.5 * distance * distance)

    def far_weight(distance):
        return -0.5 * (distance - 1.0) * (2.0 - distance) * (2.0 - distance)

    return [far_weight(1.0 + frac), near_weight(frac), near_weight(1.0 - frac), far_weight(2.0 - frac)]


ROWS = ATOMS_DEV // LANES
GROUP = 16
UNITS = 2
SHARE = GROUP // UNITS
GRID_X = X1[1] + X1[1] % 2
TILES_Y = YP1 // 8
TILES_Z = NZ // 8
REAL_X, REAL_Y, REAL_Z, REAL_TY, REAL_TZ = 0, 4, 8, 12, 14
REALS, PLACES = 16, 8
PARTS = 4


def fill_tables(reals, places, charge, frac_ref, cell_ref, total_y):
    first_y = lax.axis_index("gy") * CY + 1

    def put(ref, index, value):
        ref[index * ROWS : (index + 1) * ROWS, :] = value

    for dim, base in ((0, REAL_X), (1, REAL_Y), (2, REAL_Z)):
        weights = spline_weights(frac_ref[dim])
        for tap in range(4):
            put(reals, base + tap, weights[tap] if charge is None or dim else weights[tap] * charge)
    block_y = cell_ref[pl.ds(0, ROWS, stride=2), :] - first_y
    block_y = jnp.where(block_y < 0, block_y + total_y, block_y)
    block_z = (cell_ref[pl.ds(1, ROWS, stride=2), :] - 1) & (NZ - 1)
    for tap in range(4):
        put(places, tap, (block_y + tap) & 7)
        put(places, 4 + tap, (block_z + tap) & 7)
    tile_y = block_y >> 3
    tile_z = block_z >> 3
    put(reals, REAL_TY, tile_y.astype(jnp.float32))
    put(reals, REAL_TY + 1, (tile_y + 1).astype(jnp.float32))
    put(reals, REAL_TZ, tile_z.astype(jnp.float32))
    put(reals, REAL_TZ + 1, ((tile_z + 1) & (TILES_Z - 1)).astype(jnp.float32))


def spread_row(ref, index, row):
    return ref[pl.ds(index * ROWS + row, 8, stride=0), :]


def pattern_y(reals, places, row):
    index = lax.broadcasted_iota(jnp.int32, (8, LANES), 0)
    table = jnp.zeros((8, LANES), jnp.float32)
    for tap in range(4):
        place = spread_row(places, tap, row)
        table = jnp.where(index == place, spread_row(reals, REAL_Y + tap, row), table)
    start = spread_row(places, 0, row)
    tile = jnp.where(index >= start, spread_row(reals, REAL_TY, row), spread_row(reals, REAL_TY + 1, row))
    return table, tile


def along_z(reals, places, row):
    index = lax.broadcasted_iota(jnp.int32, (8, LANES), 0)
    table = jnp.zeros((8, LANES), jnp.float32)
    for tap in range(4):
        table = jnp.where(index == spread_row(places, 4 + tap, row), spread_row(reals, REAL_Z + tap, row), table)
    start = spread_row(places, 4, row)
    tile = jnp.where(index >= start, spread_row(reals, REAL_TZ, row), spread_row(reals, REAL_TZ + 1, row))
    high = jnp.concatenate([table, table], axis=0).astype(jnp.bfloat16)
    low = table - high.astype(jnp.float32)[0:8]
    low = jnp.concatenate([low, low], axis=0).astype(jnp.bfloat16)
    tile = jnp.concatenate([tile, tile - 1.0], axis=0).astype(jnp.bfloat16)
    zero = jnp.zeros((16, LANES), jnp.bfloat16)
    highs, lows = [], []
    for t in range(0, TILES_Z, 2):
        same = tile == jnp.bfloat16(t)
        highs.append(jnp.where(same, high, zero))
        lows.append(jnp.where(same, low, zero))
    return highs, lows


def along_xy(reals, places, row):
    table, tile = pattern_y(reals, places, row)
    tile = jnp.concatenate([tile, tile], axis=0).astype(jnp.bfloat16)
    zero = jnp.zeros((16, LANES), jnp.bfloat16)
    same = [tile == jnp.bfloat16(t) for t in range(TILES_Y)]
    taps = []
    for pair in range(2):
        both = jnp.concatenate([table * spread_row(reals, REAL_X + 2 * pair + m, row) for m in range(2)], axis=0)
        high = both.astype(jnp.bfloat16).astype(jnp.float32)
        low = both - high
        for at in (slice(0, 8), slice(8, 16)):
            value = jnp.concatenate([high[at], low[at]], axis=0).astype(jnp.bfloat16)
            taps.append(jnp.concatenate([jnp.where(mask, value, zero) for mask in same], axis=0))
    return taps


def halves(value):
    high = value.astype(jnp.bfloat16)
    low = (value - high.astype(jnp.float32)).astype(jnp.bfloat16)
    return high, low


def lane_index(shape):
    return lax.broadcasted_iota(jnp.int32, shape, len(shape) - 1)


def restrict_x(load, window_in, window_out):
    first, count = window_in
    outs = []
    for m in range(window_out[0], window_out[0] + window_out[1]):
        total = None
        for k, weight in RESTRICT_TAPS:
            place = 2 * m + k - first
            if 0 <= place < count:
                term = load(place) if weight == 1.0 else weight * load(place)
                total = term if total is None else total + term
        outs.append(total)
    return outs


def restrict_y(source, window_in, window_out, rows_out):
    total = None
    for k, weight in RESTRICT_TAPS:
        start = 2 * window_out[0] + k - window_in[0] + PAD
        term = source[:, pl.ds(start, rows_out, stride=2), :]
        term = term if weight == 1.0 else weight * term
        total = term if total is None else total + term
    places = lax.broadcasted_iota(jnp.int32, total.shape, 1)
    return jnp.where(places < window_out[1], total, 0.0)


def deposit_kernel(
    charge_ref, frac_ref, cell_ref, depth_ref,
    raw_ref, part_ref, low_ref, high_ref, message_ref,
    table, table_sem, reals, places, grid, coarse, half2, half3, half4, last,
    *, total_y, devices,
):
    fetch = pltpu.make_async_copy(depth_ref, table, table_sem)
    fetch.start()
    fill_tables(reals, places, charge_ref[...], frac_ref, cell_ref, total_y)
    grid[...] = jnp.zeros_like(grid)

    def planes(group, *accs):
        sums = [None] * (GROUP + 3)

        def pop(unit, i):
            value = pltpu.matmul_pop(accs[unit * (SHARE + 3) + i])
            parts = []
            for t in range(TILES_Y):
                upper = value[16 * t : 16 * t + 8, :NZ] + value[16 * t : 16 * t + 8, NZ:]
                parts.append(upper + value[16 * t + 8 : 16 * t + 16, :NZ])
            layer = jnp.concatenate(parts, axis=0)
            at = unit * SHARE + i
            sums[at] = layer if sums[at] is None else sums[at] + layer

        for q in range(SHARE):
            for unit in range(UNITS):
                taps, tables = [], []
                for chunk in range(CHUNKS):
                    row = (group * GROUP + unit * SHARE + q) * CHUNKS + chunk
                    taps.append(along_xy(reals, places, row))
                    highs, lows = along_z(reals, places, row)
                    tables.append(jnp.concatenate(highs + lows, axis=0))
                for half in range(CHUNKS // 2):
                    both = (2 * half, 2 * half + 1)
                    table = jnp.concatenate([tables[c] for c in both], axis=1)
                    pltpu.matmul_push_rhs(table, half, unit, transpose=True)
                    for m in range(4):
                        left = jnp.concatenate([taps[c][m] for c in both], axis=1)
                        target = accs[unit * (SHARE + 3) + q + m]
                        pltpu.matmul_acc_lhs(target, left, half if m == 0 else None)
                pop(unit, q)
        for unit in range(UNITS):
            for i in range(SHARE, SHARE + 3):
                pop(unit, i)
        for i in range(GROUP + 3):
            at = group * GROUP + i
            grid[at] = grid[at] + sums[i]

    def step(group, carry):
        shape = (2 * YP1, 2 * NZ)
        units = [unit for unit in range(UNITS) for _ in range(SHARE + 3)]
        pl.run_scoped(functools.partial(planes, group), *(pltpu.ACC(mxu_id=u)(shape, jnp.float32) for u in units))
        return carry

    lax.fori_loop(0, CX // GROUP, step, 0)
    fetch.wait()

    def transform(*accs):
        span = GRID_X // UNITS
        for unit, acc in enumerate(accs):
            rows = grid[unit * span : (unit + 1) * span].reshape(span * YP1, NZ)
            left = jnp.concatenate(halves(rows), axis=1)
            for part in range(2):
                pltpu.matmul_push_rhs(table[part * 2 * NZ : (part + 1) * 2 * NZ, :], part, unit)
                pltpu.matmul_acc_lhs(acc, left, part)
        for unit, acc in enumerate(accs):
            value = pltpu.matmul_pop(acc).reshape(span, YP1, 2 * LANES)
            count = min(span, X1[1] - unit * span)
            raw_ref[unit * span : unit * span + count] = value[:count, :, :LANES]
            coarse[unit * span : unit * span + count] = value[:count, :, LANES:]

    shape = (GRID_X // UNITS * YP1, 2 * LANES)
    pl.run_scoped(transform, *(pltpu.ACC(mxu_id=unit)(shape, jnp.float32) for unit in range(UNITS)))

    def padded(half, outs, rows):
        half[...] = jnp.zeros_like(half)
        for i, value in enumerate(outs):
            half[i, PAD : PAD + rows, :] = value

    padded(half2, restrict_x(lambda i: coarse[i], X1, X2), YP1)
    level2 = restrict_y(half2, Y1, Y2, YP2)
    padded(half3, restrict_x(lambda i: level2[i], X2, X3), YP2)
    level3 = restrict_y(half3, Y2, Y3, YP3)
    padded(half4, restrict_x(lambda i: level3[i], X3, X4), YP3)
    last[...] = restrict_y(half4, Y3, Y4, YP4).reshape(X4[1] * YP4, LANES)

    lane2 = lane_index((YP2, LANES)) < Z2
    for i in range(X2[1]):
        other = level3[i] if i < X3[1] else jnp.zeros((YP2, LANES), jnp.float32)
        part_ref[i] = jnp.where(lane2, level2[i], other)
    for r in range(6):
        at = slice(r * Y1[1], (r + 1) * Y1[1])
        low_ref[at, :] = raw_ref[r, 0 : Y1[1], :]
        high_ref[at, :] = raw_ref[CX - 3 + r, 0 : Y1[1], :]
    base2 = CX // 2 - 4 - X2[0]
    base3 = CX // 4 - 5 - X3[0]
    for ref, at2, at3 in ((low_ref, 0, 0), (high_ref, base2, base3)):
        for r in range(4):
            first = part_ref[at2 + r, 0 : Y2[1], :]
            if r < 3:
                second = pltpu.roll(part_ref[at2 + 4 + r, 0 : YP2, :], Z2, 1)[: Y2[1]]
            else:
                second = jnp.zeros((Y2[1], LANES), jnp.float32)
            at = SLAB2 + r * Y2[1]
            ref[at : at + Y2[1], :] = jnp.where(lane_index((Y2[1], LANES)) < Z2, first, second)
        for r in range(2):
            total = jnp.zeros((YP3, LANES), jnp.float32)
            lanes3 = lane_index((YP3, LANES))
            for g in range(4):
                moved = part_ref[at3 + 2 * g + r, 0:YP3, :]
                moved = pltpu.roll(moved, (g * Z3 - LANE3) % LANES, 1)
                total = jnp.where((lanes3 >= g * Z3) & (lanes3 < (g + 1) * Z3), moved, total)
            at = SLAB3 + r * Y3[1]
            ref[at : at + Y3[1], :] = total[: Y3[1]]
        ref[SLAB3 + 2 * Y3[1] :, :] = jnp.zeros((SLAB - SLAB3 - 2 * Y3[1], LANES), jnp.float32)
    lanes = lane_index((8, LANES))
    message = jnp.zeros((8, LANES), jnp.float32)
    for b in range(Y4[1]):
        rows = last[pl.ds(b, 8, stride=YP4), :]
        moved = pltpu.roll(rows, (b * Z4 - LANE4) % LANES, 1)
        message = jnp.where((lanes >= b * Z4) & (lanes < (b + 1) * Z4), moved, message)
    tail = pltpu.roll(last[8 * YP4 : 9 * YP4, :], Y4[1] * Z4 - LANE4, 1)
    message = jnp.where(lanes >= Y4[1] * Z4, tail, message)
    for d in range(devices):
        message_ref[d] = message


def merge_pair(part_ref, below_ref, above_ref, pair, row0):
    lane2 = lane_index((Y2[1], LANES)) < Z2
    lanes3 = lane_index((Y3[1], LANES))
    inside3 = (lanes3 >= LANE3) & (lanes3 < LANE4)

    def add(x, value):
        if x < PAIR_X:
            rows = slice(row0, row0 + value.shape[0])
            pair[x, rows, :] = pair[x, rows, :] + value

    for r in range(X2[1]):
        pair[3 + r, row0 : row0 + YP2, :] = part_ref[r]
    for ref, at2, at3 in ((below_ref, 0, 0), (above_ref, CX // 2 + 3, CX // 4 + 3)):
        for r in range(4):
            both = ref[SLAB2 + r * Y2[1] : SLAB2 + (r + 1) * Y2[1], :]
            add(at2 + r, jnp.where(lane2, both, 0.0))
            if r < 3:
                add(at2 + 4 + r, jnp.where(lane2, pltpu.roll(both, Z2, 1), 0.0))
        for r in range(2):
            four = ref[SLAB3 + r * Y3[1] : SLAB3 + (r + 1) * Y3[1], :]
            for g in range(4):
                moved = pltpu.roll(four, (LANE3 - g * Z3) % LANES, 1)
                add(at3 + 2 * g + r, jnp.where(inside3, moved, 0.0))


def edges_kernel(raw_ref, part_ref, below_ref, above_ref, up_ref, down_ref, up2_ref, down2_ref, pair):
    for x in range(FINE_X):
        for ref, start in ((up_ref, CY - 3), (down_ref, 0)):
            value = None
            if 3 <= x < FINE_X - 3:
                value = raw_ref[x - 3, start : start + 6, :]
            for slab, at in ((below_ref, x), (above_ref, x - CX - 3)):
                if 0 <= at < 6:
                    extra = slab[at * Y1[1] + start : at * Y1[1] + start + 6, :]
                    value = extra if value is None else value + extra
            ref[6 * x : 6 * x + 6, :] = value
    pair[...] = jnp.zeros_like(pair)
    merge_pair(part_ref, below_ref, above_ref, pair, 0)
    low2 = lane_index((8, LANES)) < Z2
    lanes = lane_index((8, LANES))
    keep = lax.broadcasted_iota(jnp.int32, (8, LANES), 0) < 7
    zero = jnp.zeros((8, LANES), jnp.float32)
    for ref, far, at2, at3, at_far in (
        (up_ref, up2_ref, CY // 2 - 3, CY // 4 - 3, CY // 2 - 3),
        (down_ref, down2_ref, 0, 0, 0),
    ):
        if EDGE2 > 6 * FINE_X:
            ref[6 * FINE_X : EDGE2, :] = jnp.zeros((EDGE2 - 6 * FINE_X, LANES), jnp.float32)
        for r in range(PACK2):
            first = pair[r, at2 : at2 + 8, :]
            second = zero
            if r + PACK2 < PAIR_X:
                second = pltpu.roll(pair[r + PACK2, at2 : at2 + 8, :], Z2, 1)
            ref[EDGE2 + 8 * r : EDGE2 + 8 * r + 8, :] = jnp.where(keep, jnp.where(low2, first, second), 0.0)
        for r in range(PACK3):
            total, total_far = zero, zero
            for g in range(4):
                x = g * PACK3 + r
                if x >= SPAN3:
                    continue
                inside = (lanes >= g * Z3) & (lanes < (g + 1) * Z3)
                turn = (g * Z3 - LANE3) % LANES
                total = jnp.where(inside, pltpu.roll(pair[x, at3 : at3 + 8, :], turn, 1), total)
                total_far = jnp.where(inside, pltpu.roll(pair[x, at_far : at_far + 8, :], turn, 1), total_far)
            ref[EDGE3 + 8 * r : EDGE3 + 8 * r + 8, :] = total
            far[4 * r : 4 * r + 4, :] = total_far[0:4]
        if FAR > 4 * PACK3:
            far[4 * PACK3 :, :] = jnp.zeros((FAR - 4 * PACK3, LANES), jnp.float32)


def merge_fine(raw_ref, below_ref, above_ref, south_ref, north_ref, fine):
    fine[...] = jnp.zeros_like(fine)
    for x in range(FINE_X):
        if 3 <= x < FINE_X - 3:
            fine[x, 3 : 3 + YP1, :] = raw_ref[x - 3]
        for slab, at in ((below_ref, x), (above_ref, x - CX - 3)):
            if 0 <= at < 6:
                rows = slice(3, 3 + Y1[1])
                fine[x, rows, :] = fine[x, rows, :] + slab[at * Y1[1] : (at + 1) * Y1[1], :]
        fine[x, 0:6, :] = fine[x, 0:6, :] + south_ref[6 * x : 6 * x + 6, :]
        fine[x, CY + 3 : CY + 9, :] = fine[x, CY + 3 : CY + 9, :] + north_ref[6 * x : 6 * x + 6, :]


def merge_coarse(part_ref, below_ref, above_ref, south_ref, north_ref, south2_ref, north2_ref, pair):
    pair[...] = jnp.zeros_like(pair)
    merge_pair(part_ref, below_ref, above_ref, pair, 3)
    low2 = lane_index((8, LANES)) < Z2
    lanes = lane_index((8, LANES))
    inside = (lanes >= LANE3) & (lanes < LANE4)
    for ref, far, at2, at3, at_far in (
        (south_ref, south2_ref, 0, 0, 0),
        (north_ref, north2_ref, CY // 2 + 3, CY // 4 + 3, CY // 2 + 3),
    ):
        for r in range(PACK2):
            both = ref[EDGE2 + 8 * r : EDGE2 + 8 * r + 8, :]
            pair[r, at2 : at2 + 8, :] = pair[r, at2 : at2 + 8, :] + jnp.where(low2, both, 0.0)
            x = r + PACK2
            if x < PAIR_X:
                moved = jnp.where(low2, pltpu.roll(both, Z2, 1), 0.0)
                pair[x, at2 : at2 + 8, :] = pair[x, at2 : at2 + 8, :] + moved
        for r in range(PACK3):
            four = ref[EDGE3 + 8 * r : EDGE3 + 8 * r + 8, :]
            four_far = far[4 * r : 4 * r + 4, :]
            for g in range(4):
                x = g * PACK3 + r
                if x >= SPAN3:
                    continue
                turn = (LANE3 - g * Z3) % LANES
                moved = jnp.where(inside, pltpu.roll(four, turn, 1), 0.0)
                pair[x, at3 : at3 + 8, :] = pair[x, at3 : at3 + 8, :] + moved
                moved = jnp.where(inside[0:4], pltpu.roll(four_far, turn, 1), 0.0)
                pair[x, at_far : at_far + 4, :] = pair[x, at_far : at_far + 4, :] + moved


def stencil_rows(source, count, rows_out, table, target, planes):
    for i in range(count + 6):
        sums = [source[i, 3 : 3 + rows_out, :]]
        for b in range(1, 4):
            sums.append(source[i, 3 - b : 3 - b + rows_out, :] + source[i, 3 + b : 3 + b + rows_out, :])
        for a in range(4):
            value = table[4 * a : 4 * a + 1] * sums[0]
            for b in range(1, 4):
                value = value + table[4 * a + b : 4 * a + b + 1] * sums[b]
            planes[a, i] = value
    for i in range(count):
        value = planes[0, i + 3]
        for a in range(1, 4):
            value = value + (planes[a, i + 3 - a] + planes[a, i + 3 + a])
        target[i] = value


def prolong_x(load, window_in, window_out):
    outs = []
    first = window_in[0]
    for n in range(window_out[0], window_out[0] + window_out[1]):
        if n % 2 == 0:
            outs.append(load(n // 2 - first))
        else:
            m = (n - 1) // 2 - first
            outs.append(0.5625 * (load(m) + load(m + 1)) - 0.0625 * (load(m - 1) + load(m + 2)))
    return outs


def prolong_y(source, window_in, window_out, target):
    first, count = window_out
    even = first % 2
    evens = (count - even + 1) // 2
    start = (first + even) // 2 - window_in[0]
    target[:, pl.ds(even, evens, stride=2), :] = source[:, start : start + evens, :]
    odds = count - evens
    m = (first + 1 - even - 1) // 2 - window_in[0]

    def taken(shift):
        return source[:, m + shift : m + shift + odds, :]

    target[:, pl.ds(1 - even, odds, stride=2), :] = 0.5625 * (taken(0) + taken(1)) - 0.0625 * (taken(-1) + taken(2))


def rise(load, window_in, window_out, wide_in, wide_out, half, target):
    target[...] = jnp.zeros_like(target)
    for r, value in enumerate(prolong_x(load, window_in, window_out)):
        half[r] = value
    prolong_y(half, wide_in, wide_out, target)


def coarse_kernel(
    message_ref, gather_ref, basis_ref, spectrum_ref, window_ref, level3_ref, ninth, level4, half3, *, size_x, size_y
):
    devices = size_x * size_y
    width = CY // 8 * size_y * Z4
    blocks = width // LANES
    used = Y4[1] * Z4
    tails = lane_index((devices, LANES))
    gathered = jnp.zeros((devices, LANES), jnp.float32)
    for b in range(Y4[1]):
        rows = message_ref[pl.ds(b, devices, stride=8), :]
        moved = pltpu.roll(rows, (b * Z4 - used) % LANES, 1)
        gathered = jnp.where((tails >= b * Z4) & (tails < (b + 1) * Z4), moved, gathered)
    ninth[...] = gathered

    def assemble(load, rows):
        total = [jnp.zeros((rows, LANES), jnp.float32) for _ in range(blocks)]
        lanes = lane_index((rows, LANES))
        for j in range(size_y):
            position = (j * (CY // 8) + Y4[0]) * Z4 % width
            block, offset = (position // LANES, position % LANES)
            value = jnp.where(lanes < used, load(j), 0.0)
            if offset == 0:
                total[block] = total[block] + value
                continue
            value = pltpu.roll(value, offset, 1)
            following = (block + 1) % blocks
            total[block] = total[block] + jnp.where(lanes >= offset, value, 0.0)
            total[following] = total[following] + jnp.where(lanes < offset, value, 0.0)
        return jnp.concatenate(total, axis=1)

    strips = []
    for i in range(size_x):
        strips.append(assemble(lambda j: message_ref[(i * size_y + j) * 8 : (i * size_y + j + 1) * 8, :], 8))
    tail = assemble(lambda j: ninth[pl.ds(j, size_x, stride=size_y), :], size_x)
    if size_x % 8:
        tail = jnp.concatenate([tail, jnp.zeros((8 - size_x % 8, width), jnp.float32)], axis=0)
    strips.append(tail)
    strips = jnp.concatenate(strips, axis=0)
    exact = dict(precision=HIGHEST, preferred_element_type=jnp.float32)
    modes = jnp.dot(gather_ref[...], strips, **exact)
    modes = lax.dot_general(modes, basis_ref[...], (((1,), (1,)), ((), ())), **exact)
    modes = jnp.dot(modes * spectrum_ref[...], basis_ref[...], **exact)
    shift = (width - (lax.axis_index("gy") * (CY // 8) + Y4[0]) * Z4) % width
    modes = pltpu.roll(modes, shift, 1)[:, :LANES]
    own = jnp.dot(window_ref[lax.axis_index("gx")], modes, **exact)
    lanes = lane_index(own.shape)
    inside4 = (lanes >= LANE4) & (lanes < LANE4 + Z4)
    level4[...] = jnp.zeros_like(level4)
    for b in range(Y4[1]):
        moved = jnp.where(inside4, pltpu.roll(own, (LANE4 - b * Z4) % LANES, 1), 0.0)
        level4[pl.ds(b, X4[1], stride=YP4), :] = moved[: X4[1]]

    rise(lambda i: level4[i * YP4 : (i + 1) * YP4, :], X4, X3, Y4, Y3, half3, level3_ref)


def part_copies(pairs, sems, part):
    copies = []
    for i, (source, target) in enumerate(pairs):
        rows = source.shape[0] // PARTS
        at = pl.ds(pl.multiple_of(part * rows, 8), rows)
        copies.append(pltpu.make_async_copy(source.at[at], target.at[at], sems.at[i, part]))
    return copies


def atoms_kernel(frac_ref, cell_ref, token_ref, real_ref, place_ref, reals, places, sems, *, total_y):
    fill_tables(reals, places, None, frac_ref, cell_ref, total_y)
    pairs = ((reals, real_ref), (places, place_ref))
    for part in range(PARTS):
        for copy in part_copies(pairs, sems, part):
            copy.start()
    for part in range(PARTS):
        for copy in part_copies(pairs, sems, part):
            copy.wait()


def field_kernel(
    raw_ref, part_ref, below_ref, above_ref, south_ref, north_ref, south2_ref, north2_ref,
    coarse_ref, spectrum_ref, depth_ref, real_ref, place_ref,
    potential_ref, atom_ref,
    reals, places, sems, fine, pair, planes, planes_pair, smooth, smooth_pair,
    level3, half2, level2, half1, level1, field, partial,
):
    pairs = ((real_ref, reals), (place_ref, places))

    def fetch(part, carry):
        for copy in part_copies(pairs, sems, part):
            copy.start()
        return carry

    lax.fori_loop(0, PARTS, fetch, 0)
    merge_fine(raw_ref, below_ref, above_ref, south_ref, north_ref, fine)
    merge_coarse(part_ref, below_ref, above_ref, south_ref, north_ref, south2_ref, north2_ref, pair)
    stencil_rows(pair, X2[1], YP2, spectrum_ref[1], smooth_pair, planes_pair)
    lanes3 = lane_index((YP3, LANES))
    inside3 = (lanes3 >= LANE3) & (lanes3 < LANE4)
    for r in range(X3[1]):
        level3[r] = coarse_ref[r] + jnp.where(inside3, smooth_pair[r, 0:YP3, :], 0.0)
    rise(lambda i: level3[i], X3, X2, Y3, Y2, half2, level2)
    inside2 = lane_index((YP2, LANES)) < Z2
    for r in range(X2[1]):
        level2[r] = level2[r] + jnp.where(inside2, smooth_pair[r], 0.0)
    rise(lambda i: level2[i], X2, X1, Y2, Y1, half1, level1)
    stencil_rows(fine, X1[1], YP1, spectrum_ref[0], smooth, planes)


    def transform(*accs):
        span = GRID_X // UNITS
        for unit, acc in enumerate(accs):
            at = slice(unit * span, (unit + 1) * span)
            parts = [value[at].reshape(span * YP1, LANES) for value in (smooth, level1)]
            high, low = halves(jnp.concatenate(parts, axis=1))
            pltpu.matmul_push_rhs(depth_ref[...], 0, unit)
            pltpu.matmul_acc_lhs(acc, high, 0)
            pltpu.matmul_acc_lhs(acc, low, None)
        for unit, acc in enumerate(accs):
            value = pltpu.matmul_pop(acc)
            field[unit * span : (unit + 1) * span] = (value[:, :NZ] + value[:, NZ:]).reshape(span, YP1, NZ)

    shape = (GRID_X // UNITS * YP1, 2 * NZ)
    pl.run_scoped(transform, *(pltpu.ACC(mxu_id=unit)(shape, jnp.float32) for unit in range(UNITS)))
    potential_ref[...] = field[0:CX, 0:CY, :]
    for part in range(PARTS):
        for copy in part_copies(pairs, sems, part):
            copy.wait()

    half = CHUNKS // UNITS
    rows = 4 * YP1

    def sample(plane, unit, acc):
        product = pltpu.matmul_pop(acc)
        for c in range(half):
            row = plane * CHUNKS + unit * half + c
            lanes = slice(c * LANES, (c + 1) * LANES)
            weights = [spread_row(reals, REAL_X + m, row) for m in range(4)]
            table, tile = pattern_y(reals, places, row)
            value = None
            for t in range(TILES_Y):
                layer = None
                for m in range(4):
                    at = m * YP1 + 8 * t
                    term = product[at : at + 8, lanes] * weights[m]
                    layer = term if layer is None else layer + term
                value = layer if value is None else jnp.where(tile == t, layer, value)
            partial[pl.ds(row * 8, 8), :] = value * table

    def planes_of(group, *accs):
        depth = len(accs) // UNITS
        for p in range(GROUP):
            plane = group * GROUP + p
            high, low = halves(jnp.concatenate([field[plane + m] for m in range(4)], axis=0))
            first = jnp.concatenate([high, high], axis=1)
            second = jnp.concatenate([low, jnp.zeros_like(low)], axis=1)
            for unit in range(UNITS):
                tables = []
                for c in range(half):
                    highs, lows = along_z(reals, places, plane * CHUNKS + unit * half + c)
                    tables.append(jnp.concatenate(highs + lows, axis=0))
                acc = accs[unit * depth + p % depth]
                pltpu.matmul_push_rhs(jnp.concatenate(tables, axis=1), p % 2, unit)
                pltpu.matmul_acc_lhs(acc, first, p % 2)
                pltpu.matmul_acc_lhs(acc, second, None)
            if p > 0:
                for unit in range(UNITS):
                    sample(plane - 1, unit, accs[unit * depth + (p - 1) % depth])
        for unit in range(UNITS):
            sample(group * GROUP + GROUP - 1, unit, accs[unit * depth + (GROUP - 1) % depth])

    def step(group, carry):
        units = [unit for unit in range(UNITS) for _ in range(4)]
        accs = (pltpu.ACC(mxu_id=u)((rows, half * LANES), jnp.float32) for u in units)
        pl.run_scoped(functools.partial(planes_of, group), *accs)
        return carry

    lax.fori_loop(0, CX // GROUP, step, 0)
    for g in range(ROWS // 8):
        total = partial[pl.ds(g * 64, 8, stride=8), :]
        for r in range(1, 8):
            total = total + partial[pl.ds(g * 64 + r, 8, stride=8), :]
        atom_ref[g * 8 : g * 8 + 8, :] = total


VM = pl.BlockSpec(memory_space=pltpu.VMEM)
HB = pl.BlockSpec(memory_space=pl.ANY)


RESIDENT = 2**19


def f32(*shape):
    if 4 * int(np.prod(shape)) <= RESIDENT:
        return pltpu.VMEM(shape, jnp.float32)
    return jax.ShapeDtypeStruct(shape, jnp.float32)


def scratch(*shape):
    return pltpu.VMEM(shape, jnp.float32)


def shifted(value, axis, steps):
    count = lax.axis_size(axis)
    return lax.ppermute(value, axis, [(source, (source + steps) % count) for source in range(count)])


def integers(*shape):
    return pltpu.VMEM(shape, jnp.int32)


def call(kernel, name, outs, scratches, *operands, far_in=(), far_out=()):
    return pl.pallas_call(
        kernel,
        in_specs=[VM] * len(operands) + [HB] * len(far_in),
        out_specs=[VM] * len(outs) + [HB] * len(far_out),
        out_shape=[*outs, *far_out],
        scratch_shapes=scratches,
        name=name,
    )(*operands, *far_in)


def resident(*values):
    return [
        pltpu.with_memory_space_constraint(value, pltpu.VMEM) if value.nbytes <= RESIDENT else value
        for value in values
    ]


def local(charges, fractions, cells):
    size_x = lax.axis_size("gx")
    size_y = lax.axis_size("gy")
    devices = size_x * size_y
    total_y = CY * size_y
    down_table, up_table = depth_tables()
    gather, basis, coarse_spectrum, window = (jnp.asarray(t) for t in coarse_tables(size_x, size_y))
    charge = charges.reshape(ROWS, LANES)
    frac = fractions.reshape(3, ROWS, LANES)
    cell = cells.reshape(2, ROWS, LANES).transpose(1, 0, 2).reshape(2 * ROWS, LANES)
    raw, part, low, high, message = call(
        functools.partial(deposit_kernel, total_y=total_y, devices=devices),
        "deposit",
        [
            f32(X1[1], YP1, LANES),
            f32(X2[1], YP2, LANES),
            f32(SLAB, LANES),
            f32(SLAB, LANES),
            f32(devices, 8, LANES),
        ],
        [
            pltpu.VMEM(down_table.shape, down_table.dtype),
            pltpu.SemaphoreType.DMA(()),
            scratch(REALS * ROWS, LANES),
            integers(PLACES * ROWS, LANES),
            scratch(GRID_X, YP1, NZ),
            scratch(X1[1], YP1, LANES),
            scratch(X2[1], YP1 + 16, LANES),
            scratch(X3[1], YP2 + 24, LANES),
            scratch(X4[1], YP3 + 16, LANES),
            scratch(X4[1] * YP4, LANES),
        ],
        charge, frac, cell,
        far_in=[down_table],
    )
    everyone = lax.all_to_all(message, ("gx", "gy"), 0, 0)
    below = shifted(high, "gx", 1)
    above = shifted(low, "gx", -1)
    up, down, up2, down2 = call(
        edges_kernel,
        "edges",
        [f32(EDGE, LANES), f32(EDGE, LANES), f32(FAR, LANES), f32(FAR, LANES)],
        [scratch(PAIR_X, YP2, LANES)],
        *resident(raw, part, below, above),
    )
    south = shifted(up, "gy", 1)
    north = shifted(down, "gy", -1)
    south2 = shifted(up2, "gy", 2)
    north2 = shifted(down2, "gy", -2)
    (coarse,) = call(
        functools.partial(coarse_kernel, size_x=size_x, size_y=size_y),
        "coarse",
        [f32(X3[1], YP3, LANES)],
        [scratch(devices, LANES), scratch(X4[1] * YP4, LANES), scratch(X3[1], YP4, LANES)],
        *resident(everyone.reshape(devices * 8, LANES), gather, basis, coarse_spectrum, window),
    )
    sems = pltpu.SemaphoreType.DMA((2, PARTS))
    tables = call(
        functools.partial(atoms_kernel, total_y=total_y),
        "atoms",
        [],
        [scratch(REALS * ROWS, LANES), integers(PLACES * ROWS, LANES), sems],
        *resident(frac, cell),
        far_in=[up2],
        far_out=[pltpu.HBM((REALS * ROWS, LANES), jnp.float32), pltpu.HBM((PLACES * ROWS, LANES), jnp.int32)],
    )
    potential, atoms = call(
        field_kernel,
        "field",
        [jax.ShapeDtypeStruct((CX, CY, NZ), jnp.float32), jax.ShapeDtypeStruct((ROWS, LANES), jnp.float32)],
        [
            scratch(REALS * ROWS, LANES),
            integers(PLACES * ROWS, LANES),
            sems,
            scratch(FINE_X, 32, LANES),
            scratch(PAIR_X, 24, LANES),
            scratch(4, FINE_X, YP1, LANES),
            scratch(4, PAIR_X, YP2, LANES),
            scratch(GRID_X, YP1, LANES),
            scratch(X2[1], YP2, LANES),
            scratch(X3[1], YP3, LANES),
            scratch(X2[1], YP3, LANES),
            scratch(X2[1], YP2, LANES),
            scratch(GRID_X, YP2, LANES),
            scratch(GRID_X, YP1, LANES),
            scratch(GRID_X, YP1, NZ),
            scratch(8 * ROWS, LANES),
        ],
        *resident(raw, part, below, above, south, north, south2, north2),
        *resident(coarse, jnp.asarray(spectra().astype(np.float32)), up_table),
        far_in=tables,
    )
    return (potential, atoms.reshape(1, 1, ATOMS_DEV))


def solution(mesh):
    placed = (P("gx", "gy", None), P("gx", "gy", None, None), P("gx", "gy", None, None))
    return jax.shard_map(
        local,
        mesh=mesh,
        in_specs=placed,
        out_specs=(P("gx", "gy", None), P("gx", "gy", None)),
        check_vma=False,
    )
```
